128 devices in a mesh: gx: 16 (over z, x), gy: 8 (over y, core).
Axes of the slice: x: 4, y: 4, z: 4, core: 2. Of those that a mesh axis runs over, the one named last changes fastest.
Arguments:
- velocity: float32 [3, 256, 256, 128], P(None, 'gx', 'gy'), may hold values from -3 to 3
- theta: float32 [256, 256, 128], P('gx', 'gy'), may hold values from -4 to 4
- vapour: float32 [256, 256, 128], P('gx', 'gy'), may hold values from 0.5 to 1.5
- radius_sq: float32 [64, 4096], P(None, ('gx', 'gy')), may hold values from 0.5 to 2
- multiplicity: float32 [64, 4096], P(None, ('gx', 'gy')), may hold values from 0.5 to 2
- counts: int32 [4096], P(('gx', 'gy')), may hold values from 16 to 64
- pairing: int32 [4096, 64], P(('gx', 'gy')), may hold values from 0 to 63, each once within a row
- destination: int32 [64, 4096], P(None, ('gx', 'gy')), may hold values from 0 to 4095, as said below
Outputs:
- velocity_new: float32 [3, 256, 256, 128], P(None, 'gx', 'gy')
- theta_new: float32 [256, 256, 128], P('gx', 'gy')
- vapour_new: float32 [256, 256, 128], P('gx', 'gy')
- moments: float32 [3, 4096], P(None, ('gx', 'gy'))
The draws below stay inside these ranges and needn't reach their ends.
Inputs may be any that keep to these rules, and one draw needn't show every extreme that they name: Each slot's destination is its own box or one of the eight boxes around it, with box columns wrapping around 64 and box rows around 64, numbered as in the reference program. `pairing`: each row is a permutation of 0 to 63.
All inputs are finite; a program needn't handle non-finite values.
Results may differ from the reference program's by a relative error of at most 0.0003.
Values sent between devices are 32-bit elements; how exact they have to be, the bound alone decides.
A program may use at most 64 MiB of HBM per device.

```python
import math
import jax
import jax.numpy as jnp
from jax import lax

NZ = 128
BW = 4
SLOTS = 64
NX = 256
NY = 256
BXD = 4
BYD = 8
BOX_DEV = 32
BOXES = 4096
NBX = 64
NBY = 64
N_GX = 16
N_GY = 8


def draw_destination(key, part):
    own_key = jax.random.fold_in(key, 11)
    key_x, key_y = jax.random.split(own_key)
    step_x = jax.random.randint(key_x, (SLOTS, BOXES), -1, 2)
    step_y = jax.random.randint(key_y, (SLOTS, BOXES), -1, 2)
    box_number = jnp.arange(BOXES)
    device_number = box_number // BOX_DEV
    local_number = box_number % BOX_DEV
    grid_rows = NBY // BYD
    column = device_number // grid_rows * BXD + local_number // BYD
    row_index = device_number % grid_rows * BYD + local_number % BYD
    target_x = (column[None, :] + step_x) % NBX
    target_y = (row_index[None, :] + step_y) % NBY
    target = (target_x // BXD * grid_rows + target_y // BYD) * BOX_DEV + target_x % BXD * BYD + target_y % BYD
    return target.astype(jnp.int32)


def place_ends(result, stream_key, smallest, top_value):
    place = [jax.random.randint(jax.random.fold_in(stream_key, axis), (), 0, length) for axis, length in enumerate(result.shape)]
    widest = result.shape.index(max(result.shape))
    neighbour = place[:widest] + [(place[widest] + 1) % result.shape[widest]] + place[widest + 1:]
    return result.at[tuple(place)].set(smallest).at[tuple(neighbour)].set(top_value)


def shard_levels(stream_key, shape, shards, low, top_value):
    def one(axis_at, parts):
        heights = jax.random.uniform(jax.random.fold_in(jax.random.fold_in(stream_key, 6), axis_at), (parts,), jnp.float32, low / len(shards), top_value / len(shards))
        return jnp.repeat(jnp.exp(heights), shape[axis_at] // parts).reshape((-1,) + (1,) * (len(shape) - axis_at - 1))

    factor_of = one(*shards[0])
    for cut in shards[1:]:
        factor_of = factor_of * one(*cut)
    return factor_of


def normal_values(key, extent, deviation, most, pieces=(), dtype=jnp.bfloat16):
    gain = shard_levels(key, extent, pieces, -0.22, 0.18) if pieces else 1.0
    drawn = jax.random.normal(key, extent, jnp.float32) * deviation * gain
    return jnp.minimum(jnp.maximum(drawn, -most), most).astype(dtype)


def setup_inputs(seed: int = 0) -> dict:
    arg_keys = jax.random.split(jax.random.key(seed), 9)
    velocity = normal_values(arg_keys[0], (3, NX, NY, NZ), 0.5, 3.0, ((1, 16), (2, 8)), jnp.float32)
    theta = normal_values(arg_keys[1], (NX, NY, NZ), 1.0, 4.0, ((0, 16), (1, 8)), jnp.float32)
    vapour = jnp.clip(0.5 + 1.0 * jax.random.uniform(arg_keys[2], (NX, NY, NZ), jnp.float32) ** shard_levels(arg_keys[2], (NX, NY, NZ), ((0, 16), (1, 8)), -0.2, 0.2), 0.5, 1.5)
    radius_sq = jnp.clip(jnp.exp(math.log(2.0) - 1.3862944 * jax.random.uniform(arg_keys[3], (SLOTS, BOXES), jnp.float32) ** shard_levels(arg_keys[3], (SLOTS, BOXES), ((1, 128),), -0.2, 0.2)), 0.5, 2.0)
    multiplicity = jnp.clip(jnp.exp(math.log(2.0) - 1.3862944 * jax.random.uniform(arg_keys[4], (SLOTS, BOXES), jnp.float32) ** shard_levels(arg_keys[4], (SLOTS, BOXES), ((1, 128),), -0.2, 0.2)), 0.5, 2.0)
    counts = place_ends(jax.random.randint(arg_keys[5], (BOXES,), SLOTS // 4, SLOTS + 1), jax.random.fold_in(arg_keys[5], 1), SLOTS // 4, SLOTS).astype(jnp.int32)
    pairing = jax.vmap(lambda own: jax.random.permutation(own, SLOTS))(jax.random.split(arg_keys[6], BOXES)).reshape((BOXES, SLOTS)).astype(jnp.int32)
    destination = draw_destination(jax.random.fold_in(arg_keys[8], 71), 0)
    return dict(velocity=velocity, theta=theta, vapour=vapour, radius_sq=radius_sq, multiplicity=multiplicity, counts=counts, pairing=pairing, destination=destination)


TIME_STEP = 0.2
DIFFUSION = 0.05
BUOYANCY = 0.5
GROWTH = 0.5
COLLISION = 0.05
CONDENSE = 0.002
HIGHEST = lax.Precision.HIGHEST

def vertical_pair(values):
    upper_cell = jnp.concatenate([values[..., 1:], values[..., -1:]], axis=-1)
    lower_cell = jnp.concatenate([values[..., :1], values[..., :-1]], axis=-1)
    return (upper_cell, lower_cell)

def advect_one(values, speed_x, speed_y, speed_z):
    east_cell = jnp.roll(values, -1, 0)
    west_cell = jnp.roll(values, 1, 0)
    north_cell = jnp.roll(values, -1, 1)
    south_cell = jnp.roll(values, 1, 1)
    upper_cell, lower_cell = vertical_pair(values)
    carried = -0.5 * (speed_x * (east_cell - west_cell) + speed_y * (north_cell - south_cell) + speed_z * (upper_cell - lower_cell))
    spread = east_cell + west_cell + north_cell + south_cell + upper_cell + lower_cell - 6.0 * values
    return values + TIME_STEP * (carried + DIFFUSION * spread)

def cosine_table(levels):
    level_index = jnp.arange(levels).astype(jnp.float32)
    return jnp.cos(math.pi * (level_index[:, None] + 0.5) * level_index[None, :] / levels)

def poisson(divergence):
    levels = divergence.shape[2]
    level_table = cosine_table(levels)
    spectral = jnp.einsum('ijz,zm->mij', divergence, level_table, precision=HIGHEST)
    wave_x = 2.0 * jnp.cos(2.0 * math.pi * jnp.arange(NX).astype(jnp.float32) / NX) - 2.0
    wave_y = 2.0 * jnp.cos(2.0 * math.pi * jnp.arange(NY).astype(jnp.float32) / NY) - 2.0

    def solve_mode(operand):
        one_plane, mode_number = operand
        wave_z = 2.0 * jnp.cos(math.pi * mode_number.astype(jnp.float32) / levels) - 2.0
        eigenvalue = wave_x[:, None] + wave_y[None, :] + wave_z
        anchor = (mode_number == 0) & (jnp.arange(NX)[:, None] == 0) & (jnp.arange(NY)[None, :] == 0)
        safe_value = jnp.where(anchor, 1.0, eigenvalue)
        mode_values = jnp.fft.fft2(one_plane)
        solved = jnp.where(anchor, 0.0, mode_values / safe_value)
        return jnp.real(jnp.fft.ifft2(solved))
    modal = lax.map(solve_mode, (spectral, jnp.arange(levels).astype(jnp.int32)))
    weight = jnp.where(jnp.arange(levels) == 0, 1.0 / levels, 2.0 / levels)
    return jnp.einsum('mij,zm->ijz', modal, level_table * weight[None, :], precision=HIGHEST)

def to_boxes(grid_values):
    return grid_values.reshape(N_GX, BXD, N_GY, BYD).transpose(0, 2, 1, 3).reshape(BOXES)

def from_boxes(box_values):
    return box_values.reshape(N_GX, N_GY, BXD, BYD).transpose(0, 2, 1, 3).reshape(NBX, NBY)

def reference(velocity, theta, vapour, radius_sq, multiplicity, counts, pairing, destination):
    speed_x, speed_y, speed_z = (velocity[0], velocity[1], velocity[2])
    advected = [advect_one(values, speed_x, speed_y, speed_z) for values in (velocity[0], velocity[1], velocity[2], theta, vapour)]
    star_x = advected[0]
    star_y = advected[1]
    star_z = advected[2] + TIME_STEP * BUOYANCY * theta
    below_z = jnp.concatenate([jnp.zeros_like(star_z[..., :1]), star_z[..., :-1]], axis=-1)
    divergence = star_x - jnp.roll(star_x, 1, 0) + (star_y - jnp.roll(star_y, 1, 1)) + (star_z - below_z)
    pressure = poisson(divergence)
    step_east = jnp.roll(pressure, -1, 0) - pressure
    step_north = jnp.roll(pressure, -1, 1) - pressure
    step_up = jnp.concatenate([pressure[..., 1:], pressure[..., -1:]], axis=-1) - pressure
    velocity_new = jnp.stack([star_x - step_east, star_y - step_north, star_z - step_up])
    theta_new = advected[3]
    moist_field = advected[4]
    box_mean = to_boxes(moist_field.reshape(NBX, BW, NBY, BW, NZ).mean(axis=(1, 3, 4)))
    slot_index = jnp.arange(SLOTS)[:, None]
    live_weight = jnp.where(slot_index < counts[None, :], multiplicity, 0.0)
    grown_sq = radius_sq + GROWTH * jax.nn.softplus(box_mean)[None, :]
    mass_before = radius_sq * jnp.sqrt(radius_sq)
    mass_grown = grown_sq * jnp.sqrt(grown_sq)
    condensed = lax.optimization_barrier(jnp.sum(live_weight * (mass_grown - mass_before), axis=0))
    vapour_new = (moist_field.reshape(NBX, BW, NBY, BW, NZ) - CONDENSE * from_boxes(condensed)[:, None, :, None, None]).reshape(NX, NY, NZ)
    row_index = jnp.arange(BOXES)[:, None]
    partner = jnp.zeros_like(pairing).at[row_index, pairing].set(jnp.roll(pairing, -(SLOTS // 2), axis=1)).T
    other_grown = jnp.take_along_axis(grown_sq, partner, axis=0)
    other_live = jnp.take_along_axis(live_weight, partner, axis=0)
    other_mass = jnp.take_along_axis(mass_grown, partner, axis=0)
    radius_sum = jnp.sqrt(grown_sq) + jnp.sqrt(other_grown)
    collide_rate = radius_sum * radius_sum * jnp.abs(grown_sq - other_grown) * other_live
    mass_final = (mass_grown + COLLISION * collide_rate * other_mass) / (1.0 + COLLISION * collide_rate)
    carried_load = jnp.stack([live_weight, live_weight * mass_final, live_weight * mass_final * mass_final]).reshape(3, SLOTS * BOXES)
    flat_target = destination.reshape(SLOTS * BOXES)
    moments = jax.vmap(lambda line: jax.ops.segment_sum(line, flat_target, num_segments=BOXES))(carried_load) / SLOTS
    return (velocity_new, theta_new, vapour_new, moments)
```

```python
import functools
import math

import jax
import jax.numpy as jnp
import numpy as np
from jax import lax
from jax.experimental import pallas as pl
from jax.experimental.pallas import tpu as pltpu
from jax.sharding import PartitionSpec as P

MESH = pl.DeviceIdType.MESH
GX, GY = 16, 8
DEV = GX * GY
SX, SY, NZ = 16, 32, 128
NX, NY = 256, 256
HALF = 72
F32 = jnp.float32
BF16 = jnp.bfloat16
ANY = pl.BlockSpec(memory_space=pl.ANY)


def split_table(table):
    table = np.asarray(table, np.float32)
    high = table.astype(jnp.bfloat16)
    low = (table - high.astype(np.float32)).astype(jnp.bfloat16)
    return np.stack([high, low])


@functools.cache
def tables():
    tau = 2.0 * math.pi
    z = np.arange(NZ)
    cosine = np.cos(math.pi * (z[None, :] + 0.5) * z[:, None] / NZ)
    weight = np.where(z == 0, 1.0 / NZ, 2.0 / NZ)
    back = cosine * weight[:, None]
    rows, factor, seen = [], [], set()
    for p in range(16):
        for q in range(8):
            if (p, q) in seen:
                continue
            mirror = (-p % 16, -q % 8)
            seen.update({(p, q), mirror})
            rows.append((p, q))
            factor.append(1.0 if mirror == (p, q) else 2.0)
    pad = HALF - len(rows)
    low_x = np.array([r[0] for r in rows] + [0] * pad)
    low_y = np.array([r[1] for r in rows] + [0] * pad)
    factor = np.array(factor + [0.0] * pad)
    used = np.array([1.0] * len(rows) + [0.0] * pad)
    a = np.repeat(np.arange(16), 8)
    b = np.tile(np.arange(8), 16)
    first, last = [], []
    for c in range(4):
        angle = tau * (
            low_x[:, None] * a[None] / 16.0
            + low_y[:, None] * b[None] / 8.0
            + low_x[:, None] * c / 64.0
        )
        first.append(np.concatenate([np.cos(angle) * used[:, None], -np.sin(angle) * used[:, None]]))
        scale = factor[:, None] / (NX * NY)
        last.append(np.concatenate([np.cos(angle) * scale, -np.sin(angle) * scale]).T)
    lane_i = np.repeat(np.arange(4), 32)
    lane_j = np.tile(np.arange(32), 4)
    turn_cos, turn_sin, wave = [], [], []
    for q in range(4):
        kx0 = low_x + 16 * q
        angle = tau * (kx0[:, None] * lane_i[None] + low_y[:, None] * lane_j[None]) / 256.0
        turn_cos.append(np.cos(angle))
        turn_sin.append(np.sin(angle))
        kx = kx0[:, None] + 64 * lane_i[None]
        ky = low_y[:, None] + 8 * lane_j[None]
        wave.append(-4.0 * np.sin(math.pi * kx / NX) ** 2 - 4.0 * np.sin(math.pi * ky / NY) ** 2)
    turns = np.stack([np.concatenate(turn_cos), np.concatenate(turn_sin), np.concatenate(wave)])
    angle = tau * (lane_i[:, None] * lane_i[None] / 4.0 + lane_j[:, None] * lane_j[None] / 32.0)
    cos2, sin2 = np.cos(angle), np.sin(angle)
    ahead = np.block([[cos2, -sin2], [sin2, cos2]])
    behind = np.block([[cos2, sin2], [-sin2, cos2]])
    wave_z = -4.0 * np.sin(math.pi * z / (2.0 * NZ)) ** 2
    wave_z = np.broadcast_to(wave_z[:, None], (NZ, 128)).astype(np.float32)
    box = np.zeros((32, 128), np.float32)
    for column in range(4):
        for j in range(32):
            box[column * 8 + j // 4, column * 32 + j] = 1.0
    return dict(
        cosine=split_table(cosine),
        first=split_table(np.stack(first)),
        ahead=split_table(ahead),
        behind=split_table(behind),
        last=split_table(np.stack(last)),
        turns=turns.astype(np.float32),
        wave_z=wave_z,
        box=box.astype(jnp.bfloat16),
        back=split_table(back),
    )


def halves(values):
    high = values.astype(BF16)
    return high, (values - high.astype(F32)).astype(BF16)


def product(left, right, dims):
    def one(x, y):
        return lax.dot_general(x, y, (dims, ((), ())), preferred_element_type=F32)

    (left_high, left_low), (right_high, right_low) = left, right
    return one(left_high, right_high) + (one(left_high, right_low) + one(left_low, right_high))


NN = ((1,), (0,))
NT = ((1,), (1,))
TN = ((0,), (0,))


def step_kernel(
    vel, theta, vapour, radius, multi, counts, pairing, dest,
    cosine_h, first_h, ahead_h, behind_h, last_h, turns_h, wave_h, box_h,
    modes, star, theta_out, vapour_out, moments_out,
    fp, ad, xu2, yl, yh, corner, row_y0, below_y, quad, send1, got1, send2,
    cosine, first, ahead, behind, last, turns, wave, box,
    rad_v, mul_v, cnt_v, pair_v, dst_v, cond, load, near, res,
    load_sem, drop_sem, table_sem, hs_sem, hr_sem, s1_sem, r1_sem, s2_sem, r2_sem, own_sem,
    ms_sem, mr_sem, out_sem,
):
    gx = lax.axis_index("gx")
    gy = lax.axis_index("gy")
    me = gx * GY + gy
    east, west = lax.rem(gx + 1, GX), lax.rem(gx + GX - 1, GX)
    north, south = lax.rem(gy + 1, GY), lax.rem(gy + GY - 1, GY)
    peers_y = [lax.rem(gy + r, GY) for r in range(GY)]

    loads = [
        pltpu.make_async_copy(vel, fp.at[pl.ds(0, 3), pl.ds(1, SX)], load_sem.at[0]),
        pltpu.make_async_copy(theta, fp.at[3, pl.ds(1, SX)], load_sem.at[1]),
        pltpu.make_async_copy(vapour, fp.at[4, pl.ds(1, SX)], load_sem.at[2]),
    ]
    drops = [
        pltpu.make_async_copy(source, target, drop_sem.at[k])
        for k, (source, target) in enumerate(
            [(radius, rad_v), (multi, mul_v), (counts, cnt_v), (pairing, pair_v), (dest, dst_v)]
        )
    ]
    table_pairs = [
        (cosine_h, cosine), (box_h, box), (first_h, first), (turns_h, turns), (ahead_h, ahead),
        (wave_h, wave), (behind_h, behind), (last_h, last),
    ]
    fetches = [
        pltpu.make_async_copy(source, target, table_sem.at[k])
        for k, (source, target) in enumerate(table_pairs)
    ]
    for copy in loads + drops + fetches:
        copy.start()

    barrier = pltpu.get_barrier_semaphore()

    def greet(px, ry):
        pl.semaphore_signal(barrier, inc=1, device_id=(px, peers_y[ry]), device_id_type=MESH)

    for ry in range(1, GY):
        greet(gx, ry)

    def greet_column(rx, carry):
        px = lax.rem(gx + rx, GX)
        for ry in range(GY):
            greet(px, ry)
        return carry

    lax.fori_loop(1, GX, greet_column, 0)

    for copy in drops:
        copy.wait()
    slot = lax.broadcasted_iota(jnp.int32, (64, 32), 0)
    live = jnp.where(slot < cnt_v[...][None, :], mul_v[...], 0.0)
    target = dst_v[...]
    local_box = lax.broadcasted_iota(jnp.int32, (64, 32), 1)
    source_x = gx * 4 + (local_box >> 3)
    source_y = gy * 8 + (local_box & 7)
    target_x = (target >> 8) * 4 + ((target & 31) >> 3)
    target_y = ((target >> 5) & 7) * 8 + (target & 7)
    offset_x = (target_x - source_x + 1) & 63
    offset_y = (target_y - source_y + 1) & 63
    code = (offset_x * 3 + offset_y).astype(F32)
    wide = jnp.concatenate([rad_v[...], live, code, jnp.zeros((64, 32), F32)], axis=1)
    flat = jnp.concatenate([wide, wide], axis=0).T
    pair = pair_v[...]
    order = jnp.concatenate([pair, pltpu.roll(jnp.concatenate([pair, pair], axis=1), 32, 1)[:, :64]], axis=1)
    radius_p = jnp.take_along_axis(flat[0:32], order, axis=1)
    live_p = jnp.take_along_axis(flat[32:64], order, axis=1)
    code_p = jnp.take_along_axis(flat[64:96], order, axis=1)

    pl.semaphore_wait(barrier, DEV - 1)

    def remote(source, target_ref, k, device):
        return pltpu.make_async_remote_copy(
            src_ref=source, dst_ref=target_ref, send_sem=hs_sem.at[k], recv_sem=hr_sem.at[k],
            device_id=device, device_id_type=MESH,
        )

    halo = [
        remote(vel.at[:, SX - 1], fp.at[pl.ds(0, 3), 0], 0, (east, gy)),
        remote(theta.at[SX - 1], fp.at[3, 0], 1, (east, gy)),
        remote(vapour.at[SX - 1], fp.at[4, 0], 2, (east, gy)),
        remote(vel.at[0, SX - 2], xu2, 3, (east, gy)),
        remote(vel.at[:, 0], fp.at[pl.ds(0, 3), SX + 1], 4, (west, gy)),
        remote(theta.at[0], fp.at[3, SX + 1], 5, (west, gy)),
        remote(vapour.at[0], fp.at[4, SX + 1], 6, (west, gy)),
        remote(vel.at[:, :, SY - 1], yl.at[pl.ds(0, 3)], 7, (gx, north)),
        remote(theta.at[:, SY - 1], yl.at[3], 8, (gx, north)),
        remote(vapour.at[:, SY - 1], yl.at[4], 9, (gx, north)),
        remote(vel.at[1, :, SY - 2], yl.at[5], 10, (gx, north)),
        remote(vel.at[:, :, 0], yh.at[pl.ds(0, 3)], 11, (gx, south)),
        remote(theta.at[:, 0], yh.at[3], 12, (gx, south)),
        remote(vapour.at[:, 0], yh.at[4], 13, (gx, south)),
        remote(vel.at[0, SX - 1, pl.ds(SY - 1, 1)], corner.at[0, pl.ds(0, 1)], 14, (east, north)),
        remote(vel.at[0, SX - 1, pl.ds(0, 1)], corner.at[1, pl.ds(0, 1)], 15, (east, south)),
        remote(vel.at[1, SX - 1, pl.ds(SY - 1, 1)], corner.at[2, pl.ds(0, 1)], 16, (east, north)),
        remote(vel.at[1, 0, pl.ds(SY - 1, 1)], corner.at[3, pl.ds(0, 1)], 17, (west, north)),
    ]
    for copy in halo:
        copy.start()
    for copy in loads:
        copy.wait()

    row = lax.broadcasted_iota(jnp.int32, (SY, NZ), 0)
    lane = lax.broadcasted_iota(jnp.int32, (SY, NZ), 1)
    tile_row = lax.broadcasted_iota(jnp.int32, (8, NZ), 0)

    def upward(values):
        return pltpu.roll(values, NZ - 1, 1)

    def downward(values):
        return pltpu.roll(values, 1, 1)

    def coefficients(speed, shape_lane=None):
        scaled = 0.1 * speed
        return 0.01 - scaled, 0.01 + scaled

    def vertical(speed, lanes):
        up, down = coefficients(speed)
        top, bottom = lanes == NZ - 1, lanes == 0
        centre = 0.94 + jnp.where(top, up, 0.0) + jnp.where(bottom, down, 0.0)
        return jnp.where(top, 0.0, up), jnp.where(bottom, 0.0, down), centre

    def advect_plane(x):
        c_east, c_west = coefficients(fp[0, x + 1])
        c_north, c_south = coefficients(fp[1, x + 1])
        c_north = jnp.where(row == SY - 1, 0.0, c_north)
        c_south = jnp.where(row == 0, 0.0, c_south)
        c_up, c_down, c_mid = vertical(fp[2, x + 1], lane)
        for f in range(5):
            centre = fp[f, x + 1]
            ad[f, x + 1] = (
                (c_mid * centre + c_east * fp[f, x + 2] + c_west * fp[f, x])
                + (c_north * pltpu.roll(centre, SY - 1, 0) + c_south * pltpu.roll(centre, 1, 0))
                + (c_up * upward(centre) + c_down * downward(centre))
            )
        row_y0[pl.ds(x, 1), :] = fp[1, x + 1, 0:1, :]

    def inner(x, carry):
        advect_plane(x)
        return carry

    lax.fori_loop(1, SX - 1, inner, 0)
    for copy in halo:
        copy.wait_recv()
    advect_plane(0)
    advect_plane(SX - 1)

    speed = fp[0, 0]
    c_east, c_west = coefficients(speed)
    c_north, c_south = coefficients(fp[1, 0])
    c_up, c_down, c_mid = vertical(fp[2, 0], lane)
    above = jnp.where(row == SY - 1, corner[1, 0:1, :], pltpu.roll(speed, SY - 1, 0))
    beneath = jnp.where(row == 0, corner[0, 0:1, :], pltpu.roll(speed, 1, 0))
    ad[0, 0] = (
        (c_mid * speed + c_east * fp[0, 1] + c_west * xu2[...])
        + (c_north * above + c_south * beneath)
        + (c_up * upward(speed) + c_down * downward(speed))
    )
    speed = yl[1]
    row_x = lax.broadcasted_iota(jnp.int32, (SX, NZ), 0)
    lane_x = lax.broadcasted_iota(jnp.int32, (SX, NZ), 1)
    c_east, c_west = coefficients(yl[0])
    c_north, c_south = coefficients(speed)
    c_up, c_down, c_mid = vertical(yl[2], lane_x)
    after = jnp.where(row_x == SX - 1, corner[3, 0:1, :], pltpu.roll(speed, SX - 1, 0))
    before = jnp.where(row_x == 0, corner[2, 0:1, :], pltpu.roll(speed, 1, 0))
    below_y[...] = (
        (c_mid * speed + c_east * after + c_west * before)
        + (c_north * row_y0[...] + c_south * yl[5])
        + (c_up * upward(speed) + c_down * downward(speed))
    )
    fetches[0].wait()

    def block(c, carry):
        total = jnp.zeros((SY, NZ), F32)
        parts = []
        for i in range(4):
            x = c * 4 + i
            _, c_south = coefficients(fp[1, x + 1, 0:8, :])
            c_north, _ = coefficients(fp[1, x + 1, SY - 8 : SY, :])
            c_south = jnp.where(tile_row == 0, c_south, 0.0)
            c_north = jnp.where(tile_row == 7, c_north, 0.0)
            for f in range(5):
                ad[f, x + 1, 0:8, :] += c_south * yl[f, pl.ds(x, 1), :]
                ad[f, x + 1, SY - 8 : SY, :] += c_north * yh[f, pl.ds(x, 1), :]
            star_w = ad[2, x + 1] + 0.1 * fp[3, x + 1]
            ad[2, x + 1] = star_w
            star_v = ad[1, x + 1]
            behind_v = jnp.where(row == 0, below_y[pl.ds(x, 1), :], pltpu.roll(star_v, 1, 0))
            below_w = jnp.where(lane == 0, 0.0, downward(star_w))
            parts.append((ad[0, x + 1] - ad[0, x]) + (star_v - behind_v) + (star_w - below_w))
            total = total + ad[4, x + 1]
        quad[c] = total
        chunk = jnp.concatenate(parts, axis=0)
        send1[c] = product((cosine[0], cosine[1]), halves(chunk), NT)
        return carry

    lax.fori_loop(0, 4, block, 0)

    def scatter(source, target_ref, send_sem, recv_sem):
        def one(px, ry):
            py = peers_y[ry]
            pltpu.make_async_remote_copy(
                src_ref=source.at[:, pl.ds(px * GY + py, 1), :],
                dst_ref=target_ref.at[:, pl.ds(me, 1), :],
                send_sem=send_sem, recv_sem=recv_sem, device_id=(px, py), device_id_type=MESH,
            ).start()

        def column(rx, carry):
            px = lax.rem(gx + rx, GX)
            for ry in range(GY):
                one(px, ry)
            return carry

        lax.fori_loop(1, GX, column, 0)
        for ry in range(1, GY):
            one(gx, ry)

    def drained(source, target_ref, sem):
        count = pl.ds(0, DEV - 1)
        pltpu.make_async_copy(source.at[:, count, :], target_ref.at[:, count, :], sem).wait()

    scatter(send1, got1, s1_sem, r1_sem)
    got1[:, pl.ds(me, 1), :] = send1[:, pl.ds(me, 1), :]

    outs = [
        pltpu.make_async_copy(ad.at[pl.ds(0, 3), pl.ds(1, SX)], star, out_sem.at[0]),
        pltpu.make_async_copy(ad.at[3, pl.ds(1, SX)], theta_out, out_sem.at[1]),
        pltpu.make_async_copy(ad.at[4, pl.ds(1, SX)], vapour_out, out_sem.at[2]),
    ]
    outs[0].start()
    outs[1].start()
    fetches[1].wait()
    high, low = halves(quad[...].reshape(128, NZ))
    sums = lax.dot_general(box[...], high, (NN, ((), ())), preferred_element_type=F32)
    sums = sums + lax.dot_general(box[...], low, (NN, ((), ())), preferred_element_type=F32)
    mean = jnp.sum(sums, axis=1, keepdims=True) * (1.0 / (16 * NZ))
    soft = jnp.maximum(mean, 0.0) + jnp.log1p(jnp.exp(-jnp.abs(mean)))
    grown = radius_p + 0.5 * soft
    root = jnp.sqrt(grown)
    mass = grown * root
    gain = mass - radius_p * jnp.sqrt(radius_p)

    def other(values):
        return pltpu.roll(values, 64, 1)

    root_sum = root + other(root)
    rate = 0.05 * (root_sum * root_sum * jnp.abs(grown - other(grown)) * other(live_p))
    final = (mass + rate * other(mass)) / (1.0 + rate)
    lanes = lax.broadcasted_iota(jnp.int32, (32, 128), 1)
    own_live = jnp.where(lanes < 64, live_p, 0.0)
    cond[...] = jnp.broadcast_to(jnp.sum(own_live * gain, axis=1, keepdims=True), (32, 128)) * 0.002
    carried = [own_live, own_live * final, own_live * final * final]
    packed = jnp.zeros((32, 128), F32)
    for d in range(9):
        chosen = code_p == float(d)
        for k in range(3):
            amount = jnp.sum(jnp.where(chosen, carried[k], 0.0), axis=1, keepdims=True)
            packed = packed + jnp.where(lanes == d * 3 + k, amount, 0.0)
    load[...] = packed

    def share(source, target_ref, k, device):
        return pltpu.make_async_remote_copy(
            src_ref=source, dst_ref=target_ref, send_sem=ms_sem.at[k], recv_sem=mr_sem.at[k],
            device_id=device, device_id_type=MESH,
        )

    top, bottom = pl.ds(24, 8), pl.ds(0, 8)
    shares = [
        share(load.at[top], near.at[0, bottom], 0, (east, gy)),
        share(load.at[bottom], near.at[1, bottom], 1, (west, gy)),
        share(load, near.at[2], 2, (gx, north)),
        share(load, near.at[3], 3, (gx, south)),
        share(load.at[top], near.at[4, bottom], 4, (east, north)),
        share(load.at[top], near.at[5, bottom], 5, (east, south)),
        share(load.at[bottom], near.at[6, bottom], 6, (west, north)),
        share(load.at[bottom], near.at[7, bottom], 7, (west, south)),
    ]
    for copy in shares:
        copy.start()

    def dry(x, carry):
        first_box = (x // 4) * 8
        for t in range(4):
            drop = jnp.where(
                tile_row < 4,
                cond[pl.ds(first_box + 2 * t, 1), :],
                cond[pl.ds(first_box + 2 * t + 1, 1), :],
            )
            ad[4, x + 1, 8 * t : 8 * t + 8, :] -= drop
        return carry

    lax.fori_loop(0, SX, dry, 0)
    outs[2].start()

    for copy in fetches[2:]:
        copy.wait()
    drained(send1, got1, r1_sem)
    z_re, z_im = [], []
    for c in range(4):
        both = product((first[0, c], first[1, c]), halves(got1[c]), NN)
        z_re.append(both[:HALF])
        z_im.append(both[HALF:])

    def butterfly(re, im, sign):
        s02r, s02i = re[0] + re[2], im[0] + im[2]
        d02r, d02i = re[0] - re[2], im[0] - im[2]
        s13r, s13i = re[1] + re[3], im[1] + im[3]
        d13r, d13i = re[1] - re[3], im[1] - im[3]
        if sign < 0:
            return (
                [s02r + s13r, d02r + d13i, s02r - s13r, d02r - d13i],
                [s02i + s13i, d02i - d13r, s02i - s13i, d02i + d13r],
            )
        return (
            [s02r + s13r, d02r - d13i, s02r - s13r, d02r + d13i],
            [s02i + s13i, d02i + d13r, s02i - s13i, d02i - d13r],
        )

    q_re, q_im = butterfly(z_re, z_im, -1)
    re, im = jnp.concatenate(q_re, axis=0), jnp.concatenate(q_im, axis=0)
    turn_cos, turn_sin = turns[0], turns[1]
    joined = jnp.concatenate([re * turn_cos + im * turn_sin, im * turn_cos - re * turn_sin], axis=1)
    spectrum = product(halves(joined), (ahead[0], ahead[1]), NN)
    eigen = turns[2] + wave[pl.ds(me, 1), :]
    inverse = jnp.where(eigen == 0.0, 0.0, 1.0 / jnp.where(eigen == 0.0, 1.0, eigen))
    solved = spectrum * jnp.concatenate([inverse, inverse], axis=1)
    turned = product(halves(solved), (behind[0], behind[1]), NN)
    re, im = turned[:, :128], turned[:, 128:]
    back_re, back_im = re * turn_cos - im * turn_sin, im * turn_cos + re * turn_sin
    v_re, v_im = butterfly(
        [back_re[HALF * q : HALF * (q + 1)] for q in range(4)],
        [back_im[HALF * q : HALF * (q + 1)] for q in range(4)],
        1,
    )
    wide_lane = lax.broadcasted_iota(jnp.int32, (128, 128), 1)
    edge = None
    for c in range(4):
        stacked = jnp.concatenate([v_re[c], v_im[c]], axis=0)
        plane = product((last[0, c], last[1, c]), halves(stacked), NN)
        send2[c] = plane
        if c == 0:
            next_x = pltpu.roll(plane, 120, 0)
        picked = jnp.where((wide_lane & 31) == 0, plane, 0.0)
        picked = picked if c == 0 else pltpu.roll(picked, c, 1)
        edge = picked if edge is None else edge + picked
    row_b = lax.broadcasted_iota(jnp.int32, (128, 128), 0) & 7
    edge = jnp.where(row_b == 7, pltpu.roll(edge, 7, 0), pltpu.roll(edge, 127, 0))
    moved = pltpu.roll(edge, 36, 1)
    in_move = (wide_lane >= 36) & (wide_lane < 40)
    send2[4] = jnp.where(wide_lane < 32, next_x, jnp.where(in_move, moved, edge))

    scatter(send2, modes, s2_sem, r2_sem)
    own = pltpu.make_async_copy(
        send2.at[:, pl.ds(me, 1), :], modes.at[:, pl.ds(me, 1), :], own_sem
    )
    own.start()

    for copy in shares:
        copy.wait_recv()
    tile_lane = lax.broadcasted_iota(jnp.int32, (8, 128), 1)

    def column_of(x):
        if x < 0:
            return near[0, 0:8, :], near[4, 7:8, :], near[5, 0:1, :]
        if x > 3:
            return near[1, 0:8, :], near[6, 7:8, :], near[7, 0:1, :]
        return load[8 * x : 8 * x + 8, :], near[2, 8 * x + 7 : 8 * x + 8, :], near[3, 8 * x : 8 * x + 1, :]

    arrived = [jnp.zeros((8, 128), F32) for _ in range(4)]
    for x in range(-1, 5):
        centre, low_row, high_row = column_of(x)
        shifted = [
            jnp.where(tile_row == 7, high_row, pltpu.roll(centre, 7, 0)),
            centre,
            jnp.where(tile_row == 0, low_row, pltpu.roll(centre, 1, 0)),
        ]
        for dx in (-1, 0, 1):
            if not 0 <= x + dx < 4:
                continue
            for dy in (-1, 0, 1):
                d = (dx + 1) * 3 + dy + 1
                values = shifted[dy + 1]
                values = values if d == 0 else pltpu.roll(values, 128 - 3 * d, 1)
                arrived[x + dx] = arrived[x + dx] + values
    stacked = jnp.concatenate(arrived + [jnp.zeros((96, 128), F32)], axis=0) * (1.0 / 64)
    res[...] = stacked.T[0:8, :]
    outs.append(pltpu.make_async_copy(res, moments_out, out_sem.at[3]))
    outs[3].start()

    for copy in halo:
        copy.wait_send()
    for copy in shares:
        copy.wait_send()
    drained(send1, got1, s1_sem)
    for copy in outs:
        copy.wait()
    own.wait()
    drained(send2, send2, s2_sem)
    drained(send2, modes, r2_sem)


def final_kernel(
    modes, star, theta, vapour, moments, back_h,
    vel_out, theta_out, vapour_out, moments_out,
    mode_v, star_v, theta_v, vapour_v, mom_v, mom_o, back, pressure, in_sem, out_sem,
):
    loads = [
        pltpu.make_async_copy(source, target, in_sem.at[k])
        for k, (source, target) in enumerate(
            [(modes, mode_v), (back_h, back), (star, star_v), (theta, theta_v), (vapour, vapour_v), (moments, mom_v)]
        )
    ]
    for copy in loads:
        copy.start()
    loads[0].wait()
    loads[1].wait()
    for c in range(5):
        pressure[pl.ds(128 * c, 128), :] = product(halves(mode_v[c]), (back[0], back[1]), TN)
    for copy in loads[2:]:
        copy.wait()
    mom_o[...] = mom_v[0:3, 0:32]
    outs = [
        pltpu.make_async_copy(theta_v, theta_out, out_sem.at[0]),
        pltpu.make_async_copy(vapour_v, vapour_out, out_sem.at[1]),
        pltpu.make_async_copy(mom_o, moments_out, out_sem.at[2]),
    ]
    for copy in outs:
        copy.start()
    row = lax.broadcasted_iota(jnp.int32, (SY, NZ), 0)
    lane = lax.broadcasted_iota(jnp.int32, (SY, NZ), 1)
    for x in range(SX):
        c, i = x // 4, x % 4
        here = pressure[pl.ds(32 * x, 32), :]
        ahead = pressure[pl.ds(32 * x + 32, 32), :]
        line = 512 + (36, 32, 64, 96)[i] + c
        side = jnp.where(row == SY - 1, pressure[line : line + 1, :], pltpu.roll(here, SY - 1, 0))
        above = jnp.where(lane == NZ - 1, here, pltpu.roll(here, NZ - 1, 1))
        star_v[0, x] = star_v[0, x] - (ahead - here)
        star_v[1, x] = star_v[1, x] - (side - here)
        star_v[2, x] = star_v[2, x] - (above - here)
    last = pltpu.make_async_copy(star_v, vel_out, out_sem.at[3])
    last.start()
    for copy in outs:
        copy.wait()
    last.wait()


def shards(velocity, theta, vapour, radius_sq, multiplicity, counts, pairing, destination):
    t = tables()
    names = ["cosine", "first", "ahead", "behind", "last", "turns", "wave_z", "box"]
    held = [jnp.asarray(t[name]) for name in names]
    block = (SX, SY, NZ)
    shape = jax.ShapeDtypeStruct
    vmem = pltpu.VMEM
    dma = pltpu.SemaphoreType.DMA
    modes, star, theta_new, vapour_new, moments = pl.pallas_call(
        step_kernel,
        out_shape=(
            shape((5, DEV, 128), F32),
            shape((3,) + block, F32),
            shape(block, F32),
            shape(block, F32),
            shape((8, 128), F32),
        ),
        in_specs=[ANY] * 16,
        out_specs=(ANY,) * 5,
        scratch_shapes=[
            vmem((5, SX + 2, SY, NZ), F32),
            vmem((5, SX + 1, SY, NZ), F32),
            vmem((SY, NZ), F32),
            vmem((6, SX, NZ), F32),
            vmem((5, SX, NZ), F32),
            vmem((4, 8, NZ), F32),
            vmem((SX, NZ), F32),
            vmem((SX, NZ), F32),
            vmem((4, SY, NZ), F32),
            vmem((4, DEV, 128), F32),
            vmem((4, DEV, 128), F32),
            vmem((5, DEV, 128), F32),
        ]
        + [vmem(t[name].shape, t[name].dtype) for name in names]
        + [
            vmem((64, 32), F32),
            vmem((64, 32), F32),
            vmem((32,), jnp.int32),
            vmem((32, 64), jnp.int32),
            vmem((64, 32), jnp.int32),
            vmem((32, 128), F32),
            vmem((32, 128), F32),
            vmem((8, 32, 128), F32),
            vmem((8, 128), F32),
            dma((3,)),
            dma((5,)),
            dma((8,)),
            dma((18,)),
            dma((18,)),
            dma(()),
            dma(()),
            dma(()),
            dma(()),
            dma(()),
            dma((8,)),
            dma((8,)),
            dma((4,)),
        ],
        compiler_params=pltpu.CompilerParams(has_side_effects=True, collective_id=1),
        name="cloud_step",
    )(velocity, theta, vapour, radius_sq, multiplicity, counts, pairing, destination, *held)
    return pl.pallas_call(
        final_kernel,
        out_shape=(
            shape((3,) + block, F32),
            shape(block, F32),
            shape(block, F32),
            shape((3, 32), F32),
        ),
        in_specs=[ANY] * 6,
        out_specs=(ANY,) * 4,
        scratch_shapes=[
            vmem((5, DEV, 128), F32),
            vmem((3,) + block, F32),
            vmem(block, F32),
            vmem(block, F32),
            vmem((8, 128), F32),
            vmem((3, 32), F32),
            vmem((2, NZ, NZ), BF16),
            vmem((640, 128), F32),
            dma((6,)),
            dma((4,)),
        ],
        name="project",
    )(modes, star, theta_new, vapour_new, moments, jnp.asarray(t["back"]))


def solution(mesh):
    placed = (
        P(None, "gx", "gy", None),
        P("gx", "gy", None),
        P("gx", "gy", None),
        P(None, ("gx", "gy")),
        P(None, ("gx", "gy")),
        P(("gx", "gy")),
        P(("gx", "gy"), None),
        P(None, ("gx", "gy")),
    )
    return jax.shard_map(
        shards,
        mesh=mesh,
        in_specs=placed,
        out_specs=(
            P(None, "gx", "gy", None),
            P("gx", "gy", None),
            P("gx", "gy", None),
            P(None, ("gx", "gy")),
        ),
        check_vma=False,
    )
```

```python
import functools
import math

import jax
import jax.numpy as jnp
import numpy as np
from jax import lax
from jax.experimental import pallas as pl
from jax.experimental.pallas import tpu as pltpu
from jax.sharding import PartitionSpec as P

MESH = pl.DeviceIdType.MESH
GX, GY = 16, 8
DEV = GX * GY
SX, SY, NZ = 16, 32, 128
NX, NY = 256, 256
HALF = 72
F32 = jnp.float32
BF16 = jnp.bfloat16
FAR_X = (10, 6, 9, 11, 14, 2, 8, 5, 7, 13, 15, 1, 3, 4, 12, 0)
FAR_Y = (4, 3, 5, 2, 6, 1, 7, 0)
ANY = pl.BlockSpec(memory_space=pl.ANY)


def split_table(table):
    table = np.asarray(table, np.float32)
    high = table.astype(jnp.bfloat16)
    low = (table - high.astype(np.float32)).astype(jnp.bfloat16)
    return np.stack([high, low])


@functools.cache
def tables():
    tau = 2.0 * math.pi
    z = np.arange(NZ)
    cosine = np.cos(math.pi * (z[None, :] + 0.5) * z[:, None] / NZ)
    weight = np.where(z == 0, 1.0 / NZ, 2.0 / NZ)
    back = cosine * weight[:, None]
    rows, factor, seen = [], [], set()
    for p in range(16):
        for q in range(8):
            if (p, q) in seen:
                continue
            mirror = (-p % 16, -q % 8)
            seen.update({(p, q), mirror})
            rows.append((p, q))
            factor.append(1.0 if mirror == (p, q) else 2.0)
    pad = HALF - len(rows)
    low_x = np.array([r[0] for r in rows] + [0] * pad)
    low_y = np.array([r[1] for r in rows] + [0] * pad)
    factor = np.array(factor + [0.0] * pad)
    used = np.array([1.0] * len(rows) + [0.0] * pad)
    a = np.repeat(np.arange(16), 8)
    b = np.tile(np.arange(8), 16)
    first, last = [], []
    for c in range(4):
        angle = tau * (
            low_x[:, None] * a[None] / 16.0
            + low_y[:, None] * b[None] / 8.0
            + low_x[:, None] * c / 64.0
        )
        first.append(np.concatenate([np.cos(angle) * used[:, None], -np.sin(angle) * used[:, None]]))
        scale = factor[:, None] / (NX * NY)
        last.append(np.concatenate([np.cos(angle) * scale, -np.sin(angle) * scale]).T)
    lane_i = np.repeat(np.arange(4), 32)
    lane_j = np.tile(np.arange(32), 4)
    turn_cos, turn_sin, wave = [], [], []
    for q in range(4):
        kx0 = low_x + 16 * q
        angle = tau * (kx0[:, None] * lane_i[None] + low_y[:, None] * lane_j[None]) / 256.0
        turn_cos.append(np.cos(angle))
        turn_sin.append(np.sin(angle))
        kx = kx0[:, None] + 64 * lane_i[None]
        ky = low_y[:, None] + 8 * lane_j[None]
        wave.append(-4.0 * np.sin(math.pi * kx / NX) ** 2 - 4.0 * np.sin(math.pi * ky / NY) ** 2)
    turns = np.stack([np.concatenate(turn_cos), np.concatenate(turn_sin), np.concatenate(wave)])
    angle = tau * (lane_i[:, None] * lane_i[None] / 4.0 + lane_j[:, None] * lane_j[None] / 32.0)
    cos2, sin2 = np.cos(angle), np.sin(angle)
    ahead = np.block([[cos2, -sin2], [sin2, cos2]])
    behind = np.block([[cos2, sin2], [-sin2, cos2]])
    wave_z = -4.0 * np.sin(math.pi * z / (2.0 * NZ)) ** 2
    wave_z = np.broadcast_to(wave_z[:, None], (NZ, 128)).astype(np.float32)
    box = np.zeros((32, 128), np.float32)
    for column in range(4):
        for j in range(32):
            box[column * 8 + j // 4, column * 32 + j] = 1.0
    return dict(
        cosine=split_table(cosine),
        first=split_table(np.stack(first)),
        ahead=split_table(ahead),
        behind=split_table(behind),
        last=split_table(np.stack(last)),
        turns=turns.astype(np.float32),
        wave_z=wave_z,
        box=box.astype(jnp.bfloat16),
        back=split_table(back),
    )


def halves(values):
    high = values.astype(BF16)
    return high, (values - high.astype(F32)).astype(BF16)


def product(left, right, dims):
    def one(x, y):
        return lax.dot_general(x, y, (dims, ((), ())), preferred_element_type=F32)

    (left_high, left_low), (right_high, right_low) = left, right
    return one(left_high, right_high) + (one(left_high, right_low) + one(left_low, right_high))


NN = ((1,), (0,))
NT = ((1,), (1,))
TN = ((0,), (0,))


def step_kernel(
    vel, theta, vapour, radius, multi, counts, pairing, dest,
    cosine_h, first_h, ahead_h, behind_h, last_h, turns_h, wave_h, box_h,
    modes, star, theta_out, vapour_out, moments_out,
    fp, ad, xu2, yl, yh, corner, row_y0, below_y, quad, send1, got1, send2,
    cosine, first, ahead, behind, last, turns, wave, box,
    rad_v, mul_v, cnt_v, pair_v, dst_v, cond, load, near, res,
    known, load_sem, drop_sem, table_sem, hs_sem, hr_sem, s1_sem, r1_sem, s2_sem, r2_sem, own_sem,
    ms_sem, mr_sem, out_sem,
):
    gx = lax.axis_index("gx")
    gy = lax.axis_index("gy")
    me = gx * GY + gy
    east, west = lax.rem(gx + 1, GX), lax.rem(gx + GX - 1, GX)
    north, south = lax.rem(gy + 1, GY), lax.rem(gy + GY - 1, GY)
    peers_y = [lax.rem(gy + r, GY) for r in range(GY)]

    loads = [
        pltpu.make_async_copy(vel, fp.at[pl.ds(0, 3), pl.ds(1, SX)], load_sem.at[0]),
        pltpu.make_async_copy(theta, fp.at[3, pl.ds(1, SX)], load_sem.at[1]),
        pltpu.make_async_copy(vapour, fp.at[4, pl.ds(1, SX)], load_sem.at[2]),
    ]
    drops = [
        pltpu.make_async_copy(source, target, drop_sem.at[k])
        for k, (source, target) in enumerate(
            [(radius, rad_v), (multi, mul_v), (counts, cnt_v), (pairing, pair_v), (dest, dst_v)]
        )
    ]
    table_pairs = [
        (cosine_h, cosine), (box_h, box), (first_h, first), (turns_h, turns), (ahead_h, ahead),
        (wave_h, wave), (behind_h, behind), (last_h, last),
    ]
    fetches = [
        pltpu.make_async_copy(source, target, table_sem.at[k])
        for k, (source, target) in enumerate(table_pairs)
    ]
    for copy in loads + drops + fetches:
        copy.start()

    barrier = pltpu.get_barrier_semaphore()

    columns = (gx, east, west)
    lines = (gy, north, south)
    around = [(px, py) for px in columns for py in lines][1:]
    for device in around:
        pl.semaphore_signal(barrier, inc=1, device_id=device, device_id_type=MESH)
    pl.semaphore_wait(barrier, len(around))

    def remote(source, target_ref, k, device):
        return pltpu.make_async_remote_copy(
            src_ref=source, dst_ref=target_ref, send_sem=hs_sem.at[k], recv_sem=hr_sem.at[k],
            device_id=device, device_id_type=MESH,
        )

    wind = [
        remote(vel.at[:, SX - 1], fp.at[pl.ds(0, 3), 0], 0, (east, gy)),
        remote(vel.at[:, 0], fp.at[pl.ds(0, 3), SX + 1], 1, (west, gy)),
        remote(vel.at[0, SX - 2], xu2, 2, (east, gy)),
        remote(vel.at[:, :, SY - 1], yl.at[pl.ds(0, 3)], 3, (gx, north)),
        remote(vel.at[:, :, 0], yh.at[pl.ds(0, 3)], 4, (gx, south)),
        remote(vel.at[1, :, SY - 2], yl.at[5], 5, (gx, north)),
        remote(vel.at[0, SX - 1, pl.ds(SY - 1, 1)], corner.at[0, pl.ds(0, 1)], 6, (east, north)),
        remote(vel.at[0, SX - 1, pl.ds(0, 1)], corner.at[1, pl.ds(0, 1)], 7, (east, south)),
        remote(vel.at[1, SX - 1, pl.ds(SY - 1, 1)], corner.at[2, pl.ds(0, 1)], 8, (east, north)),
        remote(vel.at[1, 0, pl.ds(SY - 1, 1)], corner.at[3, pl.ds(0, 1)], 9, (west, north)),
    ]
    air = [
        remote(theta.at[SX - 1], fp.at[3, 0], 10, (east, gy)),
        remote(vapour.at[SX - 1], fp.at[4, 0], 11, (east, gy)),
        remote(theta.at[0], fp.at[3, SX + 1], 12, (west, gy)),
        remote(vapour.at[0], fp.at[4, SX + 1], 13, (west, gy)),
        remote(theta.at[:, SY - 1], yl.at[3], 14, (gx, north)),
        remote(vapour.at[:, SY - 1], yl.at[4], 15, (gx, north)),
        remote(theta.at[:, 0], yh.at[3], 16, (gx, south)),
        remote(vapour.at[:, 0], yh.at[4], 17, (gx, south)),
    ]
    halo = wind + air
    for copy in halo:
        copy.start()

    def pass_on(k, devices):
        for device in devices:
            pl.semaphore_signal(known.at[k], inc=1, device_id=device, device_id_type=MESH)

    def away(step_x, step_y):
        return lax.rem(gx + GX + step_x, GX), lax.rem(gy + GY + step_y, GY)

    second = [away(i, j) for i in (-2, 0, 2) for j in (-2, 0, 2) if i or j]
    third = [away(-4, 0), away(4, 0)]
    pass_on(0, around)
    for copy in loads:
        copy.wait()

    row = lax.broadcasted_iota(jnp.int32, (SY, NZ), 0)
    lane = lax.broadcasted_iota(jnp.int32, (SY, NZ), 1)
    tile_row = lax.broadcasted_iota(jnp.int32, (8, NZ), 0)

    def upward(values):
        return pltpu.roll(values, NZ - 1, 1)

    def downward(values):
        return pltpu.roll(values, 1, 1)

    def coefficients(speed, shape_lane=None):
        scaled = 0.1 * speed
        return 0.01 - scaled, 0.01 + scaled

    def vertical(speed, lanes):
        up, down = coefficients(speed)
        top, bottom = lanes == NZ - 1, lanes == 0
        centre = 0.94 + jnp.where(top, up, 0.0) + jnp.where(bottom, down, 0.0)
        return jnp.where(top, 0.0, up), jnp.where(bottom, 0.0, down), centre

    def advect_plane(x, fields):
        c_east, c_west = coefficients(fp[0, x + 1])
        c_north, c_south = coefficients(fp[1, x + 1])
        c_north = jnp.where(row == SY - 1, 0.0, c_north)
        c_south = jnp.where(row == 0, 0.0, c_south)
        c_up, c_down, c_mid = vertical(fp[2, x + 1], lane)
        for f in fields:
            centre = fp[f, x + 1]
            ad[f, x + 1] = (
                (c_mid * centre + c_east * fp[f, x + 2] + c_west * fp[f, x])
                + (c_north * pltpu.roll(centre, SY - 1, 0) + c_south * pltpu.roll(centre, 1, 0))
                + (c_up * upward(centre) + c_down * downward(centre))
            )

    def inner(x, carry):
        advect_plane(x, (0, 1, 2))
        row_y0[pl.ds(x, 1), :] = fp[1, x + 1, 0:1, :]
        return carry

    lax.fori_loop(1, SX - 1, inner, 0)
    pl.semaphore_wait(known.at[0], len(around))
    pass_on(1, second)
    for x in (0, SX - 1):
        row_y0[pl.ds(x, 1), :] = fp[1, x + 1, 0:1, :]
    for copy in wind:
        copy.wait_recv()
    pl.semaphore_wait(known.at[1], len(second))
    pass_on(2, third)
    advect_plane(0, (0, 1, 2))
    advect_plane(SX - 1, (0, 1, 2))

    speed = fp[0, 0]
    c_east, c_west = coefficients(speed)
    c_north, c_south = coefficients(fp[1, 0])
    c_up, c_down, c_mid = vertical(fp[2, 0], lane)
    above = jnp.where(row == SY - 1, corner[1, 0:1, :], pltpu.roll(speed, SY - 1, 0))
    beneath = jnp.where(row == 0, corner[0, 0:1, :], pltpu.roll(speed, 1, 0))
    ad[0, 0] = (
        (c_mid * speed + c_east * fp[0, 1] + c_west * xu2[...])
        + (c_north * above + c_south * beneath)
        + (c_up * upward(speed) + c_down * downward(speed))
    )
    speed = yl[1]
    row_x = lax.broadcasted_iota(jnp.int32, (SX, NZ), 0)
    lane_x = lax.broadcasted_iota(jnp.int32, (SX, NZ), 1)
    c_east, c_west = coefficients(yl[0])
    c_north, c_south = coefficients(speed)
    c_up, c_down, c_mid = vertical(yl[2], lane_x)
    after = jnp.where(row_x == SX - 1, corner[3, 0:1, :], pltpu.roll(speed, SX - 1, 0))
    before = jnp.where(row_x == 0, corner[2, 0:1, :], pltpu.roll(speed, 1, 0))
    below_y[...] = (
        (c_mid * speed + c_east * after + c_west * before)
        + (c_north * row_y0[...] + c_south * yl[5])
        + (c_up * upward(speed) + c_down * downward(speed))
    )
    fetches[0].wait()

    def border(x, fields):
        _, c_south = coefficients(fp[1, x + 1, 0:8, :])
        c_north, _ = coefficients(fp[1, x + 1, SY - 8 : SY, :])
        c_south = jnp.where(tile_row == 0, c_south, 0.0)
        c_north = jnp.where(tile_row == 7, c_north, 0.0)
        for f in fields:
            ad[f, x + 1, 0:8, :] += c_south * yl[f, pl.ds(x, 1), :]
            ad[f, x + 1, SY - 8 : SY, :] += c_north * yh[f, pl.ds(x, 1), :]

    def block(c, carry):
        parts = []
        for i in range(4):
            x = c * 4 + i
            border(x, (0, 1, 2))
            star_w = ad[2, x + 1] + 0.1 * fp[3, x + 1]
            ad[2, x + 1] = star_w
            star_v = ad[1, x + 1]
            behind_v = jnp.where(row == 0, below_y[pl.ds(x, 1), :], pltpu.roll(star_v, 1, 0))
            below_w = jnp.where(lane == 0, 0.0, downward(star_w))
            parts.append((ad[0, x + 1] - ad[0, x]) + (star_v - behind_v) + (star_w - below_w))
        chunk = jnp.concatenate(parts, axis=0)
        send1[c] = product((cosine[0], cosine[1]), halves(chunk), NT)
        return carry

    def scalars(c, carry):
        total = jnp.zeros((SY, NZ), F32)
        for i in range(4):
            x = c * 4 + i
            advect_plane(x, (3, 4))
            border(x, (3, 4))
            total = total + ad[4, x + 1]
        quad[c] = total
        return carry

    lax.fori_loop(0, 4, block, 0)
    pl.semaphore_wait(known.at[2], len(third))

    def scatter(source, target_ref, send_sem, recv_sem):
        def one(px, ry):
            py = peers_y[ry]
            pltpu.make_async_remote_copy(
                src_ref=source.at[:, pl.ds(px * GY + py, 1), :],
                dst_ref=target_ref.at[:, pl.ds(me, 1), :],
                send_sem=send_sem, recv_sem=recv_sem, device_id=(px, py), device_id_type=MESH,
            ).start()

        for rx in FAR_X:
            px = lax.rem(gx + rx, GX)
            for ry in FAR_Y:
                if rx or ry:
                    one(px, ry)

    def drained(source, target_ref, sem):
        count = pl.ds(0, DEV - 1)
        pltpu.make_async_copy(source.at[:, count, :], target_ref.at[:, count, :], sem).wait()

    scatter(send1, got1, s1_sem, r1_sem)
    got1[:, pl.ds(me, 1), :] = send1[:, pl.ds(me, 1), :]

    outs = [
        pltpu.make_async_copy(ad.at[pl.ds(0, 3), pl.ds(1, SX)], star, out_sem.at[0]),
        pltpu.make_async_copy(ad.at[3, pl.ds(1, SX)], theta_out, out_sem.at[1]),
        pltpu.make_async_copy(ad.at[4, pl.ds(1, SX)], vapour_out, out_sem.at[2]),
    ]
    outs[0].start()
    for copy in drops:
        copy.wait()
    box_row = lax.broadcasted_iota(jnp.int32, (32, 32), 0)
    box_lane = lax.broadcasted_iota(jnp.int32, (32, 32), 1)
    spread = jnp.where(box_row == box_lane, cnt_v[...][None, :].astype(F32), 0.0)
    used = jnp.sum(spread, axis=1, keepdims=True)
    slot = lax.broadcasted_iota(jnp.int32, (32, 64), 1).astype(F32)
    live = jnp.where(slot < used, mul_v[...], 0.0)
    target = dst_v[...]
    local_box = lax.broadcasted_iota(jnp.int32, (32, 64), 0)
    source_x = gx * 4 + (local_box >> 3)
    source_y = gy * 8 + (local_box & 7)
    target_x = (target >> 8) * 4 + ((target & 31) >> 3)
    target_y = ((target >> 5) & 7) * 8 + (target & 7)
    offset_x = (target_x - source_x + 1) & 63
    offset_y = (target_y - source_y + 1) & 63
    code = (offset_x * 3 + offset_y).astype(F32)

    def twice(values):
        return jnp.concatenate([values, values], axis=1)

    pair = twice(pair_v[...])
    order = jnp.where(lax.broadcasted_iota(jnp.int32, (32, 128), 1) < 64, pair, pltpu.roll(pair, 32, 1))
    radius_p = jnp.take_along_axis(twice(rad_v[...]), order, axis=1)
    live_p = jnp.take_along_axis(twice(live), order, axis=1)
    code_p = jnp.take_along_axis(twice(code), order, axis=1)

    for copy in air:
        copy.wait_recv()
    lax.fori_loop(0, 4, scalars, 0)
    outs[1].start()
    fetches[1].wait()
    high, low = halves(quad[...].reshape(128, NZ))
    sums = lax.dot_general(box[...], high, (NN, ((), ())), preferred_element_type=F32)
    sums = sums + lax.dot_general(box[...], low, (NN, ((), ())), preferred_element_type=F32)
    mean = jnp.sum(sums, axis=1, keepdims=True) * (1.0 / (16 * NZ))
    soft = jnp.maximum(mean, 0.0) + jnp.log1p(jnp.exp(-jnp.abs(mean)))
    grown = radius_p + 0.5 * soft
    root = jnp.sqrt(grown)
    mass = grown * root
    gain = mass - radius_p * jnp.sqrt(radius_p)

    def other(values):
        return pltpu.roll(values, 64, 1)

    root_sum = root + other(root)
    rate = 0.05 * (root_sum * root_sum * jnp.abs(grown - other(grown)) * other(live_p))
    final = (mass + rate * other(mass)) / (1.0 + rate)
    lanes = lax.broadcasted_iota(jnp.int32, (32, 128), 1)
    own_live = jnp.where(lanes < 64, live_p, 0.0)
    cond[...] = jnp.broadcast_to(jnp.sum(own_live * gain, axis=1, keepdims=True), (32, 128)) * 0.002
    carried = [own_live, own_live * final, own_live * final * final]
    packed = jnp.zeros((32, 128), F32)
    for d in range(9):
        chosen = code_p == float(d)
        for k in range(3):
            amount = jnp.sum(jnp.where(chosen, carried[k], 0.0), axis=1, keepdims=True)
            packed = packed + jnp.where(lanes == d * 3 + k, amount, 0.0)
    load[...] = packed

    def share(source, target_ref, k, device):
        return pltpu.make_async_remote_copy(
            src_ref=source, dst_ref=target_ref, send_sem=ms_sem.at[k], recv_sem=mr_sem.at[k],
            device_id=device, device_id_type=MESH,
        )

    top, bottom = pl.ds(24, 8), pl.ds(0, 8)
    shares = [
        share(load.at[top], near.at[0, bottom], 0, (east, gy)),
        share(load.at[bottom], near.at[1, bottom], 1, (west, gy)),
        share(load, near.at[2], 2, (gx, north)),
        share(load, near.at[3], 3, (gx, south)),
        share(load.at[top], near.at[4, bottom], 4, (east, north)),
        share(load.at[top], near.at[5, bottom], 5, (east, south)),
        share(load.at[bottom], near.at[6, bottom], 6, (west, north)),
        share(load.at[bottom], near.at[7, bottom], 7, (west, south)),
    ]
    for copy in shares:
        copy.start()

    def dry(x, carry):
        first_box = (x // 4) * 8
        for t in range(4):
            drop = jnp.where(
                tile_row < 4,
                cond[pl.ds(first_box + 2 * t, 1), :],
                cond[pl.ds(first_box + 2 * t + 1, 1), :],
            )
            ad[4, x + 1, 8 * t : 8 * t + 8, :] -= drop
        return carry

    lax.fori_loop(0, SX, dry, 0)
    outs[2].start()

    for copy in fetches[2:]:
        copy.wait()
    drained(send1, got1, r1_sem)
    z_re, z_im = [], []
    for c in range(4):
        both = product((first[0, c], first[1, c]), halves(got1[c]), NN)
        z_re.append(both[:HALF])
        z_im.append(both[HALF:])

    def butterfly(re, im, sign):
        s02r, s02i = re[0] + re[2], im[0] + im[2]
        d02r, d02i = re[0] - re[2], im[0] - im[2]
        s13r, s13i = re[1] + re[3], im[1] + im[3]
        d13r, d13i = re[1] - re[3], im[1] - im[3]
        if sign < 0:
            return (
                [s02r + s13r, d02r + d13i, s02r - s13r, d02r - d13i],
                [s02i + s13i, d02i - d13r, s02i - s13i, d02i + d13r],
            )
        return (
            [s02r + s13r, d02r - d13i, s02r - s13r, d02r + d13i],
            [s02i + s13i, d02i + d13r, s02i - s13i, d02i - d13r],
        )

    q_re, q_im = butterfly(z_re, z_im, -1)
    re, im = jnp.concatenate(q_re, axis=0), jnp.concatenate(q_im, axis=0)
    turn_cos, turn_sin = turns[0], turns[1]
    joined = jnp.concatenate([re * turn_cos + im * turn_sin, im * turn_cos - re * turn_sin], axis=1)
    spectrum = product(halves(joined), (ahead[0], ahead[1]), NN)
    eigen = turns[2] + wave[pl.ds(me, 1), :]
    inverse = jnp.where(eigen == 0.0, 0.0, 1.0 / jnp.where(eigen == 0.0, 1.0, eigen))
    solved = spectrum * jnp.concatenate([inverse, inverse], axis=1)
    turned = product(halves(solved), (behind[0], behind[1]), NN)
    re, im = turned[:, :128], turned[:, 128:]
    back_re, back_im = re * turn_cos - im * turn_sin, im * turn_cos + re * turn_sin
    v_re, v_im = butterfly(
        [back_re[HALF * q : HALF * (q + 1)] for q in range(4)],
        [back_im[HALF * q : HALF * (q + 1)] for q in range(4)],
        1,
    )
    wide_lane = lax.broadcasted_iota(jnp.int32, (128, 128), 1)
    edge = None
    for c in range(4):
        stacked = jnp.concatenate([v_re[c], v_im[c]], axis=0)
        plane = product((last[0, c], last[1, c]), halves(stacked), NN)
        send2[c] = plane
        if c == 0:
            next_x = pltpu.roll(plane, 120, 0)
        picked = jnp.where((wide_lane & 31) == 0, plane, 0.0)
        picked = picked if c == 0 else pltpu.roll(picked, c, 1)
        edge = picked if edge is None else edge + picked
    row_b = lax.broadcasted_iota(jnp.int32, (128, 128), 0) & 7
    edge = jnp.where(row_b == 7, pltpu.roll(edge, 7, 0), pltpu.roll(edge, 127, 0))
    moved = pltpu.roll(edge, 36, 1)
    in_move = (wide_lane >= 36) & (wide_lane < 40)
    send2[4] = jnp.where(wide_lane < 32, next_x, jnp.where(in_move, moved, edge))

    scatter(send2, modes, s2_sem, r2_sem)
    own = pltpu.make_async_copy(
        send2.at[:, pl.ds(me, 1), :], modes.at[:, pl.ds(me, 1), :], own_sem
    )
    own.start()

    for copy in shares:
        copy.wait_recv()
    tile_lane = lax.broadcasted_iota(jnp.int32, (8, 128), 1)

    def column_of(x):
        if x < 0:
            return near[0, 0:8, :], near[4, 7:8, :], near[5, 0:1, :]
        if x > 3:
            return near[1, 0:8, :], near[6, 7:8, :], near[7, 0:1, :]
        return load[8 * x : 8 * x + 8, :], near[2, 8 * x + 7 : 8 * x + 8, :], near[3, 8 * x : 8 * x + 1, :]

    arrived = [jnp.zeros((8, 128), F32) for _ in range(4)]
    for x in range(-1, 5):
        centre, low_row, high_row = column_of(x)
        shifted = [
            jnp.where(tile_row == 7, high_row, pltpu.roll(centre, 7, 0)),
            centre,
            jnp.where(tile_row == 0, low_row, pltpu.roll(centre, 1, 0)),
        ]
        for dx in (-1, 0, 1):
            if not 0 <= x + dx < 4:
                continue
            for dy in (-1, 0, 1):
                d = (dx + 1) * 3 + dy + 1
                values = shifted[dy + 1]
                values = values if d == 0 else pltpu.roll(values, 128 - 3 * d, 1)
                arrived[x + dx] = arrived[x + dx] + values
    stacked = jnp.concatenate(arrived + [jnp.zeros((96, 128), F32)], axis=0) * (1.0 / 64)
    res[...] = stacked.T[0:8, :]
    outs.append(pltpu.make_async_copy(res, moments_out, out_sem.at[3]))
    outs[3].start()

    for copy in halo:
        copy.wait_send()
    for copy in shares:
        copy.wait_send()
    drained(send1, got1, s1_sem)
    for copy in outs:
        copy.wait()
    own.wait()
    drained(send2, send2, s2_sem)
    drained(send2, modes, r2_sem)


def final_kernel(
    modes, star, theta, vapour, moments, back_h,
    vel_out, theta_out, vapour_out, moments_out,
    mode_v, star_v, theta_v, vapour_v, mom_v, mom_o, back, pressure, in_sem, out_sem,
):
    loads = [
        pltpu.make_async_copy(source, target, in_sem.at[k])
        for k, (source, target) in enumerate(
            [(modes, mode_v), (back_h, back), (star, star_v), (theta, theta_v), (vapour, vapour_v), (moments, mom_v)]
        )
    ]
    for copy in loads:
        copy.start()
    loads[0].wait()
    loads[1].wait()
    for c in range(5):
        pressure[pl.ds(128 * c, 128), :] = product(halves(mode_v[c]), (back[0], back[1]), TN)
    for copy in loads[2:]:
        copy.wait()
    mom_o[...] = mom_v[0:3, 0:32]
    outs = [
        pltpu.make_async_copy(theta_v, theta_out, out_sem.at[0]),
        pltpu.make_async_copy(vapour_v, vapour_out, out_sem.at[1]),
        pltpu.make_async_copy(mom_o, moments_out, out_sem.at[2]),
    ]
    for copy in outs:
        copy.start()
    row = lax.broadcasted_iota(jnp.int32, (SY, NZ), 0)
    lane = lax.broadcasted_iota(jnp.int32, (SY, NZ), 1)
    for x in range(SX):
        c, i = x // 4, x % 4
        here = pressure[pl.ds(32 * x, 32), :]
        ahead = pressure[pl.ds(32 * x + 32, 32), :]
        line = 512 + (36, 32, 64, 96)[i] + c
        side = jnp.where(row == SY - 1, pressure[line : line + 1, :], pltpu.roll(here, SY - 1, 0))
        above = jnp.where(lane == NZ - 1, here, pltpu.roll(here, NZ - 1, 1))
        star_v[0, x] = star_v[0, x] - (ahead - here)
        star_v[1, x] = star_v[1, x] - (side - here)
        star_v[2, x] = star_v[2, x] - (above - here)
    last = pltpu.make_async_copy(star_v, vel_out, out_sem.at[3])
    last.start()
    for copy in outs:
        copy.wait()
    last.wait()


def shards(velocity, theta, vapour, radius_sq, multiplicity, counts, pairing, destination):
    t = tables()
    names = ["cosine", "first", "ahead", "behind", "last", "turns", "wave_z", "box"]
    held = [jnp.asarray(t[name]) for name in names]
    block = (SX, SY, NZ)
    shape = jax.ShapeDtypeStruct
    vmem = pltpu.VMEM
    dma = pltpu.SemaphoreType.DMA
    modes, star, theta_new, vapour_new, moments = pl.pallas_call(
        step_kernel,
        out_shape=(
            shape((5, DEV, 128), F32),
            shape((3,) + block, F32),
            shape(block, F32),
            shape(block, F32),
            shape((8, 128), F32),
        ),
        in_specs=[ANY] * 16,
        out_specs=(ANY,) * 5,
        scratch_shapes=[
            vmem((5, SX + 2, SY, NZ), F32),
            vmem((5, SX + 1, SY, NZ), F32),
            vmem((SY, NZ), F32),
            vmem((6, SX, NZ), F32),
            vmem((5, SX, NZ), F32),
            vmem((4, 8, NZ), F32),
            vmem((SX, NZ), F32),
            vmem((SX, NZ), F32),
            vmem((4, SY, NZ), F32),
            vmem((4, DEV, 128), F32),
            vmem((4, DEV, 128), F32),
            vmem((5, DEV, 128), F32),
        ]
        + [vmem(t[name].shape, t[name].dtype) for name in names]
        + [
            vmem((32, 64), F32),
            vmem((32, 64), F32),
            vmem((32,), jnp.int32),
            vmem((32, 64), jnp.int32),
            vmem((32, 64), jnp.int32),
            vmem((32, 128), F32),
            vmem((32, 128), F32),
            vmem((8, 32, 128), F32),
            vmem((8, 128), F32),
            pltpu.SemaphoreType.REGULAR((3,)),
            dma((3,)),
            dma((5,)),
            dma((8,)),
            dma((18,)),
            dma((18,)),
            dma(()),
            dma(()),
            dma(()),
            dma(()),
            dma(()),
            dma((8,)),
            dma((8,)),
            dma((4,)),
        ],
        compiler_params=pltpu.CompilerParams(has_side_effects=True, collective_id=1),
        name="cloud_step",
    )(velocity, theta, vapour, radius_sq.T, multiplicity.T, counts, pairing, destination.T, *held)
    return pl.pallas_call(
        final_kernel,
        out_shape=(
            shape((3,) + block, F32),
            shape(block, F32),
            shape(block, F32),
            shape((3, 32), F32),
        ),
        in_specs=[ANY] * 6,
        out_specs=(ANY,) * 4,
        scratch_shapes=[
            vmem((5, DEV, 128), F32),
            vmem((3,) + block, F32),
            vmem(block, F32),
            vmem(block, F32),
            vmem((8, 128), F32),
            vmem((3, 32), F32),
            vmem((2, NZ, NZ), BF16),
            vmem((640, 128), F32),
            dma((6,)),
            dma((4,)),
        ],
        name="project",
    )(modes, star, theta_new, vapour_new, moments, jnp.asarray(t["back"]))


def solution(mesh):
    placed = (
        P(None, "gx", "gy", None),
        P("gx", "gy", None),
        P("gx", "gy", None),
        P(None, ("gx", "gy")),
        P(None, ("gx", "gy")),
        P(("gx", "gy")),
        P(("gx", "gy"), None),
        P(None, ("gx", "gy")),
    )
    return jax.shard_map(
        shards,
        mesh=mesh,
        in_specs=placed,
        out_specs=(
            P(None, "gx", "gy", None),
            P("gx", "gy", None),
            P("gx", "gy", None),
            P(None, ("gx", "gy")),
        ),
        check_vma=False,
    )
```

```python
import functools
import math

import jax
import jax.numpy as jnp
import numpy as np
from jax import lax
from jax.experimental import pallas as pl
from jax.experimental.pallas import tpu as pltpu
from jax.sharding import PartitionSpec as P

MESH = pl.DeviceIdType.MESH
GX, GY = 16, 8
DEV = GX * GY
SX, SY, NZ = 16, 32, 128
NX, NY = 256, 256
HALF = 72
F32 = jnp.float32
BF16 = jnp.bfloat16
ANY = pl.BlockSpec(memory_space=pl.ANY)


def split_table(table):
    table = np.asarray(table, np.float32)
    high = table.astype(jnp.bfloat16)
    low = (table - high.astype(np.float32)).astype(jnp.bfloat16)
    return np.stack([high, low])


@functools.cache
def send_order():
    hops = (0, 1, 2, 1)
    peers = [(rx, ry) for rx in range(GX) for ry in range(GY) if rx or ry]
    peers.sort(key=lambda p: -(hops[p[0] // 4] + hops[p[0] % 4] + hops[p[1] // 2]))
    classes = {}
    for p in peers:
        classes.setdefault((p[0] // 4 > 2, p[0] % 4 > 2, p[1] // 2 > 2, p[1] % 2), []).append(p)
    queues = list(classes.values())
    order = []
    while any(queues):
        for queue in queues:
            if queue:
                order.append(queue.pop(0))
    return tuple(order)


@functools.cache
def tables():
    tau = 2.0 * math.pi
    z = np.arange(NZ)
    cosine = np.cos(math.pi * (z[None, :] + 0.5) * z[:, None] / NZ)
    weight = np.where(z == 0, 1.0 / NZ, 2.0 / NZ)
    back = cosine * weight[:, None]
    rows, factor, seen = [], [], set()
    for p in range(16):
        for q in range(8):
            if (p, q) in seen:
                continue
            mirror = (-p % 16, -q % 8)
            seen.update({(p, q), mirror})
            rows.append((p, q))
            factor.append(1.0 if mirror == (p, q) else 2.0)
    pad = HALF - len(rows)
    low_x = np.array([r[0] for r in rows] + [0] * pad)
    low_y = np.array([r[1] for r in rows] + [0] * pad)
    factor = np.array(factor + [0.0] * pad)
    used = np.array([1.0] * len(rows) + [0.0] * pad)
    a = np.repeat(np.arange(16), 8)
    b = np.tile(np.arange(8), 16)
    first, last = [], []
    for c in range(4):
        angle = tau * (
            low_x[:, None] * a[None] / 16.0
            + low_y[:, None] * b[None] / 8.0
            + low_x[:, None] * c / 64.0
        )
        first.append(np.concatenate([np.cos(angle) * used[:, None], -np.sin(angle) * used[:, None]]))
        scale = factor[:, None] / (NX * NY)
        last.append(np.concatenate([np.cos(angle) * scale, -np.sin(angle) * scale]).T)
    lane_i = np.repeat(np.arange(4), 32)
    lane_j = np.tile(np.arange(32), 4)
    turn_cos, turn_sin, wave = [], [], []
    for q in range(4):
        kx0 = low_x + 16 * q
        angle = tau * (kx0[:, None] * lane_i[None] + low_y[:, None] * lane_j[None]) / 256.0
        turn_cos.append(np.cos(angle))
        turn_sin.append(np.sin(angle))
        kx = kx0[:, None] + 64 * lane_i[None]
        ky = low_y[:, None] + 8 * lane_j[None]
        wave.append(-4.0 * np.sin(math.pi * kx / NX) ** 2 - 4.0 * np.sin(math.pi * ky / NY) ** 2)
    turns = np.stack([np.concatenate(turn_cos), np.concatenate(turn_sin), np.concatenate(wave)])
    angle = tau * (lane_i[:, None] * lane_i[None] / 4.0 + lane_j[:, None] * lane_j[None] / 32.0)
    cos2, sin2 = np.cos(angle), np.sin(angle)
    ahead = np.block([[cos2, -sin2], [sin2, cos2]])
    behind = np.block([[cos2, sin2], [-sin2, cos2]])
    wave_z = -4.0 * np.sin(math.pi * z / (2.0 * NZ)) ** 2
    wave_z = np.broadcast_to(wave_z[:, None], (NZ, 128)).astype(np.float32)
    box = np.zeros((32, 128), np.float32)
    for column in range(4):
        for j in range(32):
            box[column * 8 + j // 4, column * 32 + j] = 1.0
    return dict(
        cosine=split_table(cosine),
        first=split_table(np.stack(first)),
        ahead=split_table(ahead),
        behind=split_table(behind),
        last=split_table(np.stack(last)),
        turns=turns.astype(np.float32),
        wave_z=wave_z,
        box=box.astype(jnp.bfloat16),
        back=split_table(back),
    )


def halves(values):
    high = values.astype(BF16)
    return high, (values - high.astype(F32)).astype(BF16)


def product(left, right, dims):
    def one(x, y):
        return lax.dot_general(x, y, (dims, ((), ())), preferred_element_type=F32)

    (left_high, left_low), (right_high, right_low) = left, right
    return one(left_high, right_high) + (one(left_high, right_low) + one(left_low, right_high))


NN = ((1,), (0,))
NT = ((1,), (1,))
TN = ((0,), (0,))


def step_kernel(
    vel, theta, vapour, radius, multi, counts, pairing, dest,
    cosine_h, first_h, ahead_h, behind_h, last_h, turns_h, wave_h, box_h,
    modes, star, theta_out, vapour_out, moments_out,
    fp, ad, xu2, yl, yh, corner, row_y0, below_y, quad, send1, got1, send2,
    cosine, first, ahead, behind, last, turns, wave, box,
    rad_v, mul_v, cnt_v, pair_v, dst_v, cond, load, near, res,
    known, load_sem, drop_sem, table_sem, hs_sem, hr_sem, s1_sem, r1_sem, s2_sem, r2_sem, own_sem,
    ms_sem, mr_sem, out_sem,
):
    gx = lax.axis_index("gx")
    gy = lax.axis_index("gy")
    me = gx * GY + gy
    east, west = lax.rem(gx + 1, GX), lax.rem(gx + GX - 1, GX)
    north, south = lax.rem(gy + 1, GY), lax.rem(gy + GY - 1, GY)
    peers_x = [lax.rem(gx + r, GX) for r in range(GX)]
    peers_y = [lax.rem(gy + r, GY) for r in range(GY)]

    loads = [
        pltpu.make_async_copy(vel, fp.at[pl.ds(0, 3), pl.ds(1, SX)], load_sem.at[0]),
        pltpu.make_async_copy(theta, fp.at[3, pl.ds(1, SX)], load_sem.at[1]),
        pltpu.make_async_copy(vapour, fp.at[4, pl.ds(1, SX)], load_sem.at[2]),
    ]
    drops = [
        pltpu.make_async_copy(source, target, drop_sem.at[k])
        for k, (source, target) in enumerate(
            [(radius, rad_v), (multi, mul_v), (counts, cnt_v), (pairing, pair_v), (dest, dst_v)]
        )
    ]
    table_pairs = [
        (cosine_h, cosine), (box_h, box), (first_h, first), (turns_h, turns), (ahead_h, ahead),
        (wave_h, wave), (behind_h, behind), (last_h, last),
    ]
    fetches = [
        pltpu.make_async_copy(source, target, table_sem.at[k])
        for k, (source, target) in enumerate(table_pairs)
    ]
    for copy in loads + drops + fetches:
        copy.start()

    barrier = pltpu.get_barrier_semaphore()

    chip_z, chip_x, chip_y, core = gx // 4, lax.rem(gx, 4), gy // 2, lax.rem(gy, 2)

    def away(step_z, step_x, step_y, step_core):
        to_z, to_x, to_y = (
            lax.rem(at + 4 + step, 4)
            for at, step in ((chip_z, step_z), (chip_x, step_x), (chip_y, step_y))
        )
        return to_z * 4 + to_x, to_y * 2 + lax.rem(core + step_core, 2)

    steps = [(k, i, j, n) for k in (0, 1, -1) for i in (1, -1, 0) for j in (1, -1, 0) for n in (0, 1)]
    around = [away(*step) for step in steps if any(step)]
    corners = [away(k, i, j, 0) for k in (1, -1) for i in (1, -1) for j in (1, -1)]
    for device in around:
        pl.semaphore_signal(barrier, inc=1, device_id=device, device_id_type=MESH)
    pl.semaphore_wait(barrier, len(around))

    def remote(source, target_ref, k, device):
        return pltpu.make_async_remote_copy(
            src_ref=source, dst_ref=target_ref, send_sem=hs_sem.at[k], recv_sem=hr_sem.at[k],
            device_id=device, device_id_type=MESH,
        )

    wind = [
        remote(vel.at[:, SX - 1], fp.at[pl.ds(0, 3), 0], 0, (east, gy)),
        remote(vel.at[:, 0], fp.at[pl.ds(0, 3), SX + 1], 1, (west, gy)),
        remote(vel.at[0, SX - 2], xu2, 2, (east, gy)),
        remote(vel.at[:, :, SY - 1], yl.at[pl.ds(0, 3)], 3, (gx, north)),
        remote(vel.at[:, :, 0], yh.at[pl.ds(0, 3)], 4, (gx, south)),
        remote(vel.at[1, :, SY - 2], yl.at[5], 5, (gx, north)),
        remote(vel.at[0, SX - 1, pl.ds(SY - 1, 1)], corner.at[0, pl.ds(0, 1)], 6, (east, north)),
        remote(vel.at[0, SX - 1, pl.ds(0, 1)], corner.at[1, pl.ds(0, 1)], 7, (east, south)),
        remote(vel.at[1, SX - 1, pl.ds(SY - 1, 1)], corner.at[2, pl.ds(0, 1)], 8, (east, north)),
        remote(vel.at[1, 0, pl.ds(SY - 1, 1)], corner.at[3, pl.ds(0, 1)], 9, (west, north)),
    ]
    air = [
        remote(theta.at[SX - 1], fp.at[3, 0], 10, (east, gy)),
        remote(vapour.at[SX - 1], fp.at[4, 0], 11, (east, gy)),
        remote(theta.at[0], fp.at[3, SX + 1], 12, (west, gy)),
        remote(vapour.at[0], fp.at[4, SX + 1], 13, (west, gy)),
        remote(theta.at[:, SY - 1], yl.at[3], 14, (gx, north)),
        remote(vapour.at[:, SY - 1], yl.at[4], 15, (gx, north)),
        remote(theta.at[:, 0], yh.at[3], 16, (gx, south)),
        remote(vapour.at[:, 0], yh.at[4], 17, (gx, south)),
    ]
    halo = wind + air
    for copy in wind[6:] + wind[:6]:
        copy.start()

    def pass_on(k, devices):
        for device in devices:
            pl.semaphore_signal(known.at[k], inc=1, device_id=device, device_id_type=MESH)

    pass_on(0, corners)
    for copy in loads:
        copy.wait()

    row = lax.broadcasted_iota(jnp.int32, (SY, NZ), 0)
    lane = lax.broadcasted_iota(jnp.int32, (SY, NZ), 1)
    tile_row = lax.broadcasted_iota(jnp.int32, (8, NZ), 0)

    def upward(values):
        return pltpu.roll(values, NZ - 1, 1)

    def downward(values):
        return pltpu.roll(values, 1, 1)

    def coefficients(speed, shape_lane=None):
        scaled = 0.1 * speed
        return 0.01 - scaled, 0.01 + scaled

    def vertical(speed, lanes):
        up, down = coefficients(speed)
        top, bottom = lanes == NZ - 1, lanes == 0
        centre = 0.94 + jnp.where(top, up, 0.0) + jnp.where(bottom, down, 0.0)
        return jnp.where(top, 0.0, up), jnp.where(bottom, 0.0, down), centre

    def advect_plane(x, fields):
        c_east, c_west = coefficients(fp[0, x + 1])
        c_north, c_south = coefficients(fp[1, x + 1])
        c_north = jnp.where(row == SY - 1, 0.0, c_north)
        c_south = jnp.where(row == 0, 0.0, c_south)
        c_up, c_down, c_mid = vertical(fp[2, x + 1], lane)
        for f in fields:
            centre = fp[f, x + 1]
            ad[f, x + 1] = (
                (c_mid * centre + c_east * fp[f, x + 2] + c_west * fp[f, x])
                + (c_north * pltpu.roll(centre, SY - 1, 0) + c_south * pltpu.roll(centre, 1, 0))
                + (c_up * upward(centre) + c_down * downward(centre))
            )

    def inner(x, carry):
        advect_plane(x, (0, 1, 2))
        row_y0[pl.ds(x, 1), :] = fp[1, x + 1, 0:1, :]
        return carry

    lax.fori_loop(1, SX - 1, inner, 0)
    for copy in drops:
        copy.wait()
    box_row = lax.broadcasted_iota(jnp.int32, (32, 32), 0)
    box_lane = lax.broadcasted_iota(jnp.int32, (32, 32), 1)
    spread = jnp.where(box_row == box_lane, cnt_v[...][None, :].astype(F32), 0.0)
    used = jnp.sum(spread, axis=1, keepdims=True)
    slot = lax.broadcasted_iota(jnp.int32, (32, 64), 1).astype(F32)
    live = jnp.where(slot < used, mul_v[...], 0.0)
    target = dst_v[...]
    local_box = lax.broadcasted_iota(jnp.int32, (32, 64), 0)
    source_x = gx * 4 + (local_box >> 3)
    source_y = gy * 8 + (local_box & 7)
    target_x = (target >> 8) * 4 + ((target & 31) >> 3)
    target_y = ((target >> 5) & 7) * 8 + (target & 7)
    offset_x = (target_x - source_x + 1) & 63
    offset_y = (target_y - source_y + 1) & 63
    code = (offset_x * 3 + offset_y).astype(F32)

    def twice(values):
        return jnp.concatenate([values, values], axis=1)

    pair = twice(pair_v[...])
    order = jnp.where(lax.broadcasted_iota(jnp.int32, (32, 128), 1) < 64, pair, pltpu.roll(pair, 32, 1))
    radius_p = jnp.take_along_axis(twice(rad_v[...]), order, axis=1)
    live_p = jnp.take_along_axis(twice(live), order, axis=1)
    code_p = jnp.take_along_axis(twice(code), order, axis=1)

    for x in (0, SX - 1):
        row_y0[pl.ds(x, 1), :] = fp[1, x + 1, 0:1, :]
    for copy in wind:
        copy.wait_recv()
    for copy in air:
        copy.start()
    advect_plane(0, (0, 1, 2))
    advect_plane(SX - 1, (0, 1, 2))

    speed = fp[0, 0]
    c_east, c_west = coefficients(speed)
    c_north, c_south = coefficients(fp[1, 0])
    c_up, c_down, c_mid = vertical(fp[2, 0], lane)
    above = jnp.where(row == SY - 1, corner[1, 0:1, :], pltpu.roll(speed, SY - 1, 0))
    beneath = jnp.where(row == 0, corner[0, 0:1, :], pltpu.roll(speed, 1, 0))
    ad[0, 0] = (
        (c_mid * speed + c_east * fp[0, 1] + c_west * xu2[...])
        + (c_north * above + c_south * beneath)
        + (c_up * upward(speed) + c_down * downward(speed))
    )
    speed = yl[1]
    row_x = lax.broadcasted_iota(jnp.int32, (SX, NZ), 0)
    lane_x = lax.broadcasted_iota(jnp.int32, (SX, NZ), 1)
    c_east, c_west = coefficients(yl[0])
    c_north, c_south = coefficients(speed)
    c_up, c_down, c_mid = vertical(yl[2], lane_x)
    after = jnp.where(row_x == SX - 1, corner[3, 0:1, :], pltpu.roll(speed, SX - 1, 0))
    before = jnp.where(row_x == 0, corner[2, 0:1, :], pltpu.roll(speed, 1, 0))
    below_y[...] = (
        (c_mid * speed + c_east * after + c_west * before)
        + (c_north * row_y0[...] + c_south * yl[5])
        + (c_up * upward(speed) + c_down * downward(speed))
    )
    fetches[0].wait()

    def border(x, fields):
        _, c_south = coefficients(fp[1, x + 1, 0:8, :])
        c_north, _ = coefficients(fp[1, x + 1, SY - 8 : SY, :])
        c_south = jnp.where(tile_row == 0, c_south, 0.0)
        c_north = jnp.where(tile_row == 7, c_north, 0.0)
        for f in fields:
            ad[f, x + 1, 0:8, :] += c_south * yl[f, pl.ds(x, 1), :]
            ad[f, x + 1, SY - 8 : SY, :] += c_north * yh[f, pl.ds(x, 1), :]

    def block(c, carry):
        parts = []
        for i in range(4):
            x = c * 4 + i
            border(x, (0, 1, 2))
            star_w = ad[2, x + 1] + 0.1 * fp[3, x + 1]
            ad[2, x + 1] = star_w
            star_v = ad[1, x + 1]
            behind_v = jnp.where(row == 0, below_y[pl.ds(x, 1), :], pltpu.roll(star_v, 1, 0))
            below_w = jnp.where(lane == 0, 0.0, downward(star_w))
            parts.append((ad[0, x + 1] - ad[0, x]) + (star_v - behind_v) + (star_w - below_w))
        chunk = jnp.concatenate(parts, axis=0)
        send1[c] = product((cosine[0], cosine[1]), halves(chunk), NT)
        return carry

    def scalars(c, carry):
        total = jnp.zeros((SY, NZ), F32)
        for i in range(4):
            x = c * 4 + i
            advect_plane(x, (3, 4))
            border(x, (3, 4))
            total = total + ad[4, x + 1]
        quad[c] = total
        return carry

    lax.fori_loop(0, 4, block, 0)
    pl.semaphore_wait(known.at[0], len(corners))

    def scatter(source, target_ref, send_sem, recv_sem):
        def one(px, ry):
            py = peers_y[ry]
            pltpu.make_async_remote_copy(
                src_ref=source.at[:, pl.ds(px * GY + py, 1), :],
                dst_ref=target_ref.at[:, pl.ds(me, 1), :],
                send_sem=send_sem, recv_sem=recv_sem, device_id=(px, py), device_id_type=MESH,
            ).start()

        for rx, ry in send_order():
            one(peers_x[rx], ry)

    def drained(source, target_ref, sem):
        count = pl.ds(0, DEV - 1)
        pltpu.make_async_copy(source.at[:, count, :], target_ref.at[:, count, :], sem).wait()

    scatter(send1, got1, s1_sem, r1_sem)
    got1[:, pl.ds(me, 1), :] = send1[:, pl.ds(me, 1), :]

    outs = [
        pltpu.make_async_copy(ad.at[pl.ds(0, 3), pl.ds(1, SX)], star, out_sem.at[0]),
        pltpu.make_async_copy(ad.at[3, pl.ds(1, SX)], theta_out, out_sem.at[1]),
        pltpu.make_async_copy(ad.at[4, pl.ds(1, SX)], vapour_out, out_sem.at[2]),
    ]
    outs[0].start()
    for copy in air:
        copy.wait_recv()
    lax.fori_loop(0, 4, scalars, 0)
    outs[1].start()
    fetches[1].wait()
    high, low = halves(quad[...].reshape(128, NZ))
    sums = lax.dot_general(box[...], high, (NN, ((), ())), preferred_element_type=F32)
    sums = sums + lax.dot_general(box[...], low, (NN, ((), ())), preferred_element_type=F32)
    mean = jnp.sum(sums, axis=1, keepdims=True) * (1.0 / (16 * NZ))
    soft = jnp.maximum(mean, 0.0) + jnp.log1p(jnp.exp(-jnp.abs(mean)))
    grown = radius_p + 0.5 * soft
    root = jnp.sqrt(grown)
    mass = grown * root
    gain = mass - radius_p * jnp.sqrt(radius_p)

    def other(values):
        return pltpu.roll(values, 64, 1)

    root_sum = root + other(root)
    rate = 0.05 * (root_sum * root_sum * jnp.abs(grown - other(grown)) * other(live_p))
    final = (mass + rate * other(mass)) / (1.0 + rate)
    lanes = lax.broadcasted_iota(jnp.int32, (32, 128), 1)
    own_live = jnp.where(lanes < 64, live_p, 0.0)
    cond[...] = jnp.broadcast_to(jnp.sum(own_live * gain, axis=1, keepdims=True), (32, 128)) * 0.002
    carried = [own_live, own_live * final, own_live * final * final]
    packed = jnp.zeros((32, 128), F32)
    for d in range(9):
        chosen = code_p == float(d)
        for k in range(3):
            amount = jnp.sum(jnp.where(chosen, carried[k], 0.0), axis=1, keepdims=True)
            packed = packed + jnp.where(lanes == d * 3 + k, amount, 0.0)
    load[...] = packed

    def share(source, target_ref, k, device):
        return pltpu.make_async_remote_copy(
            src_ref=source, dst_ref=target_ref, send_sem=ms_sem.at[k], recv_sem=mr_sem.at[k],
            device_id=device, device_id_type=MESH,
        )

    top, bottom = pl.ds(24, 8), pl.ds(0, 8)
    shares = [
        share(load.at[top], near.at[0, bottom], 0, (east, gy)),
        share(load.at[bottom], near.at[1, bottom], 1, (west, gy)),
        share(load, near.at[2], 2, (gx, north)),
        share(load, near.at[3], 3, (gx, south)),
        share(load.at[top], near.at[4, bottom], 4, (east, north)),
        share(load.at[top], near.at[5, bottom], 5, (east, south)),
        share(load.at[bottom], near.at[6, bottom], 6, (west, north)),
        share(load.at[bottom], near.at[7, bottom], 7, (west, south)),
    ]
    for copy in shares:
        copy.start()

    def dry(x, carry):
        first_box = (x // 4) * 8
        for t in range(4):
            drop = jnp.where(
                tile_row < 4,
                cond[pl.ds(first_box + 2 * t, 1), :],
                cond[pl.ds(first_box + 2 * t + 1, 1), :],
            )
            ad[4, x + 1, 8 * t : 8 * t + 8, :] -= drop
        return carry

    lax.fori_loop(0, SX, dry, 0)
    outs[2].start()

    for copy in fetches[2:]:
        copy.wait()
    drained(send1, got1, r1_sem)
    z_re, z_im = [], []
    for c in range(4):
        both = product((first[0, c], first[1, c]), halves(got1[c]), NN)
        z_re.append(both[:HALF])
        z_im.append(both[HALF:])

    def butterfly(re, im, sign):
        s02r, s02i = re[0] + re[2], im[0] + im[2]
        d02r, d02i = re[0] - re[2], im[0] - im[2]
        s13r, s13i = re[1] + re[3], im[1] + im[3]
        d13r, d13i = re[1] - re[3], im[1] - im[3]
        if sign < 0:
            return (
                [s02r + s13r, d02r + d13i, s02r - s13r, d02r - d13i],
                [s02i + s13i, d02i - d13r, s02i - s13i, d02i + d13r],
            )
        return (
            [s02r + s13r, d02r - d13i, s02r - s13r, d02r + d13i],
            [s02i + s13i, d02i + d13r, s02i - s13i, d02i - d13r],
        )

    q_re, q_im = butterfly(z_re, z_im, -1)
    re, im = jnp.concatenate(q_re, axis=0), jnp.concatenate(q_im, axis=0)
    turn_cos, turn_sin = turns[0], turns[1]
    joined = jnp.concatenate([re * turn_cos + im * turn_sin, im * turn_cos - re * turn_sin], axis=1)
    spectrum = product(halves(joined), (ahead[0], ahead[1]), NN)
    eigen = turns[2] + wave[pl.ds(me, 1), :]
    inverse = jnp.where(eigen == 0.0, 0.0, 1.0 / jnp.where(eigen == 0.0, 1.0, eigen))
    solved = spectrum * jnp.concatenate([inverse, inverse], axis=1)
    turned = product(halves(solved), (behind[0], behind[1]), NN)
    re, im = turned[:, :128], turned[:, 128:]
    back_re, back_im = re * turn_cos - im * turn_sin, im * turn_cos + re * turn_sin
    v_re, v_im = butterfly(
        [back_re[HALF * q : HALF * (q + 1)] for q in range(4)],
        [back_im[HALF * q : HALF * (q + 1)] for q in range(4)],
        1,
    )
    wide_lane = lax.broadcasted_iota(jnp.int32, (128, 128), 1)
    edge = None
    for c in range(4):
        stacked = jnp.concatenate([v_re[c], v_im[c]], axis=0)
        plane = product((last[0, c], last[1, c]), halves(stacked), NN)
        send2[c] = plane
        if c == 0:
            next_x = pltpu.roll(plane, 120, 0)
        picked = jnp.where((wide_lane & 31) == 0, plane, 0.0)
        picked = picked if c == 0 else pltpu.roll(picked, c, 1)
        edge = picked if edge is None else edge + picked
    row_b = lax.broadcasted_iota(jnp.int32, (128, 128), 0) & 7
    edge = jnp.where(row_b == 7, pltpu.roll(edge, 7, 0), pltpu.roll(edge, 127, 0))
    moved = pltpu.roll(edge, 36, 1)
    in_move = (wide_lane >= 36) & (wide_lane < 40)
    send2[4] = jnp.where(wide_lane < 32, next_x, jnp.where(in_move, moved, edge))

    scatter(send2, modes, s2_sem, r2_sem)
    own = pltpu.make_async_copy(
        send2.at[:, pl.ds(me, 1), :], modes.at[:, pl.ds(me, 1), :], own_sem
    )
    own.start()

    for copy in shares:
        copy.wait_recv()
    tile_lane = lax.broadcasted_iota(jnp.int32, (8, 128), 1)

    def column_of(x):
        if x < 0:
            return near[0, 0:8, :], near[4, 7:8, :], near[5, 0:1, :]
        if x > 3:
            return near[1, 0:8, :], near[6, 7:8, :], near[7, 0:1, :]
        return load[8 * x : 8 * x + 8, :], near[2, 8 * x + 7 : 8 * x + 8, :], near[3, 8 * x : 8 * x + 1, :]

    arrived = [jnp.zeros((8, 128), F32) for _ in range(4)]
    for x in range(-1, 5):
        centre, low_row, high_row = column_of(x)
        shifted = [
            jnp.where(tile_row == 7, high_row, pltpu.roll(centre, 7, 0)),
            centre,
            jnp.where(tile_row == 0, low_row, pltpu.roll(centre, 1, 0)),
        ]
        for dx in (-1, 0, 1):
            if not 0 <= x + dx < 4:
                continue
            for dy in (-1, 0, 1):
                d = (dx + 1) * 3 + dy + 1
                values = shifted[dy + 1]
                values = values if d == 0 else pltpu.roll(values, 128 - 3 * d, 1)
                arrived[x + dx] = arrived[x + dx] + values
    stacked = jnp.concatenate(arrived + [jnp.zeros((96, 128), F32)], axis=0) * (1.0 / 64)
    res[...] = stacked.T[0:8, :]
    outs.append(pltpu.make_async_copy(res, moments_out, out_sem.at[3]))
    outs[3].start()

    for copy in halo:
        copy.wait_send()
    for copy in shares:
        copy.wait_send()
    drained(send1, got1, s1_sem)
    for copy in outs:
        copy.wait()
    own.wait()
    drained(send2, send2, s2_sem)
    drained(send2, modes, r2_sem)


def final_kernel(
    modes, star, theta, vapour, moments, back_h,
    vel_out, theta_out, vapour_out, moments_out,
    mode_v, star_v, theta_v, vapour_v, mom_v, mom_o, back, pressure, in_sem, out_sem,
):
    loads = [
        pltpu.make_async_copy(source, target, in_sem.at[k])
        for k, (source, target) in enumerate(
            [(modes, mode_v), (back_h, back), (star, star_v), (theta, theta_v), (vapour, vapour_v), (moments, mom_v)]
        )
    ]
    for copy in loads:
        copy.start()
    loads[0].wait()
    loads[1].wait()
    for c in range(5):
        pressure[pl.ds(128 * c, 128), :] = product(halves(mode_v[c]), (back[0], back[1]), TN)
    for copy in loads[2:]:
        copy.wait()
    mom_o[...] = mom_v[0:3, 0:32]
    outs = [
        pltpu.make_async_copy(theta_v, theta_out, out_sem.at[0]),
        pltpu.make_async_copy(vapour_v, vapour_out, out_sem.at[1]),
        pltpu.make_async_copy(mom_o, moments_out, out_sem.at[2]),
    ]
    for copy in outs:
        copy.start()
    row = lax.broadcasted_iota(jnp.int32, (SY, NZ), 0)
    lane = lax.broadcasted_iota(jnp.int32, (SY, NZ), 1)
    for x in range(SX):
        c, i = x // 4, x % 4
        here = pressure[pl.ds(32 * x, 32), :]
        ahead = pressure[pl.ds(32 * x + 32, 32), :]
        line = 512 + (36, 32, 64, 96)[i] + c
        side = jnp.where(row == SY - 1, pressure[line : line + 1, :], pltpu.roll(here, SY - 1, 0))
        above = jnp.where(lane == NZ - 1, here, pltpu.roll(here, NZ - 1, 1))
        star_v[0, x] = star_v[0, x] - (ahead - here)
        star_v[1, x] = star_v[1, x] - (side - here)
        star_v[2, x] = star_v[2, x] - (above - here)
    last = pltpu.make_async_copy(star_v, vel_out, out_sem.at[3])
    last.start()
    for copy in outs:
        copy.wait()
    last.wait()


def shards(velocity, theta, vapour, radius_sq, multiplicity, counts, pairing, destination):
    t = tables()
    names = ["cosine", "first", "ahead", "behind", "last", "turns", "wave_z", "box"]
    held = [jnp.asarray(t[name]) for name in names]
    block = (SX, SY, NZ)
    shape = jax.ShapeDtypeStruct
    vmem = pltpu.VMEM
    dma = pltpu.SemaphoreType.DMA
    modes, star, theta_new, vapour_new, moments = pl.pallas_call(
        step_kernel,
        out_shape=(
            shape((5, DEV, 128), F32),
            shape((3,) + block, F32),
            shape(block, F32),
            shape(block, F32),
            shape((8, 128), F32),
        ),
        in_specs=[ANY] * 16,
        out_specs=(ANY,) * 5,
        scratch_shapes=[
            vmem((5, SX + 2, SY, NZ), F32),
            vmem((5, SX + 1, SY, NZ), F32),
            vmem((SY, NZ), F32),
            vmem((6, SX, NZ), F32),
            vmem((5, SX, NZ), F32),
            vmem((4, 8, NZ), F32),
            vmem((SX, NZ), F32),
            vmem((SX, NZ), F32),
            vmem((4, SY, NZ), F32),
            vmem((4, DEV, 128), F32),
            vmem((4, DEV, 128), F32),
            vmem((5, DEV, 128), F32),
        ]
        + [vmem(t[name].shape, t[name].dtype) for name in names]
        + [
            vmem((32, 64), F32),
            vmem((32, 64), F32),
            vmem((32,), jnp.int32),
            vmem((32, 64), jnp.int32),
            vmem((32, 64), jnp.int32),
            vmem((32, 128), F32),
            vmem((32, 128), F32),
            vmem((8, 32, 128), F32),
            vmem((8, 128), F32),
            pltpu.SemaphoreType.REGULAR((1,)),
            dma((3,)),
            dma((5,)),
            dma((8,)),
            dma((18,)),
            dma((18,)),
            dma(()),
            dma(()),
            dma(()),
            dma(()),
            dma(()),
            dma((8,)),
            dma((8,)),
            dma((4,)),
        ],
        compiler_params=pltpu.CompilerParams(has_side_effects=True, collective_id=1),
        name="cloud_step",
    )(velocity, theta, vapour, radius_sq.T, multiplicity.T, counts, pairing, destination.T, *held)
    return pl.pallas_call(
        final_kernel,
        out_shape=(
            shape((3,) + block, F32),
            shape(block, F32),
            shape(block, F32),
            shape((3, 32), F32),
        ),
        in_specs=[ANY] * 6,
        out_specs=(ANY,) * 4,
        scratch_shapes=[
            vmem((5, DEV, 128), F32),
            vmem((3,) + block, F32),
            vmem(block, F32),
            vmem(block, F32),
            vmem((8, 128), F32),
            vmem((3, 32), F32),
            vmem((2, NZ, NZ), BF16),
            vmem((640, 128), F32),
            dma((6,)),
            dma((4,)),
        ],
        name="project",
    )(modes, star, theta_new, vapour_new, moments, jnp.asarray(t["back"]))


def solution(mesh):
    placed = (
        P(None, "gx", "gy", None),
        P("gx", "gy", None),
        P("gx", "gy", None),
        P(None, ("gx", "gy")),
        P(None, ("gx", "gy")),
        P(("gx", "gy")),
        P(("gx", "gy"), None),
        P(None, ("gx", "gy")),
    )
    return jax.shard_map(
        shards,
        mesh=mesh,
        in_specs=placed,
        out_specs=(
            P(None, "gx", "gy", None),
            P("gx", "gy", None),
            P("gx", "gy", None),
            P(None, ("gx", "gy")),
        ),
        check_vma=False,
    )
```

```python
import functools
import math

import jax
import jax.numpy as jnp
import numpy as np
from jax import lax
from jax.experimental import pallas as pl
from jax.experimental.pallas import tpu as pltpu
from jax.sharding import PartitionSpec as P

MESH = pl.DeviceIdType.MESH
GX, GY = 16, 8
DEV = GX * GY
SX, SY, NZ = 16, 32, 128
NX, NY = 256, 256
HALF = 72
F32 = jnp.float32
BF16 = jnp.bfloat16
ANY = pl.BlockSpec(memory_space=pl.ANY)


def split_table(table):
    table = np.asarray(table, np.float32)
    high = table.astype(jnp.bfloat16)
    low = (table - high.astype(np.float32)).astype(jnp.bfloat16)
    return np.stack([high, low])


@functools.cache
def send_order():
    hops = (0, 1, 2, 1)
    peers = [(rx, ry) for rx in range(GX) for ry in range(GY) if rx or ry]
    peers.sort(key=lambda p: -(hops[p[0] // 4] + hops[p[0] % 4] + hops[p[1] // 2]))
    classes = {}
    for p in peers:
        classes.setdefault((p[0] // 4 > 2, p[0] % 4 > 2, p[1] // 2 > 2, p[1] % 2), []).append(p)
    queues = list(classes.values())
    order = []
    while any(queues):
        for queue in queues:
            if queue:
                order.append(queue.pop(0))
    return tuple(order)


@functools.cache
def tables():
    tau = 2.0 * math.pi
    z = np.arange(NZ)
    cosine = np.cos(math.pi * (z[None, :] + 0.5) * z[:, None] / NZ)
    weight = np.where(z == 0, 1.0 / NZ, 2.0 / NZ)
    back = cosine * weight[:, None]
    rows, factor, seen = [], [], set()
    for p in range(16):
        for q in range(8):
            if (p, q) in seen:
                continue
            mirror = (-p % 16, -q % 8)
            seen.update({(p, q), mirror})
            rows.append((p, q))
            factor.append(1.0 if mirror == (p, q) else 2.0)
    pad = HALF - len(rows)
    low_x = np.array([r[0] for r in rows] + [0] * pad)
    low_y = np.array([r[1] for r in rows] + [0] * pad)
    factor = np.array(factor + [0.0] * pad)
    used = np.array([1.0] * len(rows) + [0.0] * pad)
    a = np.repeat(np.arange(16), 8)
    b = np.tile(np.arange(8), 16)
    first, last = [], []
    for c in range(4):
        angle = tau * (
            low_x[:, None] * a[None] / 16.0
            + low_y[:, None] * b[None] / 8.0
            + low_x[:, None] * c / 64.0
        )
        first.append(np.concatenate([np.cos(angle) * used[:, None], -np.sin(angle) * used[:, None]]))
        scale = factor[:, None] / (NX * NY)
        last.append(np.concatenate([np.cos(angle) * scale, -np.sin(angle) * scale]).T)
    lane_i = np.repeat(np.arange(4), 32)
    lane_j = np.tile(np.arange(32), 4)
    turn_cos, turn_sin, wave = [], [], []
    for q in range(4):
        kx0 = low_x + 16 * q
        angle = tau * (kx0[:, None] * lane_i[None] + low_y[:, None] * lane_j[None]) / 256.0
        turn_cos.append(np.cos(angle))
        turn_sin.append(np.sin(angle))
        kx = kx0[:, None] + 64 * lane_i[None]
        ky = low_y[:, None] + 8 * lane_j[None]
        wave.append(-4.0 * np.sin(math.pi * kx / NX) ** 2 - 4.0 * np.sin(math.pi * ky / NY) ** 2)
    turns = np.stack([np.concatenate(turn_cos), np.concatenate(turn_sin), np.concatenate(wave)])
    angle = tau * (lane_i[:, None] * lane_i[None] / 4.0 + lane_j[:, None] * lane_j[None] / 32.0)
    cos2, sin2 = np.cos(angle), np.sin(angle)
    ahead = np.block([[cos2, -sin2], [sin2, cos2]])
    behind = np.block([[cos2, sin2], [-sin2, cos2]])
    wave_z = -4.0 * np.sin(math.pi * z / (2.0 * NZ)) ** 2
    wave_z = np.broadcast_to(wave_z[:, None], (NZ, 128)).astype(np.float32)
    box = np.zeros((32, 128), np.float32)
    for column in range(4):
        for j in range(32):
            box[column * 8 + j // 4, column * 32 + j] = 1.0
    return dict(
        cosine=split_table(cosine),
        first=split_table(np.stack(first)),
        ahead=split_table(ahead),
        behind=split_table(behind),
        last=split_table(np.stack(last)),
        turns=turns.astype(np.float32),
        wave_z=wave_z,
        box=box.astype(jnp.bfloat16),
        back=split_table(back),
    )


def halves(values):
    high = values.astype(BF16)
    return high, (values - high.astype(F32)).astype(BF16)


def product(left, right, dims):
    def one(x, y):
        return lax.dot_general(x, y, (dims, ((), ())), preferred_element_type=F32)

    (left_high, left_low), (right_high, right_low) = left, right
    return one(left_high, right_high) + (one(left_high, right_low) + one(left_low, right_high))


NN = ((1,), (0,))
NT = ((1,), (1,))
TN = ((0,), (0,))


def step_kernel(
    vel, theta, vapour, radius, multi, counts, pairing, dest,
    cosine_h, first_h, ahead_h, behind_h, last_h, turns_h, wave_h, box_h,
    modes, ad, moments_out,
    fp, before_u, xu2, yl, yh, corner, row_y0, below_y, quad, send1, got1, send2,
    cosine, first, ahead, behind, last, turns, wave, box,
    rad_v, mul_v, cnt_v, pair_v, dst_v, cond, load, near,
    known, load_sem, drop_sem, table_sem, hs_sem, hr_sem, s1_sem, r1_sem, s2_sem, r2_sem,
    ms_sem, mr_sem,
):
    gx = lax.axis_index("gx")
    gy = lax.axis_index("gy")
    me = gx * GY + gy
    east, west = lax.rem(gx + 1, GX), lax.rem(gx + GX - 1, GX)
    north, south = lax.rem(gy + 1, GY), lax.rem(gy + GY - 1, GY)
    peers_x = [lax.rem(gx + r, GX) for r in range(GX)]
    peers_y = [lax.rem(gy + r, GY) for r in range(GY)]

    loads = [
        pltpu.make_async_copy(vel, fp.at[pl.ds(0, 3), pl.ds(1, SX)], load_sem.at[0]),
        pltpu.make_async_copy(theta, fp.at[3, pl.ds(1, SX)], load_sem.at[1]),
        pltpu.make_async_copy(vapour, fp.at[4, pl.ds(1, SX)], load_sem.at[2]),
    ]
    drops = [
        pltpu.make_async_copy(source, target, drop_sem.at[k])
        for k, (source, target) in enumerate(
            [(radius, rad_v), (multi, mul_v), (counts, cnt_v), (pairing, pair_v), (dest, dst_v)]
        )
    ]
    table_pairs = [
        (cosine_h, cosine), (box_h, box), (first_h, first), (turns_h, turns), (ahead_h, ahead),
        (wave_h, wave), (behind_h, behind), (last_h, last),
    ]
    fetches = [
        pltpu.make_async_copy(source, target, table_sem.at[k])
        for k, (source, target) in enumerate(table_pairs)
    ]
    for copy in loads + drops + fetches:
        copy.start()

    barrier = pltpu.get_barrier_semaphore()

    chip_z, chip_x, chip_y, core = gx // 4, lax.rem(gx, 4), gy // 2, lax.rem(gy, 2)

    def away(step_z, step_x, step_y, step_core):
        to_z, to_x, to_y = (
            lax.rem(at + 4 + step, 4)
            for at, step in ((chip_z, step_z), (chip_x, step_x), (chip_y, step_y))
        )
        return to_z * 4 + to_x, to_y * 2 + lax.rem(core + step_core, 2)

    steps = [(k, i, j, n) for k in (0, 1, -1) for i in (1, -1, 0) for j in (1, -1, 0) for n in (0, 1)]
    around = [away(*step) for step in steps if any(step)]
    corners = [away(k, i, j, 0) for k in (1, -1) for i in (1, -1) for j in (1, -1)]
    for device in around:
        pl.semaphore_signal(barrier, inc=1, device_id=device, device_id_type=MESH)
    pl.semaphore_wait(barrier, len(around))

    def remote(source, target_ref, k, device):
        return pltpu.make_async_remote_copy(
            src_ref=source, dst_ref=target_ref, send_sem=hs_sem.at[k], recv_sem=hr_sem.at[k],
            device_id=device, device_id_type=MESH,
        )

    wind = [
        remote(vel.at[:, SX - 1], fp.at[pl.ds(0, 3), 0], 0, (east, gy)),
        remote(vel.at[:, 0], fp.at[pl.ds(0, 3), SX + 1], 1, (west, gy)),
        remote(vel.at[0, SX - 2], xu2, 2, (east, gy)),
        remote(vel.at[:, :, SY - 1], yl.at[pl.ds(0, 3)], 3, (gx, north)),
        remote(vel.at[:, :, 0], yh.at[pl.ds(0, 3)], 4, (gx, south)),
        remote(vel.at[1, :, SY - 2], yl.at[5], 5, (gx, north)),
        remote(vel.at[0, SX - 1, pl.ds(SY - 1, 1)], corner.at[0, pl.ds(0, 1)], 6, (east, north)),
        remote(vel.at[0, SX - 1, pl.ds(0, 1)], corner.at[1, pl.ds(0, 1)], 7, (east, south)),
        remote(vel.at[1, SX - 1, pl.ds(SY - 1, 1)], corner.at[2, pl.ds(0, 1)], 8, (east, north)),
        remote(vel.at[1, 0, pl.ds(SY - 1, 1)], corner.at[3, pl.ds(0, 1)], 9, (west, north)),
    ]
    air = [
        remote(theta.at[SX - 1], fp.at[3, 0], 10, (east, gy)),
        remote(vapour.at[SX - 1], fp.at[4, 0], 11, (east, gy)),
        remote(theta.at[0], fp.at[3, SX + 1], 12, (west, gy)),
        remote(vapour.at[0], fp.at[4, SX + 1], 13, (west, gy)),
        remote(theta.at[:, SY - 1], yl.at[3], 14, (gx, north)),
        remote(vapour.at[:, SY - 1], yl.at[4], 15, (gx, north)),
        remote(theta.at[:, 0], yh.at[3], 16, (gx, south)),
        remote(vapour.at[:, 0], yh.at[4], 17, (gx, south)),
    ]
    halo = wind + air
    for copy in wind[6:] + wind[:6]:
        copy.start()

    def pass_on(k, devices):
        for device in devices:
            pl.semaphore_signal(known.at[k], inc=1, device_id=device, device_id_type=MESH)

    pass_on(0, corners)
    for copy in loads:
        copy.wait()

    row = lax.broadcasted_iota(jnp.int32, (SY, NZ), 0)
    lane = lax.broadcasted_iota(jnp.int32, (SY, NZ), 1)
    tile_row = lax.broadcasted_iota(jnp.int32, (8, NZ), 0)

    def upward(values):
        return pltpu.roll(values, NZ - 1, 1)

    def downward(values):
        return pltpu.roll(values, 1, 1)

    def coefficients(speed, shape_lane=None):
        scaled = 0.1 * speed
        return 0.01 - scaled, 0.01 + scaled

    def vertical(speed, lanes):
        up, down = coefficients(speed)
        top, bottom = lanes == NZ - 1, lanes == 0
        centre = 0.94 + jnp.where(top, up, 0.0) + jnp.where(bottom, down, 0.0)
        return jnp.where(top, 0.0, up), jnp.where(bottom, 0.0, down), centre

    def advect_plane(x, fields):
        c_east, c_west = coefficients(fp[0, x + 1])
        c_north, c_south = coefficients(fp[1, x + 1])
        c_north = jnp.where(row == SY - 1, 0.0, c_north)
        c_south = jnp.where(row == 0, 0.0, c_south)
        c_up, c_down, c_mid = vertical(fp[2, x + 1], lane)
        for f in fields:
            centre = fp[f, x + 1]
            ad[f, x] = (
                (c_mid * centre + c_east * fp[f, x + 2] + c_west * fp[f, x])
                + (c_north * pltpu.roll(centre, SY - 1, 0) + c_south * pltpu.roll(centre, 1, 0))
                + (c_up * upward(centre) + c_down * downward(centre))
            )

    def inner(x, carry):
        advect_plane(x, (0, 1, 2))
        row_y0[pl.ds(x, 1), :] = fp[1, x + 1, 0:1, :]
        return carry

    lax.fori_loop(1, SX - 1, inner, 0)
    for copy in drops:
        copy.wait()
    box_row = lax.broadcasted_iota(jnp.int32, (32, 32), 0)
    box_lane = lax.broadcasted_iota(jnp.int32, (32, 32), 1)
    spread = jnp.where(box_row == box_lane, cnt_v[...][None, :].astype(F32), 0.0)
    used = jnp.sum(spread, axis=1, keepdims=True)
    slot = lax.broadcasted_iota(jnp.int32, (32, 64), 1).astype(F32)
    live = jnp.where(slot < used, mul_v[...], 0.0)
    target = dst_v[...]
    local_box = lax.broadcasted_iota(jnp.int32, (32, 64), 0)
    source_x = gx * 4 + (local_box >> 3)
    source_y = gy * 8 + (local_box & 7)
    target_x = (target >> 8) * 4 + ((target & 31) >> 3)
    target_y = ((target >> 5) & 7) * 8 + (target & 7)
    offset_x = (target_x - source_x + 1) & 63
    offset_y = (target_y - source_y + 1) & 63
    code = (offset_x * 3 + offset_y).astype(F32)

    def twice(values):
        return jnp.concatenate([values, values], axis=1)

    pair = twice(pair_v[...])
    order = jnp.where(lax.broadcasted_iota(jnp.int32, (32, 128), 1) < 64, pair, pltpu.roll(pair, 32, 1))
    radius_p = jnp.take_along_axis(twice(rad_v[...]), order, axis=1)
    live_p = jnp.take_along_axis(twice(live), order, axis=1)
    code_p = jnp.take_along_axis(twice(code), order, axis=1)

    for x in (0, SX - 1):
        row_y0[pl.ds(x, 1), :] = fp[1, x + 1, 0:1, :]
    for copy in wind:
        copy.wait_recv()
    for copy in air:
        copy.start()
    advect_plane(0, (0, 1, 2))
    advect_plane(SX - 1, (0, 1, 2))

    speed = fp[0, 0]
    c_east, c_west = coefficients(speed)
    c_north, c_south = coefficients(fp[1, 0])
    c_up, c_down, c_mid = vertical(fp[2, 0], lane)
    above = jnp.where(row == SY - 1, corner[1, 0:1, :], pltpu.roll(speed, SY - 1, 0))
    beneath = jnp.where(row == 0, corner[0, 0:1, :], pltpu.roll(speed, 1, 0))
    before_u[...] = (
        (c_mid * speed + c_east * fp[0, 1] + c_west * xu2[...])
        + (c_north * above + c_south * beneath)
        + (c_up * upward(speed) + c_down * downward(speed))
    )
    speed = yl[1]
    row_x = lax.broadcasted_iota(jnp.int32, (SX, NZ), 0)
    lane_x = lax.broadcasted_iota(jnp.int32, (SX, NZ), 1)
    c_east, c_west = coefficients(yl[0])
    c_north, c_south = coefficients(speed)
    c_up, c_down, c_mid = vertical(yl[2], lane_x)
    after = jnp.where(row_x == SX - 1, corner[3, 0:1, :], pltpu.roll(speed, SX - 1, 0))
    before = jnp.where(row_x == 0, corner[2, 0:1, :], pltpu.roll(speed, 1, 0))
    below_y[...] = (
        (c_mid * speed + c_east * after + c_west * before)
        + (c_north * row_y0[...] + c_south * yl[5])
        + (c_up * upward(speed) + c_down * downward(speed))
    )
    fetches[0].wait()

    def border(x, fields):
        _, c_south = coefficients(fp[1, x + 1, 0:8, :])
        c_north, _ = coefficients(fp[1, x + 1, SY - 8 : SY, :])
        c_south = jnp.where(tile_row == 0, c_south, 0.0)
        c_north = jnp.where(tile_row == 7, c_north, 0.0)
        for f in fields:
            ad[f, x, 0:8, :] += c_south * yl[f, pl.ds(x, 1), :]
            ad[f, x, SY - 8 : SY, :] += c_north * yh[f, pl.ds(x, 1), :]

    def block(c, carry):
        parts = []
        for i in range(4):
            x = c * 4 + i
            border(x, (0, 1, 2))
            star_w = ad[2, x] + 0.1 * fp[3, x + 1]
            ad[2, x] = star_w
            star_v = ad[1, x]
            star_u = ad[0, x]
            if i == 0:
                last_u = jnp.where(c == 0, before_u[...], ad[0, jnp.maximum(x - 1, 0)])
            behind_v = jnp.where(row == 0, below_y[pl.ds(x, 1), :], pltpu.roll(star_v, 1, 0))
            below_w = jnp.where(lane == 0, 0.0, downward(star_w))
            parts.append((star_u - last_u) + (star_v - behind_v) + (star_w - below_w))
            last_u = star_u
        chunk = jnp.concatenate(parts, axis=0)
        send1[c] = product((cosine[0], cosine[1]), halves(chunk), NT)
        return carry

    def scalars(c, carry):
        total = jnp.zeros((SY, NZ), F32)
        for i in range(4):
            x = c * 4 + i
            advect_plane(x, (3, 4))
            border(x, (3, 4))
            total = total + ad[4, x]
        quad[c] = total
        return carry

    lax.fori_loop(0, 4, block, 0)
    pl.semaphore_wait(known.at[0], len(corners))

    def scatter(source, target_ref, send_sem, recv_sem):
        def one(px, ry):
            py = peers_y[ry]
            pltpu.make_async_remote_copy(
                src_ref=source.at[:, pl.ds(px * GY + py, 1), :],
                dst_ref=target_ref.at[:, pl.ds(me, 1), :],
                send_sem=send_sem, recv_sem=recv_sem, device_id=(px, py), device_id_type=MESH,
            ).start()

        for rx, ry in send_order():
            one(peers_x[rx], ry)

    def drained(source, target_ref, sem):
        count = pl.ds(0, DEV - 1)
        pltpu.make_async_copy(source.at[:, count, :], target_ref.at[:, count, :], sem).wait()

    scatter(send1, got1, s1_sem, r1_sem)
    got1[:, pl.ds(me, 1), :] = send1[:, pl.ds(me, 1), :]

    for copy in air:
        copy.wait_recv()
    lax.fori_loop(0, 4, scalars, 0)
    fetches[1].wait()
    high, low = halves(quad[...].reshape(128, NZ))
    sums = lax.dot_general(box[...], high, (NN, ((), ())), preferred_element_type=F32)
    sums = sums + lax.dot_general(box[...], low, (NN, ((), ())), preferred_element_type=F32)
    mean = jnp.sum(sums, axis=1, keepdims=True) * (1.0 / (16 * NZ))
    soft = jnp.maximum(mean, 0.0) + jnp.log1p(jnp.exp(-jnp.abs(mean)))
    grown = radius_p + 0.5 * soft
    root = jnp.sqrt(grown)
    mass = grown * root
    gain = mass - radius_p * jnp.sqrt(radius_p)

    def other(values):
        return pltpu.roll(values, 64, 1)

    root_sum = root + other(root)
    rate = 0.05 * (root_sum * root_sum * jnp.abs(grown - other(grown)) * other(live_p))
    final = (mass + rate * other(mass)) / (1.0 + rate)
    lanes = lax.broadcasted_iota(jnp.int32, (32, 128), 1)
    own_live = jnp.where(lanes < 64, live_p, 0.0)
    cond[...] = jnp.broadcast_to(jnp.sum(own_live * gain, axis=1, keepdims=True), (32, 128)) * 0.002
    carried = [own_live, own_live * final, own_live * final * final]
    packed = jnp.zeros((32, 128), F32)
    for d in range(9):
        chosen = code_p == float(d)
        for k in range(3):
            amount = jnp.sum(jnp.where(chosen, carried[k], 0.0), axis=1, keepdims=True)
            packed = packed + jnp.where(lanes == d * 3 + k, amount, 0.0)
    load[...] = packed

    def share(source, target_ref, k, device):
        return pltpu.make_async_remote_copy(
            src_ref=source, dst_ref=target_ref, send_sem=ms_sem.at[k], recv_sem=mr_sem.at[k],
            device_id=device, device_id_type=MESH,
        )

    top, bottom = pl.ds(24, 8), pl.ds(0, 8)
    shares = [
        share(load.at[top], near.at[0, bottom], 0, (east, gy)),
        share(load.at[bottom], near.at[1, bottom], 1, (west, gy)),
        share(load, near.at[2], 2, (gx, north)),
        share(load, near.at[3], 3, (gx, south)),
        share(load.at[top], near.at[4, bottom], 4, (east, north)),
        share(load.at[top], near.at[5, bottom], 5, (east, south)),
        share(load.at[bottom], near.at[6, bottom], 6, (west, north)),
        share(load.at[bottom], near.at[7, bottom], 7, (west, south)),
    ]
    for copy in shares:
        copy.start()

    def dry(x, carry):
        first_box = (x // 4) * 8
        for t in range(4):
            drop = jnp.where(
                tile_row < 4,
                cond[pl.ds(first_box + 2 * t, 1), :],
                cond[pl.ds(first_box + 2 * t + 1, 1), :],
            )
            ad[4, x, 8 * t : 8 * t + 8, :] -= drop
        return carry

    lax.fori_loop(0, SX, dry, 0)

    for copy in fetches[2:]:
        copy.wait()
    drained(send1, got1, r1_sem)
    z_re, z_im = [], []
    for c in range(4):
        both = product((first[0, c], first[1, c]), halves(got1[c]), NN)
        z_re.append(both[:HALF])
        z_im.append(both[HALF:])

    def butterfly(re, im, sign):
        s02r, s02i = re[0] + re[2], im[0] + im[2]
        d02r, d02i = re[0] - re[2], im[0] - im[2]
        s13r, s13i = re[1] + re[3], im[1] + im[3]
        d13r, d13i = re[1] - re[3], im[1] - im[3]
        if sign < 0:
            return (
                [s02r + s13r, d02r + d13i, s02r - s13r, d02r - d13i],
                [s02i + s13i, d02i - d13r, s02i - s13i, d02i + d13r],
            )
        return (
            [s02r + s13r, d02r - d13i, s02r - s13r, d02r + d13i],
            [s02i + s13i, d02i + d13r, s02i - s13i, d02i - d13r],
        )

    q_re, q_im = butterfly(z_re, z_im, -1)
    re, im = jnp.concatenate(q_re, axis=0), jnp.concatenate(q_im, axis=0)
    turn_cos, turn_sin = turns[0], turns[1]
    joined = jnp.concatenate([re * turn_cos + im * turn_sin, im * turn_cos - re * turn_sin], axis=1)
    spectrum = product(halves(joined), (ahead[0], ahead[1]), NN)
    eigen = turns[2] + wave[pl.ds(me, 1), :]
    inverse = jnp.where(eigen == 0.0, 0.0, 1.0 / jnp.where(eigen == 0.0, 1.0, eigen))
    solved = spectrum * jnp.concatenate([inverse, inverse], axis=1)
    turned = product(halves(solved), (behind[0], behind[1]), NN)
    re, im = turned[:, :128], turned[:, 128:]
    back_re, back_im = re * turn_cos - im * turn_sin, im * turn_cos + re * turn_sin
    v_re, v_im = butterfly(
        [back_re[HALF * q : HALF * (q + 1)] for q in range(4)],
        [back_im[HALF * q : HALF * (q + 1)] for q in range(4)],
        1,
    )
    wide_lane = lax.broadcasted_iota(jnp.int32, (128, 128), 1)
    edge = None
    for c in range(4):
        stacked = jnp.concatenate([v_re[c], v_im[c]], axis=0)
        plane = product((last[0, c], last[1, c]), halves(stacked), NN)
        send2[c] = plane
        if c == 0:
            next_x = pltpu.roll(plane, 120, 0)
        picked = jnp.where((wide_lane & 31) == 0, plane, 0.0)
        picked = picked if c == 0 else pltpu.roll(picked, c, 1)
        edge = picked if edge is None else edge + picked
    row_b = lax.broadcasted_iota(jnp.int32, (128, 128), 0) & 7
    edge = jnp.where(row_b == 7, pltpu.roll(edge, 7, 0), pltpu.roll(edge, 127, 0))
    moved = pltpu.roll(edge, 36, 1)
    in_move = (wide_lane >= 36) & (wide_lane < 40)
    send2[4] = jnp.where(wide_lane < 32, next_x, jnp.where(in_move, moved, edge))

    scatter(send2, modes, s2_sem, r2_sem)
    modes[:, pl.ds(me, 1), :] = send2[:, pl.ds(me, 1), :]

    for copy in shares:
        copy.wait_recv()
    tile_lane = lax.broadcasted_iota(jnp.int32, (8, 128), 1)

    def column_of(x):
        if x < 0:
            return near[0, 0:8, :], near[4, 7:8, :], near[5, 0:1, :]
        if x > 3:
            return near[1, 0:8, :], near[6, 7:8, :], near[7, 0:1, :]
        return load[8 * x : 8 * x + 8, :], near[2, 8 * x + 7 : 8 * x + 8, :], near[3, 8 * x : 8 * x + 1, :]

    arrived = [jnp.zeros((8, 128), F32) for _ in range(4)]
    for x in range(-1, 5):
        centre, low_row, high_row = column_of(x)
        shifted = [
            jnp.where(tile_row == 7, high_row, pltpu.roll(centre, 7, 0)),
            centre,
            jnp.where(tile_row == 0, low_row, pltpu.roll(centre, 1, 0)),
        ]
        for dx in (-1, 0, 1):
            if not 0 <= x + dx < 4:
                continue
            for dy in (-1, 0, 1):
                d = (dx + 1) * 3 + dy + 1
                values = shifted[dy + 1]
                values = values if d == 0 else pltpu.roll(values, 128 - 3 * d, 1)
                arrived[x + dx] = arrived[x + dx] + values
    stacked = jnp.concatenate(arrived + [jnp.zeros((96, 128), F32)], axis=0) * (1.0 / 64)
    moments_out[...] = stacked.T[0:8, :]

    for copy in halo:
        copy.wait_send()
    for copy in shares:
        copy.wait_send()
    drained(send1, got1, s1_sem)
    drained(send2, send2, s2_sem)
    drained(send2, modes, r2_sem)


def final_kernel(
    modes, ad, moments, back,
    vel_out, theta_out, vapour_out, moments_out,
    fresh, mom_o, pressure, out_sem,
):
    mom_o[...] = moments[0:3, 0:32]
    outs = [
        pltpu.make_async_copy(ad.at[3], theta_out, out_sem.at[0]),
        pltpu.make_async_copy(ad.at[4], vapour_out, out_sem.at[1]),
        pltpu.make_async_copy(mom_o, moments_out, out_sem.at[2]),
    ]
    for copy in outs:
        copy.start()
    row = lax.broadcasted_iota(jnp.int32, (SY, NZ), 0)
    lane = lax.broadcasted_iota(jnp.int32, (SY, NZ), 1)

    def levels(c):
        pressure[pl.ds(128 * c, 128), :] = product(halves(modes[c]), (back[0], back[1]), TN)

    levels(4)
    for c in (3, 2, 1, 0):
        levels(c)
        for i in range(4):
            x = 4 * c + i
            here = pressure[pl.ds(32 * x, 32), :]
            ahead = pressure[pl.ds(32 * x + 32, 32), :]
            line = 512 + (36, 32, 64, 96)[i] + c
            side = jnp.where(row == SY - 1, pressure[line : line + 1, :], pltpu.roll(here, SY - 1, 0))
            above = jnp.where(lane == NZ - 1, here, pltpu.roll(here, NZ - 1, 1))
            fresh[0, x] = ad[0, x] - (ahead - here)
            fresh[1, x] = ad[1, x] - (side - here)
            fresh[2, x] = ad[2, x] - (above - here)
        part = pl.ds(4 * c, 4)
        copy = pltpu.make_async_copy(fresh.at[:, part], vel_out.at[:, part], out_sem.at[3 + c])
        copy.start()
        outs.append(copy)
    for copy in outs:
        copy.wait()


def shards(velocity, theta, vapour, radius_sq, multiplicity, counts, pairing, destination):
    t = tables()
    names = ["cosine", "first", "ahead", "behind", "last", "turns", "wave_z", "box"]
    held = [jnp.asarray(t[name]) for name in names]
    block = (SX, SY, NZ)
    shape = jax.ShapeDtypeStruct
    vmem = pltpu.VMEM
    dma = pltpu.SemaphoreType.DMA
    here = pl.BlockSpec(memory_space=pltpu.VMEM)
    modes, advected, moments = pl.pallas_call(
        step_kernel,
        out_shape=(
            vmem((5, DEV, 128), F32),
            vmem((5,) + block, F32),
            vmem((8, 128), F32),
        ),
        in_specs=[ANY] * 16,
        out_specs=(here,) * 3,
        scratch_shapes=[
            vmem((5, SX + 2, SY, NZ), F32),
            vmem((SY, NZ), F32),
            vmem((SY, NZ), F32),
            vmem((6, SX, NZ), F32),
            vmem((5, SX, NZ), F32),
            vmem((4, 8, NZ), F32),
            vmem((SX, NZ), F32),
            vmem((SX, NZ), F32),
            vmem((4, SY, NZ), F32),
            vmem((4, DEV, 128), F32),
            vmem((4, DEV, 128), F32),
            vmem((5, DEV, 128), F32),
        ]
        + [vmem(t[name].shape, t[name].dtype) for name in names]
        + [
            vmem((32, 64), F32),
            vmem((32, 64), F32),
            vmem((32,), jnp.int32),
            vmem((32, 64), jnp.int32),
            vmem((32, 64), jnp.int32),
            vmem((32, 128), F32),
            vmem((32, 128), F32),
            vmem((8, 32, 128), F32),
            pltpu.SemaphoreType.REGULAR((1,)),
            dma((3,)),
            dma((5,)),
            dma((8,)),
            dma((18,)),
            dma((18,)),
            dma(()),
            dma(()),
            dma(()),
            dma(()),
            dma((8,)),
            dma((8,)),
        ],
        compiler_params=pltpu.CompilerParams(
            has_side_effects=True, collective_id=1, vmem_limit_bytes=24 << 20
        ),
        name="cloud_step",
    )(*[
        pltpu.with_memory_space_constraint(value, pltpu.HBM)
        for value in (
            velocity, theta, vapour, radius_sq.T, multiplicity.T, counts, pairing, destination.T, *held
        )
    ])
    return pl.pallas_call(
        final_kernel,
        out_shape=(
            shape((3,) + block, F32),
            shape(block, F32),
            shape(block, F32),
            shape((3, 32), F32),
        ),
        in_specs=[here] * 4,
        out_specs=(ANY,) * 4,
        scratch_shapes=[
            vmem((3,) + block, F32),
            vmem((3, 32), F32),
            vmem((640, 128), F32),
            dma((7,)),
        ],
        compiler_params=pltpu.CompilerParams(vmem_limit_bytes=12 << 20),
        name="project",
    )(
        *[pltpu.with_memory_space_constraint(value, pltpu.VMEM) for value in (modes, advected, moments)],
        jnp.asarray(t["back"]),
    )


def solution(mesh):
    placed = (
        P(None, "gx", "gy", None),
        P("gx", "gy", None),
        P("gx", "gy", None),
        P(None, ("gx", "gy")),
        P(None, ("gx", "gy")),
        P(("gx", "gy")),
        P(("gx", "gy"), None),
        P(None, ("gx", "gy")),
    )
    return jax.shard_map(
        shards,
        mesh=mesh,
        in_specs=placed,
        out_specs=(
            P(None, "gx", "gy", None),
            P("gx", "gy", None),
            P("gx", "gy", None),
            P(None, ("gx", "gy")),
        ),
        check_vma=False,
    )
```

```python
import functools
import math

import jax
import jax.numpy as jnp
import numpy as np
from jax import lax
from jax.experimental import pallas as pl
from jax.experimental.pallas import tpu as pltpu
from jax.sharding import PartitionSpec as P

MESH = pl.DeviceIdType.MESH
GX, GY = 16, 8
DEV = GX * GY
SX, SY, NZ = 16, 32, 128
NX, NY = 256, 256
HALF = 72
F32 = jnp.float32
BF16 = jnp.bfloat16
ANY = pl.BlockSpec(memory_space=pl.ANY)


def split_table(table):
    table = np.asarray(table, np.float32)
    high = table.astype(jnp.bfloat16)
    low = (table - high.astype(np.float32)).astype(jnp.bfloat16)
    return np.stack([high, low])


@functools.cache
def send_order():
    hops = (0, 1, 2, 1)
    peers = [(rx, ry) for rx in range(GX) for ry in range(GY) if rx or ry]
    peers.sort(key=lambda p: -(hops[p[0] // 4] + hops[p[0] % 4] + hops[p[1] // 2]))
    classes = {}
    for p in peers:
        classes.setdefault((p[0] // 4 > 2, p[0] % 4 > 2, p[1] // 2 > 2, p[1] % 2), []).append(p)
    queues = list(classes.values())
    order = []
    while any(queues):
        for queue in queues:
            if queue:
                order.append(queue.pop(0))
    return tuple(order)


@functools.cache
def tables():
    tau = 2.0 * math.pi
    z = np.arange(NZ)
    cosine = np.cos(math.pi * (z[None, :] + 0.5) * z[:, None] / NZ)
    weight = np.where(z == 0, 1.0 / NZ, 2.0 / NZ)
    back = cosine * weight[:, None]
    rows, factor, seen = [], [], set()
    for p in range(16):
        for q in range(8):
            if (p, q) in seen:
                continue
            mirror = (-p % 16, -q % 8)
            seen.update({(p, q), mirror})
            rows.append((p, q))
            factor.append(1.0 if mirror == (p, q) else 2.0)
    pad = HALF - len(rows)
    low_x = np.array([r[0] for r in rows] + [0] * pad)
    low_y = np.array([r[1] for r in rows] + [0] * pad)
    factor = np.array(factor + [0.0] * pad)
    used = np.array([1.0] * len(rows) + [0.0] * pad)
    a = np.repeat(np.arange(16), 8)
    b = np.tile(np.arange(8), 16)
    first, last = [], []
    for c in range(4):
        angle = tau * (
            low_x[:, None] * a[None] / 16.0
            + low_y[:, None] * b[None] / 8.0
            + low_x[:, None] * c / 64.0
        )
        first.append(np.concatenate([np.cos(angle) * used[:, None], -np.sin(angle) * used[:, None]]))
        scale = factor[:, None] / (NX * NY)
        last.append(np.concatenate([np.cos(angle) * scale, -np.sin(angle) * scale]).T)
    lane_i = np.repeat(np.arange(4), 32)
    lane_j = np.tile(np.arange(32), 4)
    turn_cos, turn_sin, wave = [], [], []
    for q in range(4):
        kx0 = low_x + 16 * q
        angle = tau * (kx0[:, None] * lane_i[None] + low_y[:, None] * lane_j[None]) / 256.0
        turn_cos.append(np.cos(angle))
        turn_sin.append(np.sin(angle))
        kx = kx0[:, None] + 64 * lane_i[None]
        ky = low_y[:, None] + 8 * lane_j[None]
        wave.append(-4.0 * np.sin(math.pi * kx / NX) ** 2 - 4.0 * np.sin(math.pi * ky / NY) ** 2)
    turns = np.stack([np.concatenate(turn_cos), np.concatenate(turn_sin), np.concatenate(wave)])
    angle = tau * (lane_i[:, None] * lane_i[None] / 4.0 + lane_j[:, None] * lane_j[None] / 32.0)
    cos2, sin2 = np.cos(angle), np.sin(angle)
    ahead = np.block([[cos2, -sin2], [sin2, cos2]])
    behind = np.block([[cos2, sin2], [-sin2, cos2]])
    wave_z = -4.0 * np.sin(math.pi * z / (2.0 * NZ)) ** 2
    wave_z = np.broadcast_to(wave_z[:, None], (NZ, 128)).astype(np.float32)
    box = np.zeros((32, 128), np.float32)
    for column in range(4):
        for j in range(32):
            box[column * 8 + j // 4, column * 32 + j] = 1.0
    return dict(
        cosine=packed_left(cosine),
        first=packed_left(np.stack(first)),
        ahead=split_table(ahead),
        behind=split_table(behind),
        last=split_table(np.stack(last)),
        turns=turns.astype(np.float32),
        wave_z=wave_z,
        box=box.astype(jnp.bfloat16),
        back=np.block([[*split_table(back)], [split_table(back)[0], np.zeros((NZ, NZ), jnp.bfloat16)]]),
    )


def halves(values):
    high = values.astype(BF16)
    return high, (values - high.astype(F32)).astype(BF16)


def product(left, right, dims):
    def one(x, y):
        return lax.dot_general(x, y, (dims, ((), ())), preferred_element_type=F32)

    (left_high, left_low), (right_high, right_low) = left, right
    return one(left_high, right_high) + (one(left_high, right_low) + one(left_low, right_high))


def packed_left(table):
    high, low = split_table(table)
    return np.concatenate([high, low], axis=-1)


def fold(wide):
    return wide[:, :128] + wide[:, 128:]


def packed_right(high, low):
    zero = jnp.zeros_like(low)
    return jnp.concatenate(
        [jnp.concatenate([high, low], axis=1), jnp.concatenate([high, zero], axis=1)], axis=0
    )


def one_product(left, right, dims):
    return lax.dot_general(left, right, (dims, ((), ())), preferred_element_type=F32)


NN = ((1,), (0,))
NT = ((1,), (1,))
TN = ((0,), (0,))


def step_kernel(
    vel, theta, vapour, radius, multi, counts, pairing, dest,
    cosine_h, first_h, ahead_h, behind_h, last_h, turns_h, wave_h, box_h,
    modes, ad, moments_out,
    fp, before_u, xu2, yl, yh, corner, row_y0, below_y, quad, send1, got1, send2,
    cosine, first, ahead, behind, last, turns, wave, box,
    rad_v, mul_v, cnt_v, pair_v, dst_v, cond, load, near,
    known, load_sem, drop_sem, table_sem, hs_sem, hr_sem, s1_sem, r1_sem, s2_sem, r2_sem,
    ms_sem, mr_sem,
):
    gx = lax.axis_index("gx")
    gy = lax.axis_index("gy")
    me = gx * GY + gy
    east, west = lax.rem(gx + 1, GX), lax.rem(gx + GX - 1, GX)
    north, south = lax.rem(gy + 1, GY), lax.rem(gy + GY - 1, GY)
    peers_x = [lax.rem(gx + r, GX) for r in range(GX)]
    peers_y = [lax.rem(gy + r, GY) for r in range(GY)]

    loads = [
        pltpu.make_async_copy(vel, fp.at[pl.ds(0, 3), pl.ds(1, SX)], load_sem.at[0]),
        pltpu.make_async_copy(theta, fp.at[3, pl.ds(1, SX)], load_sem.at[1]),
        pltpu.make_async_copy(vapour, fp.at[4, pl.ds(1, SX)], load_sem.at[2]),
    ]
    drops = [
        pltpu.make_async_copy(source, target, drop_sem.at[k])
        for k, (source, target) in enumerate(
            [(radius, rad_v), (multi, mul_v), (counts, cnt_v), (pairing, pair_v), (dest, dst_v)]
        )
    ]
    table_pairs = [
        (cosine_h, cosine), (box_h, box), (first_h, first), (turns_h, turns), (ahead_h, ahead),
        (wave_h, wave), (behind_h, behind), (last_h, last),
    ]
    fetches = [
        pltpu.make_async_copy(source, target, table_sem.at[k])
        for k, (source, target) in enumerate(table_pairs)
    ]
    for copy in loads + drops + fetches:
        copy.start()

    barrier = pltpu.get_barrier_semaphore()

    chip_z, chip_x, chip_y, core = gx // 4, lax.rem(gx, 4), gy // 2, lax.rem(gy, 2)

    def away(step_z, step_x, step_y, step_core):
        to_z, to_x, to_y = (
            lax.rem(at + 4 + step, 4)
            for at, step in ((chip_z, step_z), (chip_x, step_x), (chip_y, step_y))
        )
        return to_z * 4 + to_x, to_y * 2 + lax.rem(core + step_core, 2)

    steps = [(k, i, j, n) for k in (0, 1, -1) for i in (1, -1, 0) for j in (1, -1, 0) for n in (0, 1)]
    around = [away(*step) for step in steps if any(step)]
    corners = [away(k, i, j, 0) for k in (1, -1) for i in (1, -1) for j in (1, -1)]
    for device in around:
        pl.semaphore_signal(barrier, inc=1, device_id=device, device_id_type=MESH)
    pl.semaphore_wait(barrier, len(around))

    def remote(source, target_ref, k, device):
        return pltpu.make_async_remote_copy(
            src_ref=source, dst_ref=target_ref, send_sem=hs_sem.at[k], recv_sem=hr_sem.at[k],
            device_id=device, device_id_type=MESH,
        )

    wind = [
        remote(vel.at[:, SX - 1], fp.at[pl.ds(0, 3), 0], 0, (east, gy)),
        remote(vel.at[:, 0], fp.at[pl.ds(0, 3), SX + 1], 1, (west, gy)),
        remote(vel.at[0, SX - 2], xu2, 2, (east, gy)),
        remote(vel.at[:, :, SY - 1], yl.at[pl.ds(0, 3)], 3, (gx, north)),
        remote(vel.at[:, :, 0], yh.at[pl.ds(0, 3)], 4, (gx, south)),
        remote(vel.at[1, :, SY - 2], yl.at[5], 5, (gx, north)),
        remote(vel.at[0, SX - 1, pl.ds(SY - 1, 1)], corner.at[0, pl.ds(0, 1)], 6, (east, north)),
        remote(vel.at[0, SX - 1, pl.ds(0, 1)], corner.at[1, pl.ds(0, 1)], 7, (east, south)),
        remote(vel.at[1, SX - 1, pl.ds(SY - 1, 1)], corner.at[2, pl.ds(0, 1)], 8, (east, north)),
        remote(vel.at[1, 0, pl.ds(SY - 1, 1)], corner.at[3, pl.ds(0, 1)], 9, (west, north)),
    ]
    air = [
        remote(theta.at[SX - 1], fp.at[3, 0], 10, (east, gy)),
        remote(vapour.at[SX - 1], fp.at[4, 0], 11, (east, gy)),
        remote(theta.at[0], fp.at[3, SX + 1], 12, (west, gy)),
        remote(vapour.at[0], fp.at[4, SX + 1], 13, (west, gy)),
        remote(theta.at[:, SY - 1], yl.at[3], 14, (gx, north)),
        remote(vapour.at[:, SY - 1], yl.at[4], 15, (gx, north)),
        remote(theta.at[:, 0], yh.at[3], 16, (gx, south)),
        remote(vapour.at[:, 0], yh.at[4], 17, (gx, south)),
    ]
    halo = wind + air
    for copy in wind[6:] + wind[:6]:
        copy.start()

    def pass_on(k, devices):
        for device in devices:
            pl.semaphore_signal(known.at[k], inc=1, device_id=device, device_id_type=MESH)

    pass_on(0, corners)
    for copy in loads:
        copy.wait()

    row = lax.broadcasted_iota(jnp.int32, (SY, NZ), 0)
    lane = lax.broadcasted_iota(jnp.int32, (SY, NZ), 1)
    tile_row = lax.broadcasted_iota(jnp.int32, (8, NZ), 0)

    def upward(values):
        return pltpu.roll(values, NZ - 1, 1)

    def downward(values):
        return pltpu.roll(values, 1, 1)

    def coefficients(speed, shape_lane=None):
        scaled = 0.1 * speed
        return 0.01 - scaled, 0.01 + scaled

    def vertical(speed, lanes):
        up, down = coefficients(speed)
        top, bottom = lanes == NZ - 1, lanes == 0
        centre = 0.94 + jnp.where(top, up, 0.0) + jnp.where(bottom, down, 0.0)
        return jnp.where(top, 0.0, up), jnp.where(bottom, 0.0, down), centre

    def advect_plane(x, fields):
        c_east, c_west = coefficients(fp[0, x + 1])
        c_north, c_south = coefficients(fp[1, x + 1])
        c_north = jnp.where(row == SY - 1, 0.0, c_north)
        c_south = jnp.where(row == 0, 0.0, c_south)
        c_up, c_down, c_mid = vertical(fp[2, x + 1], lane)
        for f in fields:
            centre = fp[f, x + 1]
            ad[f, x] = (
                (c_mid * centre + c_east * fp[f, x + 2] + c_west * fp[f, x])
                + (c_north * pltpu.roll(centre, SY - 1, 0) + c_south * pltpu.roll(centre, 1, 0))
                + (c_up * upward(centre) + c_down * downward(centre))
            )

    def inner(x, carry):
        advect_plane(x, (0, 1, 2))
        row_y0[pl.ds(x, 1), :] = fp[1, x + 1, 0:1, :]
        return carry

    lax.fori_loop(1, SX - 1, inner, 0)
    for copy in drops:
        copy.wait()
    box_row = lax.broadcasted_iota(jnp.int32, (32, 32), 0)
    box_lane = lax.broadcasted_iota(jnp.int32, (32, 32), 1)
    spread = jnp.where(box_row == box_lane, cnt_v[...][None, :].astype(F32), 0.0)
    used = jnp.sum(spread, axis=1, keepdims=True)
    slot = lax.broadcasted_iota(jnp.int32, (32, 64), 1).astype(F32)
    live = jnp.where(slot < used, mul_v[...], 0.0)
    target = dst_v[...]
    local_box = lax.broadcasted_iota(jnp.int32, (32, 64), 0)
    source_x = gx * 4 + (local_box >> 3)
    source_y = gy * 8 + (local_box & 7)
    target_x = (target >> 8) * 4 + ((target & 31) >> 3)
    target_y = ((target >> 5) & 7) * 8 + (target & 7)
    offset_x = (target_x - source_x + 1) & 63
    offset_y = (target_y - source_y + 1) & 63
    code = (offset_x * 3 + offset_y).astype(F32)

    def twice(values):
        return jnp.concatenate([values, values], axis=1)

    pair = twice(pair_v[...])
    order = jnp.where(lax.broadcasted_iota(jnp.int32, (32, 128), 1) < 64, pair, pltpu.roll(pair, 32, 1))
    radius_p = jnp.take_along_axis(twice(rad_v[...]), order, axis=1)
    live_p = jnp.take_along_axis(twice(live), order, axis=1)
    code_p = jnp.take_along_axis(twice(code), order, axis=1)

    for x in (0, SX - 1):
        row_y0[pl.ds(x, 1), :] = fp[1, x + 1, 0:1, :]
    for copy in wind:
        copy.wait_recv()
    for copy in air:
        copy.start()
    advect_plane(0, (0, 1, 2))
    advect_plane(SX - 1, (0, 1, 2))

    speed = fp[0, 0]
    c_east, c_west = coefficients(speed)
    c_north, c_south = coefficients(fp[1, 0])
    c_up, c_down, c_mid = vertical(fp[2, 0], lane)
    above = jnp.where(row == SY - 1, corner[1, 0:1, :], pltpu.roll(speed, SY - 1, 0))
    beneath = jnp.where(row == 0, corner[0, 0:1, :], pltpu.roll(speed, 1, 0))
    before_u[...] = (
        (c_mid * speed + c_east * fp[0, 1] + c_west * xu2[...])
        + (c_north * above + c_south * beneath)
        + (c_up * upward(speed) + c_down * downward(speed))
    )
    speed = yl[1]
    row_x = lax.broadcasted_iota(jnp.int32, (SX, NZ), 0)
    lane_x = lax.broadcasted_iota(jnp.int32, (SX, NZ), 1)
    c_east, c_west = coefficients(yl[0])
    c_north, c_south = coefficients(speed)
    c_up, c_down, c_mid = vertical(yl[2], lane_x)
    after = jnp.where(row_x == SX - 1, corner[3, 0:1, :], pltpu.roll(speed, SX - 1, 0))
    before = jnp.where(row_x == 0, corner[2, 0:1, :], pltpu.roll(speed, 1, 0))
    below_y[...] = (
        (c_mid * speed + c_east * after + c_west * before)
        + (c_north * row_y0[...] + c_south * yl[5])
        + (c_up * upward(speed) + c_down * downward(speed))
    )
    fetches[0].wait()

    def border(x, fields):
        _, c_south = coefficients(fp[1, x + 1, 0:8, :])
        c_north, _ = coefficients(fp[1, x + 1, SY - 8 : SY, :])
        c_south = jnp.where(tile_row == 0, c_south, 0.0)
        c_north = jnp.where(tile_row == 7, c_north, 0.0)
        for f in fields:
            ad[f, x, 0:8, :] += c_south * yl[f, pl.ds(x, 1), :]
            ad[f, x, SY - 8 : SY, :] += c_north * yh[f, pl.ds(x, 1), :]

    def block(c):
        parts = []
        for i in range(4):
            x = c * 4 + i
            border(x, (0, 1, 2))
            star_w = ad[2, x] + 0.1 * fp[3, x + 1]
            ad[2, x] = star_w
            star_v = ad[1, x]
            star_u = ad[0, x]
            if i == 0:
                last_u = before_u[...] if c == 0 else ad[0, x - 1]
            behind_v = jnp.where(row == 0, below_y[pl.ds(x, 1), :], pltpu.roll(star_v, 1, 0))
            below_w = jnp.where(lane == 0, 0.0, downward(star_w))
            parts.append((star_u - last_u) + (star_v - behind_v) + (star_w - below_w))
            last_u = star_u
        chunk = jnp.concatenate(parts, axis=0)
        high, low = halves(chunk)
        wide = jnp.concatenate(
            [jnp.concatenate([high, high], axis=1), jnp.concatenate([low, jnp.zeros_like(low)], axis=1)],
            axis=0,
        )
        send1[c] = fold(one_product(cosine[...], wide, NT))

    def scalars(c, carry):
        total = jnp.zeros((SY, NZ), F32)
        for i in range(4):
            x = c * 4 + i
            advect_plane(x, (3, 4))
            border(x, (3, 4))
            total = total + ad[4, x]
        quad[c] = total
        return carry

    for c in range(4):
        block(c)
    pl.semaphore_wait(known.at[0], len(corners))

    def scatter(source, target_ref, send_sem, recv_sem):
        def one(px, ry):
            py = peers_y[ry]
            pltpu.make_async_remote_copy(
                src_ref=source.at[:, pl.ds(px * GY + py, 1), :],
                dst_ref=target_ref.at[:, pl.ds(me, 1), :],
                send_sem=send_sem, recv_sem=recv_sem, device_id=(px, py), device_id_type=MESH,
            ).start()

        for rx, ry in send_order():
            one(peers_x[rx], ry)

    def drained(source, target_ref, sem):
        count = pl.ds(0, DEV - 1)
        pltpu.make_async_copy(source.at[:, count, :], target_ref.at[:, count, :], sem).wait()

    scatter(send1, got1, s1_sem, r1_sem)
    got1[:, pl.ds(me, 1), :] = send1[:, pl.ds(me, 1), :]

    for copy in air:
        copy.wait_recv()
    lax.fori_loop(0, 4, scalars, 0)
    fetches[1].wait()
    high, low = halves(quad[...].reshape(128, NZ))
    sums = lax.dot_general(box[...], high, (NN, ((), ())), preferred_element_type=F32)
    sums = sums + lax.dot_general(box[...], low, (NN, ((), ())), preferred_element_type=F32)
    mean = jnp.sum(sums, axis=1, keepdims=True) * (1.0 / (16 * NZ))
    soft = jnp.maximum(mean, 0.0) + jnp.log1p(jnp.exp(-jnp.abs(mean)))
    grown = radius_p + 0.5 * soft
    root = jnp.sqrt(grown)
    mass = grown * root
    gain = mass - radius_p * jnp.sqrt(radius_p)

    def other(values):
        return pltpu.roll(values, 64, 1)

    root_sum = root + other(root)
    rate = 0.05 * (root_sum * root_sum * jnp.abs(grown - other(grown)) * other(live_p))
    final = (mass + rate * other(mass)) / (1.0 + rate)
    lanes = lax.broadcasted_iota(jnp.int32, (32, 128), 1)
    own_live = jnp.where(lanes < 64, live_p, 0.0)
    cond[...] = jnp.broadcast_to(jnp.sum(own_live * gain, axis=1, keepdims=True), (32, 128)) * 0.002
    carried = [own_live, own_live * final, own_live * final * final]
    packed = jnp.zeros((32, 128), F32)
    for d in range(9):
        chosen = code_p == float(d)
        for k in range(3):
            amount = jnp.sum(jnp.where(chosen, carried[k], 0.0), axis=1, keepdims=True)
            packed = packed + jnp.where(lanes == d * 3 + k, amount, 0.0)
    load[...] = packed

    def share(source, target_ref, k, device):
        return pltpu.make_async_remote_copy(
            src_ref=source, dst_ref=target_ref, send_sem=ms_sem.at[k], recv_sem=mr_sem.at[k],
            device_id=device, device_id_type=MESH,
        )

    top, bottom = pl.ds(24, 8), pl.ds(0, 8)
    shares = [
        share(load.at[top], near.at[0, bottom], 0, (east, gy)),
        share(load.at[bottom], near.at[1, bottom], 1, (west, gy)),
        share(load, near.at[2], 2, (gx, north)),
        share(load, near.at[3], 3, (gx, south)),
        share(load.at[top], near.at[4, bottom], 4, (east, north)),
        share(load.at[top], near.at[5, bottom], 5, (east, south)),
        share(load.at[bottom], near.at[6, bottom], 6, (west, north)),
        share(load.at[bottom], near.at[7, bottom], 7, (west, south)),
    ]
    for copy in shares:
        copy.start()

    def dry(x, carry):
        first_box = (x // 4) * 8
        for t in range(4):
            drop = jnp.where(
                tile_row < 4,
                cond[pl.ds(first_box + 2 * t, 1), :],
                cond[pl.ds(first_box + 2 * t + 1, 1), :],
            )
            ad[4, x, 8 * t : 8 * t + 8, :] -= drop
        return carry

    lax.fori_loop(0, SX, dry, 0)

    for copy in fetches[2:]:
        copy.wait()
    drained(send1, got1, r1_sem)
    z_re, z_im = [], []
    for c in range(4):
        both = fold(one_product(first[c], packed_right(*halves(got1[c])), NN))
        z_re.append(both[:HALF])
        z_im.append(both[HALF:])

    def butterfly(re, im, sign):
        s02r, s02i = re[0] + re[2], im[0] + im[2]
        d02r, d02i = re[0] - re[2], im[0] - im[2]
        s13r, s13i = re[1] + re[3], im[1] + im[3]
        d13r, d13i = re[1] - re[3], im[1] - im[3]
        if sign < 0:
            return (
                [s02r + s13r, d02r + d13i, s02r - s13r, d02r - d13i],
                [s02i + s13i, d02i - d13r, s02i - s13i, d02i + d13r],
            )
        return (
            [s02r + s13r, d02r - d13i, s02r - s13r, d02r + d13i],
            [s02i + s13i, d02i + d13r, s02i - s13i, d02i - d13r],
        )

    q_re, q_im = butterfly(z_re, z_im, -1)
    re, im = jnp.concatenate(q_re, axis=0), jnp.concatenate(q_im, axis=0)
    turn_cos, turn_sin = turns[0], turns[1]
    joined = jnp.concatenate([re * turn_cos + im * turn_sin, im * turn_cos - re * turn_sin], axis=1)
    spectrum = product(halves(joined), (ahead[0], ahead[1]), NN)
    eigen = turns[2] + wave[pl.ds(me, 1), :]
    inverse = jnp.where(eigen == 0.0, 0.0, 1.0 / jnp.where(eigen == 0.0, 1.0, eigen))
    solved = spectrum * jnp.concatenate([inverse, inverse], axis=1)
    turned = product(halves(solved), (behind[0], behind[1]), NN)
    re, im = turned[:, :128], turned[:, 128:]
    back_re, back_im = re * turn_cos - im * turn_sin, im * turn_cos + re * turn_sin
    v_re, v_im = butterfly(
        [back_re[HALF * q : HALF * (q + 1)] for q in range(4)],
        [back_im[HALF * q : HALF * (q + 1)] for q in range(4)],
        1,
    )
    wide_lane = lax.broadcasted_iota(jnp.int32, (128, 128), 1)
    edge = None
    for c in range(4):
        stacked = jnp.concatenate([v_re[c], v_im[c]], axis=0)
        high, low = halves(stacked)
        wide = one_product(last[0, c], jnp.concatenate([high, low], axis=1), NN)
        plane = fold(wide) + one_product(last[1, c], high, NN)
        send2[c] = plane
        if c == 0:
            next_x = pltpu.roll(plane, 120, 0)
        picked = jnp.where((wide_lane & 31) == 0, plane, 0.0)
        picked = picked if c == 0 else pltpu.roll(picked, c, 1)
        edge = picked if edge is None else edge + picked
    row_b = lax.broadcasted_iota(jnp.int32, (128, 128), 0) & 7
    edge = jnp.where(row_b == 7, pltpu.roll(edge, 7, 0), pltpu.roll(edge, 127, 0))
    moved = pltpu.roll(edge, 36, 1)
    in_move = (wide_lane >= 36) & (wide_lane < 40)
    send2[4] = jnp.where(wide_lane < 32, next_x, jnp.where(in_move, moved, edge))

    scatter(send2, modes, s2_sem, r2_sem)
    modes[:, pl.ds(me, 1), :] = send2[:, pl.ds(me, 1), :]

    for copy in shares:
        copy.wait_recv()
    tile_lane = lax.broadcasted_iota(jnp.int32, (8, 128), 1)

    def column_of(x):
        if x < 0:
            return near[0, 0:8, :], near[4, 7:8, :], near[5, 0:1, :]
        if x > 3:
            return near[1, 0:8, :], near[6, 7:8, :], near[7, 0:1, :]
        return load[8 * x : 8 * x + 8, :], near[2, 8 * x + 7 : 8 * x + 8, :], near[3, 8 * x : 8 * x + 1, :]

    arrived = [jnp.zeros((8, 128), F32) for _ in range(4)]
    for x in range(-1, 5):
        centre, low_row, high_row = column_of(x)
        shifted = [
            jnp.where(tile_row == 7, high_row, pltpu.roll(centre, 7, 0)),
            centre,
            jnp.where(tile_row == 0, low_row, pltpu.roll(centre, 1, 0)),
        ]
        for dx in (-1, 0, 1):
            if not 0 <= x + dx < 4:
                continue
            for dy in (-1, 0, 1):
                d = (dx + 1) * 3 + dy + 1
                values = shifted[dy + 1]
                values = values if d == 0 else pltpu.roll(values, 128 - 3 * d, 1)
                arrived[x + dx] = arrived[x + dx] + values
    stacked = jnp.concatenate(arrived + [jnp.zeros((96, 128), F32)], axis=0) * (1.0 / 64)
    moments_out[...] = stacked.T[0:8, :]

    for copy in halo:
        copy.wait_send()
    for copy in shares:
        copy.wait_send()
    drained(send1, got1, s1_sem)
    drained(send2, send2, s2_sem)
    drained(send2, modes, r2_sem)


def final_kernel(
    modes, ad, moments, back,
    vel_out, theta_out, vapour_out, moments_out,
    fresh, mom_o, pressure, out_sem,
):
    mom_o[...] = moments[0:3, 0:32]
    outs = [
        pltpu.make_async_copy(ad.at[3], theta_out, out_sem.at[0]),
        pltpu.make_async_copy(ad.at[4], vapour_out, out_sem.at[1]),
        pltpu.make_async_copy(mom_o, moments_out, out_sem.at[2]),
    ]
    for copy in outs:
        copy.start()
    row = lax.broadcasted_iota(jnp.int32, (SY, NZ), 0)
    lane = lax.broadcasted_iota(jnp.int32, (SY, NZ), 1)

    def levels(c):
        wide = one_product(jnp.concatenate(halves(modes[c]), axis=0), back[...], TN)
        pressure[pl.ds(128 * c, 128), :] = fold(wide)

    levels(4)
    for c in (3, 2, 1, 0):
        levels(c)
        for i in range(4):
            x = 4 * c + i
            here = pressure[pl.ds(32 * x, 32), :]
            ahead = pressure[pl.ds(32 * x + 32, 32), :]
            line = 512 + (36, 32, 64, 96)[i] + c
            side = jnp.where(row == SY - 1, pressure[line : line + 1, :], pltpu.roll(here, SY - 1, 0))
            above = jnp.where(lane == NZ - 1, here, pltpu.roll(here, NZ - 1, 1))
            fresh[0, x] = ad[0, x] - (ahead - here)
            fresh[1, x] = ad[1, x] - (side - here)
            fresh[2, x] = ad[2, x] - (above - here)
        part = pl.ds(4 * c, 4)
        copy = pltpu.make_async_copy(fresh.at[:, part], vel_out.at[:, part], out_sem.at[3 + c])
        copy.start()
        outs.append(copy)
    for copy in outs:
        copy.wait()


def shards(velocity, theta, vapour, radius_sq, multiplicity, counts, pairing, destination):
    t = tables()
    names = ["cosine", "first", "ahead", "behind", "last", "turns", "wave_z", "box"]
    held = [jnp.asarray(t[name]) for name in names]
    block = (SX, SY, NZ)
    shape = jax.ShapeDtypeStruct
    vmem = pltpu.VMEM
    dma = pltpu.SemaphoreType.DMA
    here = pl.BlockSpec(memory_space=pltpu.VMEM)
    modes, advected, moments = pl.pallas_call(
        step_kernel,
        out_shape=(
            vmem((5, DEV, 128), F32),
            vmem((5,) + block, F32),
            vmem((8, 128), F32),
        ),
        in_specs=[ANY] * 16,
        out_specs=(here,) * 3,
        scratch_shapes=[
            vmem((5, SX + 2, SY, NZ), F32),
            vmem((SY, NZ), F32),
            vmem((SY, NZ), F32),
            vmem((6, SX, NZ), F32),
            vmem((5, SX, NZ), F32),
            vmem((4, 8, NZ), F32),
            vmem((SX, NZ), F32),
            vmem((SX, NZ), F32),
            vmem((4, SY, NZ), F32),
            vmem((4, DEV, 128), F32),
            vmem((4, DEV, 128), F32),
            vmem((5, DEV, 128), F32),
        ]
        + [vmem(t[name].shape, t[name].dtype) for name in names]
        + [
            vmem((32, 64), F32),
            vmem((32, 64), F32),
            vmem((32,), jnp.int32),
            vmem((32, 64), jnp.int32),
            vmem((32, 64), jnp.int32),
            vmem((32, 128), F32),
            vmem((32, 128), F32),
            vmem((8, 32, 128), F32),
            pltpu.SemaphoreType.REGULAR((1,)),
            dma((3,)),
            dma((5,)),
            dma((8,)),
            dma((18,)),
            dma((18,)),
            dma(()),
            dma(()),
            dma(()),
            dma(()),
            dma((8,)),
            dma((8,)),
        ],
        compiler_params=pltpu.CompilerParams(
            has_side_effects=True, collective_id=1, vmem_limit_bytes=24 << 20
        ),
        name="cloud_step",
    )(*[
        pltpu.with_memory_space_constraint(value, pltpu.HBM)
        for value in (
            velocity, theta, vapour, radius_sq.T, multiplicity.T, counts, pairing, destination.T, *held
        )
    ])
    return pl.pallas_call(
        final_kernel,
        out_shape=(
            shape((3,) + block, F32),
            shape(block, F32),
            shape(block, F32),
            shape((3, 32), F32),
        ),
        in_specs=[here] * 4,
        out_specs=(ANY,) * 4,
        scratch_shapes=[
            vmem((3,) + block, F32),
            vmem((3, 32), F32),
            vmem((640, 128), F32),
            dma((7,)),
        ],
        compiler_params=pltpu.CompilerParams(vmem_limit_bytes=12 << 20),
        name="project",
    )(
        *[pltpu.with_memory_space_constraint(value, pltpu.VMEM) for value in (modes, advected, moments)],
        jnp.asarray(t["back"]),
    )


def solution(mesh):
    placed = (
        P(None, "gx", "gy", None),
        P("gx", "gy", None),
        P("gx", "gy", None),
        P(None, ("gx", "gy")),
        P(None, ("gx", "gy")),
        P(("gx", "gy")),
        P(("gx", "gy"), None),
        P(None, ("gx", "gy")),
    )
    return jax.shard_map(
        shards,
        mesh=mesh,
        in_specs=placed,
        out_specs=(
            P(None, "gx", "gy", None),
            P("gx", "gy", None),
            P("gx", "gy", None),
            P(None, ("gx", "gy")),
        ),
        check_vma=False,
    )
```

```python
import functools
import math

import jax
import jax.numpy as jnp
import numpy as np
from jax import lax
from jax.experimental import pallas as pl
from jax.experimental.pallas import tpu as pltpu
from jax.sharding import PartitionSpec as P

MESH = pl.DeviceIdType.MESH
GX, GY = 16, 8
DEV = GX * GY
SX, SY, NZ = 16, 32, 128
NX, NY = 256, 256
HALF = 72
F32 = jnp.float32
BF16 = jnp.bfloat16
ANY = pl.BlockSpec(memory_space=pl.ANY)


def split_table(table):
    table = np.asarray(table, np.float32)
    high = table.astype(jnp.bfloat16)
    low = (table - high.astype(np.float32)).astype(jnp.bfloat16)
    return np.stack([high, low])


@functools.cache
def send_order():
    hops = (0, 1, 2, 1)
    ways = ((0, 0), (1, 0), (1, 1), (0, 1))
    left = [(k, i, j, n) for k in range(4) for i in range(4) for j in range(4) for n in range(2)][1:]
    used, order = [0] * 6, []

    def after(peer):
        return [u + w for u, w in zip(used, sum((ways[step] for step in peer[:3]), ()))]

    while left:
        far = max(sum(hops[step] for step in peer[:3]) for peer in left)
        ring = [peer for peer in left if sum(hops[step] for step in peer[:3]) == far]
        best = min(ring, key=lambda peer: (max(after(peer)), sum(u * u for u in after(peer))))
        used = after(best)
        order.append(best)
        left.remove(best)
    return tuple(order)


@functools.cache
def tables():
    tau = 2.0 * math.pi
    z = np.arange(NZ)
    cosine = np.cos(math.pi * (z[None, :] + 0.5) * z[:, None] / NZ)
    weight = np.where(z == 0, 1.0 / NZ, 2.0 / NZ)
    back = cosine * weight[:, None]
    rows, factor, seen = [], [], set()
    for p in range(16):
        for q in range(8):
            if (p, q) in seen:
                continue
            mirror = (-p % 16, -q % 8)
            seen.update({(p, q), mirror})
            rows.append((p, q))
            factor.append(1.0 if mirror == (p, q) else 2.0)
    pad = HALF - len(rows)
    low_x = np.array([r[0] for r in rows] + [0] * pad)
    low_y = np.array([r[1] for r in rows] + [0] * pad)
    factor = np.array(factor + [0.0] * pad)
    used = np.array([1.0] * len(rows) + [0.0] * pad)
    a = np.repeat(np.arange(16), 8)
    b = np.tile(np.arange(8), 16)
    first, last = [], []
    for c in range(4):
        angle = tau * (
            low_x[:, None] * a[None] / 16.0
            + low_y[:, None] * b[None] / 8.0
            + low_x[:, None] * c / 64.0
        )
        first.append(np.concatenate([np.cos(angle) * used[:, None], -np.sin(angle) * used[:, None]]))
        scale = factor[:, None] / (NX * NY)
        last.append(np.concatenate([np.cos(angle) * scale, -np.sin(angle) * scale]).T)
    lane_i = np.repeat(np.arange(4), 32)
    lane_j = np.tile(np.arange(32), 4)
    turn_cos, turn_sin, wave = [], [], []
    for q in range(4):
        kx0 = low_x + 16 * q
        angle = tau * (kx0[:, None] * lane_i[None] + low_y[:, None] * lane_j[None]) / 256.0
        turn_cos.append(np.cos(angle))
        turn_sin.append(np.sin(angle))
        kx = kx0[:, None] + 64 * lane_i[None]
        ky = low_y[:, None] + 8 * lane_j[None]
        wave.append(-4.0 * np.sin(math.pi * kx / NX) ** 2 - 4.0 * np.sin(math.pi * ky / NY) ** 2)
    turns = np.stack([np.concatenate(turn_cos), np.concatenate(turn_sin), np.concatenate(wave)])
    angle = tau * (lane_i[:, None] * lane_i[None] / 4.0 + lane_j[:, None] * lane_j[None] / 32.0)
    cos2, sin2 = np.cos(angle), np.sin(angle)
    ahead = np.block([[cos2, -sin2], [sin2, cos2]])
    behind = np.block([[cos2, sin2], [-sin2, cos2]])
    wave_z = -4.0 * np.sin(math.pi * z / (2.0 * NZ)) ** 2
    wave_z = np.broadcast_to(wave_z[:, None], (NZ, 128)).astype(np.float32)
    box = np.zeros((32, 128), np.float32)
    for column in range(4):
        for j in range(32):
            box[column * 8 + j // 4, column * 32 + j] = 1.0
    return dict(
        cosine=packed_left(cosine),
        first=packed_left(np.stack(first)),
        ahead=split_table(ahead),
        behind=split_table(behind),
        last=split_table(np.stack(last)),
        turns=turns.astype(np.float32),
        wave_z=wave_z,
        box=box.astype(jnp.bfloat16),
        back=np.block([[*split_table(back)], [split_table(back)[0], np.zeros((NZ, NZ), jnp.bfloat16)]]),
    )


def halves(values):
    high = values.astype(BF16)
    return high, (values - high.astype(F32)).astype(BF16)


def product(left, right, dims):
    def one(x, y):
        return lax.dot_general(x, y, (dims, ((), ())), preferred_element_type=F32)

    (left_high, left_low), (right_high, right_low) = left, right
    return one(left_high, right_high) + (one(left_high, right_low) + one(left_low, right_high))


def packed_left(table):
    high, low = split_table(table)
    return np.concatenate([high, low], axis=-1)


def fold(wide):
    return wide[:, :128] + wide[:, 128:]


def packed_right(high, low):
    zero = jnp.zeros_like(low)
    return jnp.concatenate(
        [jnp.concatenate([high, low], axis=1), jnp.concatenate([high, zero], axis=1)], axis=0
    )


def one_product(left, right, dims):
    return lax.dot_general(left, right, (dims, ((), ())), preferred_element_type=F32)


NN = ((1,), (0,))
NT = ((1,), (1,))
TN = ((0,), (0,))


def step_kernel(
    vel, theta, vapour, radius, multi, counts, pairing, dest,
    cosine_h, first_h, ahead_h, behind_h, last_h, turns_h, wave_h, box_h,
    modes, ad, moments_out,
    fp, before_u, xu2, yl, yh, corner, row_y0, below_y, quad, send1, got1, send2,
    cosine, first, ahead, behind, last, turns, wave, box,
    rad_v, mul_v, cnt_v, pair_v, dst_v, cond, load, near,
    known, load_sem, drop_sem, table_sem, hs_sem, hr_sem, s1_sem, r1_sem, s2_sem, r2_sem,
    ms_sem, mr_sem,
):
    gx = lax.axis_index("gx")
    gy = lax.axis_index("gy")
    me = gx * GY + gy
    east, west = lax.rem(gx + 1, GX), lax.rem(gx + GX - 1, GX)
    north, south = lax.rem(gy + 1, GY), lax.rem(gy + GY - 1, GY)

    loads = [
        pltpu.make_async_copy(vel, fp.at[pl.ds(0, 3), pl.ds(1, SX)], load_sem.at[0]),
        pltpu.make_async_copy(theta, fp.at[3, pl.ds(1, SX)], load_sem.at[1]),
        pltpu.make_async_copy(vapour, fp.at[4, pl.ds(1, SX)], load_sem.at[2]),
    ]
    drops = [
        pltpu.make_async_copy(source, target, drop_sem.at[k])
        for k, (source, target) in enumerate(
            [(radius, rad_v), (multi, mul_v), (counts, cnt_v), (pairing, pair_v), (dest, dst_v)]
        )
    ]
    table_pairs = [
        (cosine_h, cosine), (box_h, box), (first_h, first), (turns_h, turns), (ahead_h, ahead),
        (wave_h, wave), (behind_h, behind), (last_h, last),
    ]
    fetches = [
        pltpu.make_async_copy(source, target, table_sem.at[k])
        for k, (source, target) in enumerate(table_pairs)
    ]
    for copy in loads + drops + fetches:
        copy.start()

    barrier = pltpu.get_barrier_semaphore()

    chip_z, chip_x, chip_y, core = gx // 4, lax.rem(gx, 4), gy // 2, lax.rem(gy, 2)

    peers_x = [[lax.rem(chip_z + k, 4) * 4 + lax.rem(chip_x + i, 4) for i in range(4)] for k in range(4)]
    peers_y = [[lax.rem(chip_y + j, 4) * 2 + lax.rem(core + n, 2) for n in range(2)] for j in range(4)]

    def away(step_z, step_x, step_y, step_core):
        return peers_x[step_z % 4][step_x % 4], peers_y[step_y % 4][step_core]

    steps = [(k, i, j, n) for k in (0, 1, -1) for i in (1, -1, 0) for j in (1, -1, 0) for n in (0, 1)]
    around = [away(*step) for step in steps if any(step)]
    corners = [away(k, i, j, 0) for k in (1, -1) for i in (1, -1) for j in (1, -1)]
    for device in around:
        pl.semaphore_signal(barrier, inc=1, device_id=device, device_id_type=MESH)
    pl.semaphore_wait(barrier, len(around))

    def remote(source, target_ref, k, device):
        return pltpu.make_async_remote_copy(
            src_ref=source, dst_ref=target_ref, send_sem=hs_sem.at[k], recv_sem=hr_sem.at[k],
            device_id=device, device_id_type=MESH,
        )

    winds = fp.at[pl.ds(0, 3)]
    wind = [
        remote(winds.at[:, SX], fp.at[pl.ds(0, 3), 0], 0, (east, gy)),
        remote(winds.at[:, 1], fp.at[pl.ds(0, 3), SX + 1], 1, (west, gy)),
        remote(fp.at[0, SX - 1], xu2, 2, (east, gy)),
        remote(winds.at[:, pl.ds(1, SX), SY - 1], yl.at[pl.ds(0, 3)], 3, (gx, north)),
        remote(winds.at[:, pl.ds(1, SX), 0], yh.at[pl.ds(0, 3)], 4, (gx, south)),
        remote(fp.at[1, pl.ds(1, SX), SY - 2], yl.at[5], 5, (gx, north)),
        remote(fp.at[0, SX, pl.ds(SY - 1, 1)], corner.at[0, pl.ds(0, 1)], 6, (east, north)),
        remote(fp.at[0, SX, pl.ds(0, 1)], corner.at[1, pl.ds(0, 1)], 7, (east, south)),
        remote(fp.at[1, SX, pl.ds(SY - 1, 1)], corner.at[2, pl.ds(0, 1)], 8, (east, north)),
        remote(fp.at[1, 1, pl.ds(SY - 1, 1)], corner.at[3, pl.ds(0, 1)], 9, (west, north)),
    ]
    air = [
        remote(fp.at[3, SX], fp.at[3, 0], 10, (east, gy)),
        remote(fp.at[4, SX], fp.at[4, 0], 11, (east, gy)),
        remote(fp.at[3, 1], fp.at[3, SX + 1], 12, (west, gy)),
        remote(fp.at[4, 1], fp.at[4, SX + 1], 13, (west, gy)),
        remote(fp.at[3, pl.ds(1, SX), SY - 1], yl.at[3], 14, (gx, north)),
        remote(fp.at[4, pl.ds(1, SX), SY - 1], yl.at[4], 15, (gx, north)),
        remote(fp.at[3, pl.ds(1, SX), 0], yh.at[3], 16, (gx, south)),
        remote(fp.at[4, pl.ds(1, SX), 0], yh.at[4], 17, (gx, south)),
    ]
    halo = wind + air
    loads[0].wait()
    for copy in wind[6:] + wind[:6]:
        copy.start()

    def pass_on(k, devices):
        for device in devices:
            pl.semaphore_signal(known.at[k], inc=1, device_id=device, device_id_type=MESH)

    pass_on(0, corners)
    for copy in loads[1:]:
        copy.wait()

    row = lax.broadcasted_iota(jnp.int32, (SY, NZ), 0)
    lane = lax.broadcasted_iota(jnp.int32, (SY, NZ), 1)
    tile_row = lax.broadcasted_iota(jnp.int32, (8, NZ), 0)

    def upward(values):
        return pltpu.roll(values, NZ - 1, 1)

    def downward(values):
        return pltpu.roll(values, 1, 1)

    def coefficients(speed, shape_lane=None):
        scaled = 0.1 * speed
        return 0.01 - scaled, 0.01 + scaled

    def vertical(speed, lanes):
        up, down = coefficients(speed)
        top, bottom = lanes == NZ - 1, lanes == 0
        centre = 0.94 + jnp.where(top, up, 0.0) + jnp.where(bottom, down, 0.0)
        return jnp.where(top, 0.0, up), jnp.where(bottom, 0.0, down), centre

    def advect_plane(x, fields):
        c_east, c_west = coefficients(fp[0, x + 1])
        c_north, c_south = coefficients(fp[1, x + 1])
        c_north = jnp.where(row == SY - 1, 0.0, c_north)
        c_south = jnp.where(row == 0, 0.0, c_south)
        c_up, c_down, c_mid = vertical(fp[2, x + 1], lane)
        for f in fields:
            centre = fp[f, x + 1]
            ad[f, x] = (
                (c_mid * centre + c_east * fp[f, x + 2] + c_west * fp[f, x])
                + (c_north * pltpu.roll(centre, SY - 1, 0) + c_south * pltpu.roll(centre, 1, 0))
                + (c_up * upward(centre) + c_down * downward(centre))
            )

    def inner(x, carry):
        advect_plane(x, (0, 1, 2))
        row_y0[pl.ds(x, 1), :] = fp[1, x + 1, 0:1, :]
        return carry

    lax.fori_loop(1, SX - 1, inner, 0)
    for copy in drops:
        copy.wait()
    box_row = lax.broadcasted_iota(jnp.int32, (32, 32), 0)
    box_lane = lax.broadcasted_iota(jnp.int32, (32, 32), 1)
    spread = jnp.where(box_row == box_lane, cnt_v[...][None, :].astype(F32), 0.0)
    used = jnp.sum(spread, axis=1, keepdims=True)
    slot = lax.broadcasted_iota(jnp.int32, (32, 64), 1).astype(F32)
    live = jnp.where(slot < used, mul_v[...], 0.0)
    target = dst_v[...]
    local_box = lax.broadcasted_iota(jnp.int32, (32, 64), 0)
    source_x = gx * 4 + (local_box >> 3)
    source_y = gy * 8 + (local_box & 7)
    target_x = (target >> 8) * 4 + ((target & 31) >> 3)
    target_y = ((target >> 5) & 7) * 8 + (target & 7)
    offset_x = (target_x - source_x + 1) & 63
    offset_y = (target_y - source_y + 1) & 63
    code = (offset_x * 3 + offset_y).astype(F32)

    def twice(values):
        return jnp.concatenate([values, values], axis=1)

    pair = twice(pair_v[...])
    order = jnp.where(lax.broadcasted_iota(jnp.int32, (32, 128), 1) < 64, pair, pltpu.roll(pair, 32, 1))
    radius_p = jnp.take_along_axis(twice(rad_v[...]), order, axis=1)
    live_p = jnp.take_along_axis(twice(live), order, axis=1)
    code_p = jnp.take_along_axis(twice(code), order, axis=1)

    for x in (0, SX - 1):
        row_y0[pl.ds(x, 1), :] = fp[1, x + 1, 0:1, :]
    for copy in wind:
        copy.wait_recv()
    for copy in air:
        copy.start()
    advect_plane(0, (0, 1, 2))
    advect_plane(SX - 1, (0, 1, 2))

    speed = fp[0, 0]
    c_east, c_west = coefficients(speed)
    c_north, c_south = coefficients(fp[1, 0])
    c_up, c_down, c_mid = vertical(fp[2, 0], lane)
    above = jnp.where(row == SY - 1, corner[1, 0:1, :], pltpu.roll(speed, SY - 1, 0))
    beneath = jnp.where(row == 0, corner[0, 0:1, :], pltpu.roll(speed, 1, 0))
    before_u[...] = (
        (c_mid * speed + c_east * fp[0, 1] + c_west * xu2[...])
        + (c_north * above + c_south * beneath)
        + (c_up * upward(speed) + c_down * downward(speed))
    )
    speed = yl[1]
    row_x = lax.broadcasted_iota(jnp.int32, (SX, NZ), 0)
    lane_x = lax.broadcasted_iota(jnp.int32, (SX, NZ), 1)
    c_east, c_west = coefficients(yl[0])
    c_north, c_south = coefficients(speed)
    c_up, c_down, c_mid = vertical(yl[2], lane_x)
    after = jnp.where(row_x == SX - 1, corner[3, 0:1, :], pltpu.roll(speed, SX - 1, 0))
    before = jnp.where(row_x == 0, corner[2, 0:1, :], pltpu.roll(speed, 1, 0))
    below_y[...] = (
        (c_mid * speed + c_east * after + c_west * before)
        + (c_north * row_y0[...] + c_south * yl[5])
        + (c_up * upward(speed) + c_down * downward(speed))
    )
    fetches[0].wait()

    def border(x, fields):
        _, c_south = coefficients(fp[1, x + 1, 0:8, :])
        c_north, _ = coefficients(fp[1, x + 1, SY - 8 : SY, :])
        c_south = jnp.where(tile_row == 0, c_south, 0.0)
        c_north = jnp.where(tile_row == 7, c_north, 0.0)
        for f in fields:
            ad[f, x, 0:8, :] += c_south * yl[f, pl.ds(x, 1), :]
            ad[f, x, SY - 8 : SY, :] += c_north * yh[f, pl.ds(x, 1), :]

    def block(c):
        parts = []
        for i in range(4):
            x = c * 4 + i
            border(x, (0, 1, 2))
            star_w = ad[2, x] + 0.1 * fp[3, x + 1]
            ad[2, x] = star_w
            star_v = ad[1, x]
            star_u = ad[0, x]
            if i == 0:
                last_u = before_u[...] if c == 0 else ad[0, x - 1]
            behind_v = jnp.where(row == 0, below_y[pl.ds(x, 1), :], pltpu.roll(star_v, 1, 0))
            below_w = jnp.where(lane == 0, 0.0, downward(star_w))
            parts.append((star_u - last_u) + (star_v - behind_v) + (star_w - below_w))
            last_u = star_u
        chunk = jnp.concatenate(parts, axis=0)
        high, low = halves(chunk)
        wide = jnp.concatenate(
            [jnp.concatenate([high, high], axis=1), jnp.concatenate([low, jnp.zeros_like(low)], axis=1)],
            axis=0,
        )
        send1[c] = fold(one_product(cosine[...], wide, NT))

    def scalars(c, carry):
        total = jnp.zeros((SY, NZ), F32)
        for i in range(4):
            x = c * 4 + i
            advect_plane(x, (3, 4))
            border(x, (3, 4))
            total = total + ad[4, x]
        quad[c] = total
        return carry

    for c in range(4):
        block(c)
    pl.semaphore_wait(known.at[0], len(corners))

    def scatter(source, target_ref, send_sem, recv_sem):
        for step_z, step_x, step_y, step_core in send_order():
            px, py = peers_x[step_z][step_x], peers_y[step_y][step_core]
            pltpu.make_async_remote_copy(
                src_ref=source.at[:, pl.ds(px * GY + py, 1), :],
                dst_ref=target_ref.at[:, pl.ds(me, 1), :],
                send_sem=send_sem, recv_sem=recv_sem, device_id=(px, py), device_id_type=MESH,
            ).start()

    def drained(source, target_ref, sem):
        count = pl.ds(0, DEV - 1)
        pltpu.make_async_copy(source.at[:, count, :], target_ref.at[:, count, :], sem).wait()

    scatter(send1, got1, s1_sem, r1_sem)
    got1[:, pl.ds(me, 1), :] = send1[:, pl.ds(me, 1), :]

    for copy in air:
        copy.wait_recv()
    lax.fori_loop(0, 4, scalars, 0)
    fetches[1].wait()
    high, low = halves(quad[...].reshape(128, NZ))
    sums = lax.dot_general(box[...], high, (NN, ((), ())), preferred_element_type=F32)
    sums = sums + lax.dot_general(box[...], low, (NN, ((), ())), preferred_element_type=F32)
    mean = jnp.sum(sums, axis=1, keepdims=True) * (1.0 / (16 * NZ))
    soft = jnp.maximum(mean, 0.0) + jnp.log1p(jnp.exp(-jnp.abs(mean)))
    grown = radius_p + 0.5 * soft
    root = jnp.sqrt(grown)
    mass = grown * root
    gain = mass - radius_p * jnp.sqrt(radius_p)

    def other(values):
        return pltpu.roll(values, 64, 1)

    root_sum = root + other(root)
    rate = 0.05 * (root_sum * root_sum * jnp.abs(grown - other(grown)) * other(live_p))
    final = (mass + rate * other(mass)) / (1.0 + rate)
    lanes = lax.broadcasted_iota(jnp.int32, (32, 128), 1)
    own_live = jnp.where(lanes < 64, live_p, 0.0)
    cond[...] = jnp.broadcast_to(jnp.sum(own_live * gain, axis=1, keepdims=True), (32, 128)) * 0.002
    carried = [own_live, own_live * final, own_live * final * final]
    packed = jnp.zeros((32, 128), F32)
    for d in range(9):
        chosen = code_p == float(d)
        for k in range(3):
            amount = jnp.sum(jnp.where(chosen, carried[k], 0.0), axis=1, keepdims=True)
            packed = packed + jnp.where(lanes == d * 3 + k, amount, 0.0)
    load[...] = packed

    def share(source, target_ref, k, device):
        return pltpu.make_async_remote_copy(
            src_ref=source, dst_ref=target_ref, send_sem=ms_sem.at[k], recv_sem=mr_sem.at[k],
            device_id=device, device_id_type=MESH,
        )

    top, bottom = pl.ds(24, 8), pl.ds(0, 8)
    shares = [
        share(load.at[top], near.at[0, bottom], 0, (east, gy)),
        share(load.at[bottom], near.at[1, bottom], 1, (west, gy)),
        share(load, near.at[2], 2, (gx, north)),
        share(load, near.at[3], 3, (gx, south)),
        share(load.at[top], near.at[4, bottom], 4, (east, north)),
        share(load.at[top], near.at[5, bottom], 5, (east, south)),
        share(load.at[bottom], near.at[6, bottom], 6, (west, north)),
        share(load.at[bottom], near.at[7, bottom], 7, (west, south)),
    ]
    for copy in shares:
        copy.start()

    def dry(x, carry):
        first_box = (x // 4) * 8
        for t in range(4):
            drop = jnp.where(
                tile_row < 4,
                cond[pl.ds(first_box + 2 * t, 1), :],
                cond[pl.ds(first_box + 2 * t + 1, 1), :],
            )
            ad[4, x, 8 * t : 8 * t + 8, :] -= drop
        return carry

    lax.fori_loop(0, SX, dry, 0)

    for copy in fetches[2:]:
        copy.wait()
    drained(send1, got1, r1_sem)
    z_re, z_im = [], []
    for c in range(4):
        both = fold(one_product(first[c], packed_right(*halves(got1[c])), NN))
        z_re.append(both[:HALF])
        z_im.append(both[HALF:])

    def butterfly(re, im, sign):
        s02r, s02i = re[0] + re[2], im[0] + im[2]
        d02r, d02i = re[0] - re[2], im[0] - im[2]
        s13r, s13i = re[1] + re[3], im[1] + im[3]
        d13r, d13i = re[1] - re[3], im[1] - im[3]
        if sign < 0:
            return (
                [s02r + s13r, d02r + d13i, s02r - s13r, d02r - d13i],
                [s02i + s13i, d02i - d13r, s02i - s13i, d02i + d13r],
            )
        return (
            [s02r + s13r, d02r - d13i, s02r - s13r, d02r + d13i],
            [s02i + s13i, d02i + d13r, s02i - s13i, d02i - d13r],
        )

    q_re, q_im = butterfly(z_re, z_im, -1)
    re, im = jnp.concatenate(q_re, axis=0), jnp.concatenate(q_im, axis=0)
    turn_cos, turn_sin = turns[0], turns[1]
    joined = jnp.concatenate([re * turn_cos + im * turn_sin, im * turn_cos - re * turn_sin], axis=1)
    spectrum = product(halves(joined), (ahead[0], ahead[1]), NN)
    eigen = turns[2] + wave[pl.ds(me, 1), :]
    inverse = jnp.where(eigen == 0.0, 0.0, 1.0 / jnp.where(eigen == 0.0, 1.0, eigen))
    solved = spectrum * jnp.concatenate([inverse, inverse], axis=1)
    turned = product(halves(solved), (behind[0], behind[1]), NN)
    re, im = turned[:, :128], turned[:, 128:]
    back_re, back_im = re * turn_cos - im * turn_sin, im * turn_cos + re * turn_sin
    v_re, v_im = butterfly(
        [back_re[HALF * q : HALF * (q + 1)] for q in range(4)],
        [back_im[HALF * q : HALF * (q + 1)] for q in range(4)],
        1,
    )
    wide_lane = lax.broadcasted_iota(jnp.int32, (128, 128), 1)
    edge = None
    for c in range(4):
        stacked = jnp.concatenate([v_re[c], v_im[c]], axis=0)
        high, low = halves(stacked)
        wide = one_product(last[0, c], jnp.concatenate([high, low], axis=1), NN)
        plane = fold(wide) + one_product(last[1, c], high, NN)
        send2[c] = plane
        if c == 0:
            next_x = pltpu.roll(plane, 120, 0)
        picked = jnp.where((wide_lane & 31) == 0, plane, 0.0)
        picked = picked if c == 0 else pltpu.roll(picked, c, 1)
        edge = picked if edge is None else edge + picked
    row_b = lax.broadcasted_iota(jnp.int32, (128, 128), 0) & 7
    edge = jnp.where(row_b == 7, pltpu.roll(edge, 7, 0), pltpu.roll(edge, 127, 0))
    moved = pltpu.roll(edge, 36, 1)
    in_move = (wide_lane >= 36) & (wide_lane < 40)
    send2[4] = jnp.where(wide_lane < 32, next_x, jnp.where(in_move, moved, edge))

    scatter(send2, modes, s2_sem, r2_sem)
    modes[:, pl.ds(me, 1), :] = send2[:, pl.ds(me, 1), :]

    for copy in shares:
        copy.wait_recv()
    tile_lane = lax.broadcasted_iota(jnp.int32, (8, 128), 1)

    def column_of(x):
        if x < 0:
            return near[0, 0:8, :], near[4, 7:8, :], near[5, 0:1, :]
        if x > 3:
            return near[1, 0:8, :], near[6, 7:8, :], near[7, 0:1, :]
        return load[8 * x : 8 * x + 8, :], near[2, 8 * x + 7 : 8 * x + 8, :], near[3, 8 * x : 8 * x + 1, :]

    arrived = [jnp.zeros((8, 128), F32) for _ in range(4)]
    for x in range(-1, 5):
        centre, low_row, high_row = column_of(x)
        shifted = [
            jnp.where(tile_row == 7, high_row, pltpu.roll(centre, 7, 0)),
            centre,
            jnp.where(tile_row == 0, low_row, pltpu.roll(centre, 1, 0)),
        ]
        for dx in (-1, 0, 1):
            if not 0 <= x + dx < 4:
                continue
            for dy in (-1, 0, 1):
                d = (dx + 1) * 3 + dy + 1
                values = shifted[dy + 1]
                values = values if d == 0 else pltpu.roll(values, 128 - 3 * d, 1)
                arrived[x + dx] = arrived[x + dx] + values
    stacked = jnp.concatenate(arrived + [jnp.zeros((96, 128), F32)], axis=0) * (1.0 / 64)
    moments_out[...] = stacked.T[0:8, :]

    for copy in halo:
        copy.wait_send()
    for copy in shares:
        copy.wait_send()
    drained(send1, got1, s1_sem)
    drained(send2, send2, s2_sem)
    drained(send2, modes, r2_sem)


def final_kernel(
    modes, ad, moments, back,
    vel_out, theta_out, vapour_out, moments_out,
    fresh, mom_o, pressure, out_sem,
):
    mom_o[...] = moments[0:3, 0:32]
    outs = [
        pltpu.make_async_copy(ad.at[3], theta_out, out_sem.at[0]),
        pltpu.make_async_copy(ad.at[4], vapour_out, out_sem.at[1]),
        pltpu.make_async_copy(mom_o, moments_out, out_sem.at[2]),
    ]
    for copy in outs:
        copy.start()
    row = lax.broadcasted_iota(jnp.int32, (SY, NZ), 0)
    lane = lax.broadcasted_iota(jnp.int32, (SY, NZ), 1)

    def levels(c):
        wide = one_product(jnp.concatenate(halves(modes[c]), axis=0), back[...], TN)
        pressure[pl.ds(128 * c, 128), :] = fold(wide)

    levels(4)
    for c in (3, 2, 1, 0):
        levels(c)
        for i in range(4):
            x = 4 * c + i
            here = pressure[pl.ds(32 * x, 32), :]
            ahead = pressure[pl.ds(32 * x + 32, 32), :]
            line = 512 + (36, 32, 64, 96)[i] + c
            side = jnp.where(row == SY - 1, pressure[line : line + 1, :], pltpu.roll(here, SY - 1, 0))
            above = jnp.where(lane == NZ - 1, here, pltpu.roll(here, NZ - 1, 1))
            fresh[0, x] = ad[0, x] - (ahead - here)
            fresh[1, x] = ad[1, x] - (side - here)
            fresh[2, x] = ad[2, x] - (above - here)
        part = pl.ds(4 * c, 4)
        copy = pltpu.make_async_copy(fresh.at[:, part], vel_out.at[:, part], out_sem.at[3 + c])
        copy.start()
        outs.append(copy)
    for copy in outs:
        copy.wait()


def shards(velocity, theta, vapour, radius_sq, multiplicity, counts, pairing, destination):
    t = tables()
    names = ["cosine", "first", "ahead", "behind", "last", "turns", "wave_z", "box"]
    held = [jnp.asarray(t[name]) for name in names]
    block = (SX, SY, NZ)
    shape = jax.ShapeDtypeStruct
    vmem = pltpu.VMEM
    dma = pltpu.SemaphoreType.DMA
    here = pl.BlockSpec(memory_space=pltpu.VMEM)
    modes, advected, moments = pl.pallas_call(
        step_kernel,
        out_shape=(
            vmem((5, DEV, 128), F32),
            vmem((5,) + block, F32),
            vmem((8, 128), F32),
        ),
        in_specs=[ANY] * 16,
        out_specs=(here,) * 3,
        scratch_shapes=[
            vmem((5, SX + 2, SY, NZ), F32),
            vmem((SY, NZ), F32),
            vmem((SY, NZ), F32),
            vmem((6, SX, NZ), F32),
            vmem((5, SX, NZ), F32),
            vmem((4, 8, NZ), F32),
            vmem((SX, NZ), F32),
            vmem((SX, NZ), F32),
            vmem((4, SY, NZ), F32),
            vmem((4, DEV, 128), F32),
            vmem((4, DEV, 128), F32),
            vmem((5, DEV, 128), F32),
        ]
        + [vmem(t[name].shape, t[name].dtype) for name in names]
        + [
            vmem((32, 64), F32),
            vmem((32, 64), F32),
            vmem((32,), jnp.int32),
            vmem((32, 64), jnp.int32),
            vmem((32, 64), jnp.int32),
            vmem((32, 128), F32),
            vmem((32, 128), F32),
            vmem((8, 32, 128), F32),
            pltpu.SemaphoreType.REGULAR((1,)),
            dma((3,)),
            dma((5,)),
            dma((8,)),
            dma((18,)),
            dma((18,)),
            dma(()),
            dma(()),
            dma(()),
            dma(()),
            dma((8,)),
            dma((8,)),
        ],
        compiler_params=pltpu.CompilerParams(
            has_side_effects=True, collective_id=1, vmem_limit_bytes=24 << 20
        ),
        name="cloud_step",
    )(*[
        pltpu.with_memory_space_constraint(value, pltpu.HBM)
        for value in (
            velocity, theta, vapour, radius_sq.T, multiplicity.T, counts, pairing, destination.T, *held
        )
    ])
    return pl.pallas_call(
        final_kernel,
        out_shape=(
            shape((3,) + block, F32),
            shape(block, F32),
            shape(block, F32),
            shape((3, 32), F32),
        ),
        in_specs=[here] * 4,
        out_specs=(ANY,) * 4,
        scratch_shapes=[
            vmem((3,) + block, F32),
            vmem((3, 32), F32),
            vmem((640, 128), F32),
            dma((7,)),
        ],
        compiler_params=pltpu.CompilerParams(vmem_limit_bytes=12 << 20),
        name="project",
    )(
        *[pltpu.with_memory_space_constraint(value, pltpu.VMEM) for value in (modes, advected, moments)],
        jnp.asarray(t["back"]),
    )


def solution(mesh):
    placed = (
        P(None, "gx", "gy", None),
        P("gx", "gy", None),
        P("gx", "gy", None),
        P(None, ("gx", "gy")),
        P(None, ("gx", "gy")),
        P(("gx", "gy")),
        P(("gx", "gy"), None),
        P(None, ("gx", "gy")),
    )
    return jax.shard_map(
        shards,
        mesh=mesh,
        in_specs=placed,
        out_specs=(
            P(None, "gx", "gy", None),
            P("gx", "gy", None),
            P("gx", "gy", None),
            P(None, ("gx", "gy")),
        ),
        check_vma=False,
    )
```

```python
import functools
import math

import jax
import jax.numpy as jnp
import numpy as np
from jax import lax
from jax.experimental import pallas as pl
from jax.experimental.pallas import tpu as pltpu
from jax.sharding import PartitionSpec as P

MESH = pl.DeviceIdType.MESH
GX, GY = 16, 8
DEV = GX * GY
SX, SY, NZ = 16, 32, 128
NX, NY = 256, 256
HALF = 72
F32 = jnp.float32
BF16 = jnp.bfloat16
ANY = pl.BlockSpec(memory_space=pl.ANY)


def split_table(table):
    table = np.asarray(table, np.float32)
    high = table.astype(jnp.bfloat16)
    low = (table - high.astype(np.float32)).astype(jnp.bfloat16)
    return np.stack([high, low])


@functools.cache
def send_order():
    hops = (0, 1, 2, 1)
    ways = ((0, 0), (1, 0), (1, 1), (0, 1))
    left = [(k, i, j, n) for k in range(4) for i in range(4) for j in range(4) for n in range(2)][1:]
    used, order = [0] * 6, []

    def after(peer):
        return [u + w for u, w in zip(used, sum((ways[step] for step in peer[:3]), ()))]

    while left:
        far = max(sum(hops[step] for step in peer[:3]) for peer in left)
        ring = [peer for peer in left if sum(hops[step] for step in peer[:3]) == far]
        best = min(ring, key=lambda peer: (max(after(peer)), sum(u * u for u in after(peer))))
        used = after(best)
        order.append(best)
        left.remove(best)
    return tuple(order)


@functools.cache
def tables():
    tau = 2.0 * math.pi
    z = np.arange(NZ)
    cosine = np.cos(math.pi * (z[None, :] + 0.5) * z[:, None] / NZ)
    weight = np.where(z == 0, 1.0 / NZ, 2.0 / NZ)
    back = cosine * weight[:, None]
    rows, factor, seen = [], [], set()
    for p in range(16):
        for q in range(8):
            if (p, q) in seen:
                continue
            mirror = (-p % 16, -q % 8)
            seen.update({(p, q), mirror})
            rows.append((p, q))
            factor.append(1.0 if mirror == (p, q) else 2.0)
    pad = HALF - len(rows)
    low_x = np.array([r[0] for r in rows] + [0] * pad)
    low_y = np.array([r[1] for r in rows] + [0] * pad)
    factor = np.array(factor + [0.0] * pad)
    used = np.array([1.0] * len(rows) + [0.0] * pad)
    a = np.repeat(np.arange(16), 8)
    b = np.tile(np.arange(8), 16)
    first, last = [], []
    for c in range(4):
        angle = tau * (
            low_x[:, None] * a[None] / 16.0
            + low_y[:, None] * b[None] / 8.0
            + low_x[:, None] * c / 64.0
        )
        first.append(np.concatenate([np.cos(angle) * used[:, None], -np.sin(angle) * used[:, None]]))
        scale = factor[:, None] / (NX * NY)
        last.append(np.concatenate([np.cos(angle) * scale, -np.sin(angle) * scale]).T)
    lane_i = np.repeat(np.arange(4), 32)
    lane_j = np.tile(np.arange(32), 4)
    turn_cos, turn_sin, wave = [], [], []
    for q in range(4):
        kx0 = low_x + 16 * q
        angle = tau * (kx0[:, None] * lane_i[None] + low_y[:, None] * lane_j[None]) / 256.0
        turn_cos.append(np.cos(angle))
        turn_sin.append(np.sin(angle))
        kx = kx0[:, None] + 64 * lane_i[None]
        ky = low_y[:, None] + 8 * lane_j[None]
        wave.append(-4.0 * np.sin(math.pi * kx / NX) ** 2 - 4.0 * np.sin(math.pi * ky / NY) ** 2)
    turns = np.stack([np.concatenate(turn_cos), np.concatenate(turn_sin), np.concatenate(wave)])
    angle = tau * (lane_i[:, None] * lane_i[None] / 4.0 + lane_j[:, None] * lane_j[None] / 32.0)
    cos2, sin2 = np.cos(angle), np.sin(angle)
    ahead = np.block([[cos2, -sin2], [sin2, cos2]])
    behind = np.block([[cos2, sin2], [-sin2, cos2]])
    wave_z = -4.0 * np.sin(math.pi * z / (2.0 * NZ)) ** 2
    wave_z = np.broadcast_to(wave_z[:, None], (NZ, 128)).astype(np.float32)
    box = np.zeros((32, 128), np.float32)
    for column in range(4):
        for j in range(32):
            box[column * 8 + j // 4, column * 32 + j] = 1.0
    return dict(
        cosine=packed_left(cosine),
        first=packed_left(np.stack(first)),
        ahead=split_table(ahead),
        behind=split_table(behind),
        last=split_table(np.stack(last)),
        turns=turns.astype(np.float32),
        wave_z=wave_z,
        box=box.astype(jnp.bfloat16),
        back=np.block([[*split_table(back)], [split_table(back)[0], np.zeros((NZ, NZ), jnp.bfloat16)]]),
    )


def halves(values):
    high = values.astype(BF16)
    return high, (values - high.astype(F32)).astype(BF16)


def product(left, right, dims):
    def one(x, y):
        return lax.dot_general(x, y, (dims, ((), ())), preferred_element_type=F32)

    (left_high, left_low), (right_high, right_low) = left, right
    return one(left_high, right_high) + (one(left_high, right_low) + one(left_low, right_high))


def packed_left(table):
    high, low = split_table(table)
    return np.concatenate([high, low], axis=-1)


def fold(wide):
    return wide[:, :128] + wide[:, 128:]


def packed_right(high, low):
    zero = jnp.zeros_like(low)
    return jnp.concatenate(
        [jnp.concatenate([high, low], axis=1), jnp.concatenate([high, zero], axis=1)], axis=0
    )


def one_product(left, right, dims):
    return lax.dot_general(left, right, (dims, ((), ())), preferred_element_type=F32)


NN = ((1,), (0,))
NT = ((1,), (1,))
TN = ((0,), (0,))


def step_kernel(
    vel, theta, vapour, radius, multi, counts, pairing, dest,
    cosine_h, first_h, ahead_h, behind_h, last_h, turns_h, wave_h, box_h,
    modes, ad, moments_out,
    fp, before_u, xu2, yl, yh, corner, row_y0, below_y, quad, send1, got1, send2,
    cosine, first, ahead, behind, last, turns, wave, box,
    rad_v, mul_v, cnt_v, pair_v, dst_v, cond, load, near,
    known, load_sem, drop_sem, table_sem, hs_sem, hr_sem, s1_sem, r1_sem, s2_sem, r2_sem,
    ms_sem, mr_sem,
):
    gx = lax.axis_index("gx")
    gy = lax.axis_index("gy")
    me = gx * GY + gy
    east, west = lax.rem(gx + 1, GX), lax.rem(gx + GX - 1, GX)
    north, south = lax.rem(gy + 1, GY), lax.rem(gy + GY - 1, GY)

    loads = [
        pltpu.make_async_copy(vel, fp.at[pl.ds(0, 3), pl.ds(1, SX)], load_sem.at[0]),
        pltpu.make_async_copy(theta, fp.at[3, pl.ds(1, SX)], load_sem.at[1]),
        pltpu.make_async_copy(vapour, fp.at[4, pl.ds(1, SX)], load_sem.at[2]),
    ]
    drops = [
        pltpu.make_async_copy(source, target, drop_sem.at[k])
        for k, (source, target) in enumerate(
            [(radius, rad_v), (multi, mul_v), (counts, cnt_v), (pairing, pair_v), (dest, dst_v)]
        )
    ]
    table_pairs = [
        (cosine_h, cosine), (box_h, box), (first_h, first), (turns_h, turns), (ahead_h, ahead),
        (wave_h, wave), (behind_h, behind), (last_h, last),
    ]
    fetches = [
        pltpu.make_async_copy(source, target, table_sem.at[k])
        for k, (source, target) in enumerate(table_pairs)
    ]
    for copy in loads + drops + fetches:
        copy.start()

    barrier = pltpu.get_barrier_semaphore()

    chip_z, chip_x, chip_y, core = gx // 4, lax.rem(gx, 4), gy // 2, lax.rem(gy, 2)

    peers_x = [[lax.rem(chip_z + k, 4) * 4 + lax.rem(chip_x + i, 4) for i in range(4)] for k in range(4)]
    peers_y = [[lax.rem(chip_y + j, 4) * 2 + lax.rem(core + n, 2) for n in range(2)] for j in range(4)]

    def away(step_z, step_x, step_y, step_core):
        return peers_x[step_z % 4][step_x % 4], peers_y[step_y % 4][step_core]

    steps = [(k, i, j, n) for k in (0, 1, -1) for i in (1, -1, 0) for j in (1, -1, 0) for n in (0, 1)]
    steps.sort(key=lambda step: -sum(map(abs, step[:3])))
    around = [away(*step) for step in steps if any(step)]
    corners = [away(k, i, j, 0) for k in (1, -1) for i in (1, -1) for j in (1, -1)]
    for device in around:
        pl.semaphore_signal(barrier, inc=1, device_id=device, device_id_type=MESH)
    pl.semaphore_wait(barrier, len(around))

    def remote(source, target_ref, k, device):
        return pltpu.make_async_remote_copy(
            src_ref=source, dst_ref=target_ref, send_sem=hs_sem.at[k], recv_sem=hr_sem.at[k],
            device_id=device, device_id_type=MESH,
        )

    winds = fp.at[pl.ds(0, 3)]
    wind = [
        remote(winds.at[:, SX], fp.at[pl.ds(0, 3), 0], 0, (east, gy)),
        remote(winds.at[:, 1], fp.at[pl.ds(0, 3), SX + 1], 1, (west, gy)),
        remote(fp.at[0, SX - 1], xu2, 2, (east, gy)),
        remote(winds.at[:, pl.ds(1, SX), SY - 1], yl.at[pl.ds(0, 3)], 3, (gx, north)),
        remote(winds.at[:, pl.ds(1, SX), 0], yh.at[pl.ds(0, 3)], 4, (gx, south)),
        remote(fp.at[1, pl.ds(1, SX), SY - 2], yl.at[5], 5, (gx, north)),
        remote(fp.at[0, SX, pl.ds(SY - 1, 1)], corner.at[0, pl.ds(0, 1)], 6, (east, north)),
        remote(fp.at[0, SX, pl.ds(0, 1)], corner.at[1, pl.ds(0, 1)], 7, (east, south)),
        remote(fp.at[1, SX, pl.ds(SY - 1, 1)], corner.at[2, pl.ds(0, 1)], 8, (east, north)),
        remote(fp.at[1, 1, pl.ds(SY - 1, 1)], corner.at[3, pl.ds(0, 1)], 9, (west, north)),
    ]
    air = [
        remote(fp.at[3, SX], fp.at[3, 0], 10, (east, gy)),
        remote(fp.at[4, SX], fp.at[4, 0], 11, (east, gy)),
        remote(fp.at[3, 1], fp.at[3, SX + 1], 12, (west, gy)),
        remote(fp.at[4, 1], fp.at[4, SX + 1], 13, (west, gy)),
        remote(fp.at[3, pl.ds(1, SX), SY - 1], yl.at[3], 14, (gx, north)),
        remote(fp.at[4, pl.ds(1, SX), SY - 1], yl.at[4], 15, (gx, north)),
        remote(fp.at[3, pl.ds(1, SX), 0], yh.at[3], 16, (gx, south)),
        remote(fp.at[4, pl.ds(1, SX), 0], yh.at[4], 17, (gx, south)),
    ]
    halo = wind + air
    loads[0].wait()
    for copy in wind[6:] + wind[:6]:
        copy.start()

    def pass_on(k, devices):
        for device in devices:
            pl.semaphore_signal(known.at[k], inc=1, device_id=device, device_id_type=MESH)

    pass_on(0, corners)
    for copy in loads[1:]:
        copy.wait()

    row = lax.broadcasted_iota(jnp.int32, (SY, NZ), 0)
    lane = lax.broadcasted_iota(jnp.int32, (SY, NZ), 1)
    tile_row = lax.broadcasted_iota(jnp.int32, (8, NZ), 0)

    def upward(values):
        return pltpu.roll(values, NZ - 1, 1)

    def downward(values):
        return pltpu.roll(values, 1, 1)

    def coefficients(speed, shape_lane=None):
        scaled = 0.1 * speed
        return 0.01 - scaled, 0.01 + scaled

    def vertical(speed, lanes):
        up, down = coefficients(speed)
        top, bottom = lanes == NZ - 1, lanes == 0
        centre = 0.94 + jnp.where(top, up, 0.0) + jnp.where(bottom, down, 0.0)
        return jnp.where(top, 0.0, up), jnp.where(bottom, 0.0, down), centre

    def advect_plane(x, fields):
        c_east, c_west = coefficients(fp[0, x + 1])
        c_north, c_south = coefficients(fp[1, x + 1])
        c_north = jnp.where(row == SY - 1, 0.0, c_north)
        c_south = jnp.where(row == 0, 0.0, c_south)
        c_up, c_down, c_mid = vertical(fp[2, x + 1], lane)
        for f in fields:
            centre = fp[f, x + 1]
            ad[f, x] = (
                (c_mid * centre + c_east * fp[f, x + 2] + c_west * fp[f, x])
                + (c_north * pltpu.roll(centre, SY - 1, 0) + c_south * pltpu.roll(centre, 1, 0))
                + (c_up * upward(centre) + c_down * downward(centre))
            )

    def inner(x, carry):
        advect_plane(x, (0, 1, 2))
        row_y0[pl.ds(x, 1), :] = fp[1, x + 1, 0:1, :]
        return carry

    lax.fori_loop(1, SX - 1, inner, 0)
    for copy in air:
        copy.start()

    for copy in drops:
        copy.wait()
    box_row = lax.broadcasted_iota(jnp.int32, (32, 32), 0)
    box_lane = lax.broadcasted_iota(jnp.int32, (32, 32), 1)
    spread = jnp.where(box_row == box_lane, cnt_v[...][None, :].astype(F32), 0.0)
    used = jnp.sum(spread, axis=1, keepdims=True)
    slot = lax.broadcasted_iota(jnp.int32, (32, 64), 1).astype(F32)
    live = jnp.where(slot < used, mul_v[...], 0.0)
    target = dst_v[...]
    local_box = lax.broadcasted_iota(jnp.int32, (32, 64), 0)
    source_x = gx * 4 + (local_box >> 3)
    source_y = gy * 8 + (local_box & 7)
    target_x = (target >> 8) * 4 + ((target & 31) >> 3)
    target_y = ((target >> 5) & 7) * 8 + (target & 7)
    offset_x = (target_x - source_x + 1) & 63
    offset_y = (target_y - source_y + 1) & 63
    code = (offset_x * 3 + offset_y).astype(F32)

    def twice(values):
        return jnp.concatenate([values, values], axis=1)

    pair = twice(pair_v[...])
    order = jnp.where(lax.broadcasted_iota(jnp.int32, (32, 128), 1) < 64, pair, pltpu.roll(pair, 32, 1))
    radius_p = jnp.take_along_axis(twice(rad_v[...]), order, axis=1)
    live_p = jnp.take_along_axis(twice(live), order, axis=1)
    code_p = jnp.take_along_axis(twice(code), order, axis=1)

    for x in (0, SX - 1):
        row_y0[pl.ds(x, 1), :] = fp[1, x + 1, 0:1, :]
    for copy in wind:
        copy.wait_recv()
    advect_plane(0, (0, 1, 2))
    advect_plane(SX - 1, (0, 1, 2))

    speed = fp[0, 0]
    c_east, c_west = coefficients(speed)
    c_north, c_south = coefficients(fp[1, 0])
    c_up, c_down, c_mid = vertical(fp[2, 0], lane)
    above = jnp.where(row == SY - 1, corner[1, 0:1, :], pltpu.roll(speed, SY - 1, 0))
    beneath = jnp.where(row == 0, corner[0, 0:1, :], pltpu.roll(speed, 1, 0))
    before_u[...] = (
        (c_mid * speed + c_east * fp[0, 1] + c_west * xu2[...])
        + (c_north * above + c_south * beneath)
        + (c_up * upward(speed) + c_down * downward(speed))
    )
    speed = yl[1]
    row_x = lax.broadcasted_iota(jnp.int32, (SX, NZ), 0)
    lane_x = lax.broadcasted_iota(jnp.int32, (SX, NZ), 1)
    c_east, c_west = coefficients(yl[0])
    c_north, c_south = coefficients(speed)
    c_up, c_down, c_mid = vertical(yl[2], lane_x)
    after = jnp.where(row_x == SX - 1, corner[3, 0:1, :], pltpu.roll(speed, SX - 1, 0))
    before = jnp.where(row_x == 0, corner[2, 0:1, :], pltpu.roll(speed, 1, 0))
    below_y[...] = (
        (c_mid * speed + c_east * after + c_west * before)
        + (c_north * row_y0[...] + c_south * yl[5])
        + (c_up * upward(speed) + c_down * downward(speed))
    )
    fetches[0].wait()

    def border(x, fields):
        _, c_south = coefficients(fp[1, x + 1, 0:8, :])
        c_north, _ = coefficients(fp[1, x + 1, SY - 8 : SY, :])
        c_south = jnp.where(tile_row == 0, c_south, 0.0)
        c_north = jnp.where(tile_row == 7, c_north, 0.0)
        for f in fields:
            ad[f, x, 0:8, :] += c_south * yl[f, pl.ds(x, 1), :]
            ad[f, x, SY - 8 : SY, :] += c_north * yh[f, pl.ds(x, 1), :]

    def block(c):
        parts = []
        for i in range(4):
            x = c * 4 + i
            border(x, (0, 1, 2))
            star_w = ad[2, x] + 0.1 * fp[3, x + 1]
            ad[2, x] = star_w
            star_v = ad[1, x]
            star_u = ad[0, x]
            if i == 0:
                last_u = before_u[...] if c == 0 else ad[0, x - 1]
            behind_v = jnp.where(row == 0, below_y[pl.ds(x, 1), :], pltpu.roll(star_v, 1, 0))
            below_w = jnp.where(lane == 0, 0.0, downward(star_w))
            parts.append((star_u - last_u) + (star_v - behind_v) + (star_w - below_w))
            last_u = star_u
        chunk = jnp.concatenate(parts, axis=0)
        high, low = halves(chunk)
        wide = jnp.concatenate(
            [jnp.concatenate([high, high], axis=1), jnp.concatenate([low, jnp.zeros_like(low)], axis=1)],
            axis=0,
        )
        send1[c] = fold(one_product(cosine[...], wide, NT))

    def scalars(c, carry):
        total = jnp.zeros((SY, NZ), F32)
        for i in range(4):
            x = c * 4 + i
            advect_plane(x, (3, 4))
            border(x, (3, 4))
            total = total + ad[4, x]
        quad[c] = total
        return carry

    for c in range(4):
        block(c)
    pl.semaphore_wait(known.at[0], len(corners))

    def scatter(source, target_ref, send_sem, recv_sem):
        for step_z, step_x, step_y, step_core in send_order():
            px, py = peers_x[step_z][step_x], peers_y[step_y][step_core]
            pltpu.make_async_remote_copy(
                src_ref=source.at[:, pl.ds(px * GY + py, 1), :],
                dst_ref=target_ref.at[:, pl.ds(me, 1), :],
                send_sem=send_sem, recv_sem=recv_sem, device_id=(px, py), device_id_type=MESH,
            ).start()

    def drained(source, target_ref, sem):
        count = pl.ds(0, DEV - 1)
        pltpu.make_async_copy(source.at[:, count, :], target_ref.at[:, count, :], sem).wait()

    scatter(send1, got1, s1_sem, r1_sem)
    got1[:, pl.ds(me, 1), :] = send1[:, pl.ds(me, 1), :]

    for copy in air:
        copy.wait_recv()
    lax.fori_loop(0, 4, scalars, 0)
    fetches[1].wait()
    high, low = halves(quad[...].reshape(128, NZ))
    sums = lax.dot_general(box[...], high, (NN, ((), ())), preferred_element_type=F32)
    sums = sums + lax.dot_general(box[...], low, (NN, ((), ())), preferred_element_type=F32)
    mean = jnp.sum(sums, axis=1, keepdims=True) * (1.0 / (16 * NZ))
    soft = jnp.maximum(mean, 0.0) + jnp.log1p(jnp.exp(-jnp.abs(mean)))
    grown = radius_p + 0.5 * soft
    root = jnp.sqrt(grown)
    mass = grown * root
    gain = mass - radius_p * jnp.sqrt(radius_p)

    def other(values):
        return pltpu.roll(values, 64, 1)

    root_sum = root + other(root)
    rate = 0.05 * (root_sum * root_sum * jnp.abs(grown - other(grown)) * other(live_p))
    final = (mass + rate * other(mass)) / (1.0 + rate)
    lanes = lax.broadcasted_iota(jnp.int32, (32, 128), 1)
    own_live = jnp.where(lanes < 64, live_p, 0.0)
    cond[...] = jnp.broadcast_to(jnp.sum(own_live * gain, axis=1, keepdims=True), (32, 128)) * 0.002
    carried = [own_live, own_live * final, own_live * final * final]
    packed = jnp.zeros((32, 128), F32)
    for d in range(9):
        chosen = code_p == float(d)
        for k in range(3):
            amount = jnp.sum(jnp.where(chosen, carried[k], 0.0), axis=1, keepdims=True)
            packed = packed + jnp.where(lanes == d * 3 + k, amount, 0.0)
    load[...] = packed

    def share(source, target_ref, k, device):
        return pltpu.make_async_remote_copy(
            src_ref=source, dst_ref=target_ref, send_sem=ms_sem.at[k], recv_sem=mr_sem.at[k],
            device_id=device, device_id_type=MESH,
        )

    top, bottom = pl.ds(24, 8), pl.ds(0, 8)
    shares = [
        share(load.at[top], near.at[0, bottom], 0, (east, gy)),
        share(load.at[bottom], near.at[1, bottom], 1, (west, gy)),
        share(load, near.at[2], 2, (gx, north)),
        share(load, near.at[3], 3, (gx, south)),
        share(load.at[top], near.at[4, bottom], 4, (east, north)),
        share(load.at[top], near.at[5, bottom], 5, (east, south)),
        share(load.at[bottom], near.at[6, bottom], 6, (west, north)),
        share(load.at[bottom], near.at[7, bottom], 7, (west, south)),
    ]
    for copy in shares:
        copy.start()

    def dry(x, carry):
        first_box = (x // 4) * 8
        for t in range(4):
            drop = jnp.where(
                tile_row < 4,
                cond[pl.ds(first_box + 2 * t, 1), :],
                cond[pl.ds(first_box + 2 * t + 1, 1), :],
            )
            ad[4, x, 8 * t : 8 * t + 8, :] -= drop
        return carry

    lax.fori_loop(0, SX, dry, 0)

    for copy in fetches[2:]:
        copy.wait()
    drained(send1, got1, r1_sem)
    z_re, z_im = [], []
    for c in range(4):
        both = fold(one_product(first[c], packed_right(*halves(got1[c])), NN))
        z_re.append(both[:HALF])
        z_im.append(both[HALF:])

    def butterfly(re, im, sign):
        s02r, s02i = re[0] + re[2], im[0] + im[2]
        d02r, d02i = re[0] - re[2], im[0] - im[2]
        s13r, s13i = re[1] + re[3], im[1] + im[3]
        d13r, d13i = re[1] - re[3], im[1] - im[3]
        if sign < 0:
            return (
                [s02r + s13r, d02r + d13i, s02r - s13r, d02r - d13i],
                [s02i + s13i, d02i - d13r, s02i - s13i, d02i + d13r],
            )
        return (
            [s02r + s13r, d02r - d13i, s02r - s13r, d02r + d13i],
            [s02i + s13i, d02i + d13r, s02i - s13i, d02i - d13r],
        )

    q_re, q_im = butterfly(z_re, z_im, -1)
    re, im = jnp.concatenate(q_re, axis=0), jnp.concatenate(q_im, axis=0)
    turn_cos, turn_sin = turns[0], turns[1]
    joined = jnp.concatenate([re * turn_cos + im * turn_sin, im * turn_cos - re * turn_sin], axis=1)
    spectrum = product(halves(joined), (ahead[0], ahead[1]), NN)
    eigen = turns[2] + wave[pl.ds(me, 1), :]
    inverse = jnp.where(eigen == 0.0, 0.0, 1.0 / jnp.where(eigen == 0.0, 1.0, eigen))
    solved = spectrum * jnp.concatenate([inverse, inverse], axis=1)
    turned = product(halves(solved), (behind[0], behind[1]), NN)
    re, im = turned[:, :128], turned[:, 128:]
    back_re, back_im = re * turn_cos - im * turn_sin, im * turn_cos + re * turn_sin
    v_re, v_im = butterfly(
        [back_re[HALF * q : HALF * (q + 1)] for q in range(4)],
        [back_im[HALF * q : HALF * (q + 1)] for q in range(4)],
        1,
    )
    wide_lane = lax.broadcasted_iota(jnp.int32, (128, 128), 1)
    edge = None
    for c in range(4):
        stacked = jnp.concatenate([v_re[c], v_im[c]], axis=0)
        high, low = halves(stacked)
        wide = one_product(last[0, c], jnp.concatenate([high, low], axis=1), NN)
        plane = fold(wide) + one_product(last[1, c], high, NN)
        send2[c] = plane
        if c == 0:
            next_x = pltpu.roll(plane, 120, 0)
        picked = jnp.where((wide_lane & 31) == 0, plane, 0.0)
        picked = picked if c == 0 else pltpu.roll(picked, c, 1)
        edge = picked if edge is None else edge + picked
    row_b = lax.broadcasted_iota(jnp.int32, (128, 128), 0) & 7
    edge = jnp.where(row_b == 7, pltpu.roll(edge, 7, 0), pltpu.roll(edge, 127, 0))
    moved = pltpu.roll(edge, 36, 1)
    in_move = (wide_lane >= 36) & (wide_lane < 40)
    send2[4] = jnp.where(wide_lane < 32, next_x, jnp.where(in_move, moved, edge))

    scatter(send2, modes, s2_sem, r2_sem)
    modes[:, pl.ds(me, 1), :] = send2[:, pl.ds(me, 1), :]

    for copy in shares:
        copy.wait_recv()
    tile_lane = lax.broadcasted_iota(jnp.int32, (8, 128), 1)

    def column_of(x):
        if x < 0:
            return near[0, 0:8, :], near[4, 7:8, :], near[5, 0:1, :]
        if x > 3:
            return near[1, 0:8, :], near[6, 7:8, :], near[7, 0:1, :]
        return load[8 * x : 8 * x + 8, :], near[2, 8 * x + 7 : 8 * x + 8, :], near[3, 8 * x : 8 * x + 1, :]

    arrived = [jnp.zeros((8, 128), F32) for _ in range(4)]
    for x in range(-1, 5):
        centre, low_row, high_row = column_of(x)
        shifted = [
            jnp.where(tile_row == 7, high_row, pltpu.roll(centre, 7, 0)),
            centre,
            jnp.where(tile_row == 0, low_row, pltpu.roll(centre, 1, 0)),
        ]
        for dx in (-1, 0, 1):
            if not 0 <= x + dx < 4:
                continue
            for dy in (-1, 0, 1):
                d = (dx + 1) * 3 + dy + 1
                values = shifted[dy + 1]
                values = values if d == 0 else pltpu.roll(values, 128 - 3 * d, 1)
                arrived[x + dx] = arrived[x + dx] + values
    stacked = jnp.concatenate(arrived + [jnp.zeros((96, 128), F32)], axis=0) * (1.0 / 64)
    moments_out[...] = stacked.T[0:8, :]

    for copy in halo:
        copy.wait_send()
    for copy in shares:
        copy.wait_send()
    drained(send1, got1, s1_sem)
    drained(send2, send2, s2_sem)
    drained(send2, modes, r2_sem)


def final_kernel(
    modes, ad, moments, back,
    vel_out, theta_out, vapour_out, moments_out,
    fresh, mom_o, pressure, out_sem,
):
    mom_o[...] = moments[0:3, 0:32]
    outs = [
        pltpu.make_async_copy(ad.at[3], theta_out, out_sem.at[0]),
        pltpu.make_async_copy(ad.at[4], vapour_out, out_sem.at[1]),
        pltpu.make_async_copy(mom_o, moments_out, out_sem.at[2]),
    ]
    for copy in outs:
        copy.start()
    row = lax.broadcasted_iota(jnp.int32, (SY, NZ), 0)
    lane = lax.broadcasted_iota(jnp.int32, (SY, NZ), 1)

    def levels(c):
        wide = one_product(jnp.concatenate(halves(modes[c]), axis=0), back[...], TN)
        pressure[pl.ds(128 * c, 128), :] = fold(wide)

    levels(4)
    for c in (3, 2, 1, 0):
        levels(c)
        for i in range(4):
            x = 4 * c + i
            here = pressure[pl.ds(32 * x, 32), :]
            ahead = pressure[pl.ds(32 * x + 32, 32), :]
            line = 512 + (36, 32, 64, 96)[i] + c
            side = jnp.where(row == SY - 1, pressure[line : line + 1, :], pltpu.roll(here, SY - 1, 0))
            above = jnp.where(lane == NZ - 1, here, pltpu.roll(here, NZ - 1, 1))
            fresh[0, x] = ad[0, x] - (ahead - here)
            fresh[1, x] = ad[1, x] - (side - here)
            fresh[2, x] = ad[2, x] - (above - here)
        part = pl.ds(4 * c, 4)
        copy = pltpu.make_async_copy(fresh.at[:, part], vel_out.at[:, part], out_sem.at[3 + c])
        copy.start()
        outs.append(copy)
    for copy in outs:
        copy.wait()


def shards(velocity, theta, vapour, radius_sq, multiplicity, counts, pairing, destination):
    t = tables()
    names = ["cosine", "first", "ahead", "behind", "last", "turns", "wave_z", "box"]
    held = [jnp.asarray(t[name]) for name in names]
    block = (SX, SY, NZ)
    shape = jax.ShapeDtypeStruct
    vmem = pltpu.VMEM
    dma = pltpu.SemaphoreType.DMA
    here = pl.BlockSpec(memory_space=pltpu.VMEM)
    modes, advected, moments = pl.pallas_call(
        step_kernel,
        out_shape=(
            vmem((5, DEV, 128), F32),
            vmem((5,) + block, F32),
            vmem((8, 128), F32),
        ),
        in_specs=[ANY] * 16,
        out_specs=(here,) * 3,
        scratch_shapes=[
            vmem((5, SX + 2, SY, NZ), F32),
            vmem((SY, NZ), F32),
            vmem((SY, NZ), F32),
            vmem((6, SX, NZ), F32),
            vmem((5, SX, NZ), F32),
            vmem((4, 8, NZ), F32),
            vmem((SX, NZ), F32),
            vmem((SX, NZ), F32),
            vmem((4, SY, NZ), F32),
            vmem((4, DEV, 128), F32),
            vmem((4, DEV, 128), F32),
            vmem((5, DEV, 128), F32),
        ]
        + [vmem(t[name].shape, t[name].dtype) for name in names]
        + [
            vmem((32, 64), F32),
            vmem((32, 64), F32),
            vmem((32,), jnp.int32),
            vmem((32, 64), jnp.int32),
            vmem((32, 64), jnp.int32),
            vmem((32, 128), F32),
            vmem((32, 128), F32),
            vmem((8, 32, 128), F32),
            pltpu.SemaphoreType.REGULAR((1,)),
            dma((3,)),
            dma((5,)),
            dma((8,)),
            dma((18,)),
            dma((18,)),
            dma(()),
            dma(()),
            dma(()),
            dma(()),
            dma((8,)),
            dma((8,)),
        ],
        compiler_params=pltpu.CompilerParams(
            has_side_effects=True, collective_id=1, vmem_limit_bytes=24 << 20
        ),
        name="cloud_step",
    )(*[
        pltpu.with_memory_space_constraint(value, pltpu.HBM)
        for value in (
            velocity, theta, vapour, radius_sq.T, multiplicity.T, counts, pairing, destination.T, *held
        )
    ])
    return pl.pallas_call(
        final_kernel,
        out_shape=(
            shape((3,) + block, F32),
            shape(block, F32),
            shape(block, F32),
            shape((3, 32), F32),
        ),
        in_specs=[here] * 4,
        out_specs=(ANY,) * 4,
        scratch_shapes=[
            vmem((3,) + block, F32),
            vmem((3, 32), F32),
            vmem((640, 128), F32),
            dma((7,)),
        ],
        compiler_params=pltpu.CompilerParams(vmem_limit_bytes=12 << 20),
        name="project",
    )(
        *[pltpu.with_memory_space_constraint(value, pltpu.VMEM) for value in (modes, advected, moments)],
        jnp.asarray(t["back"]),
    )


def solution(mesh):
    placed = (
        P(None, "gx", "gy", None),
        P("gx", "gy", None),
        P("gx", "gy", None),
        P(None, ("gx", "gy")),
        P(None, ("gx", "gy")),
        P(("gx", "gy")),
        P(("gx", "gy"), None),
        P(None, ("gx", "gy")),
    )
    return jax.shard_map(
        shards,
        mesh=mesh,
        in_specs=placed,
        out_specs=(
            P(None, "gx", "gy", None),
            P("gx", "gy", None),
            P("gx", "gy", None),
            P(None, ("gx", "gy")),
        ),
        check_vma=False,
    )
```

```python
import functools
import math

import jax
import jax.numpy as jnp
import numpy as np
from jax import lax
from jax.experimental import pallas as pl
from jax.experimental.pallas import tpu as pltpu
from jax.sharding import PartitionSpec as P

MESH = pl.DeviceIdType.MESH
GX, GY = 16, 8
DEV = GX * GY
SX, SY, NZ = 16, 32, 128
NX, NY = 256, 256
HALF = 72
F32 = jnp.float32
BF16 = jnp.bfloat16
ANY = pl.BlockSpec(memory_space=pl.ANY)


def split_table(table):
    table = np.asarray(table, np.float32)
    high = table.astype(jnp.bfloat16)
    low = (table - high.astype(np.float32)).astype(jnp.bfloat16)
    return np.stack([high, low])


@functools.cache
def send_order():
    hops = (0, 1, 2, 1)
    ways = ((0, 0), (1, 0), (1, 1), (0, 1))
    left = [(k, i, j, n) for k in range(4) for i in range(4) for j in range(4) for n in range(2)][1:]
    used, order = [0] * 6, []

    def after(peer):
        return [u + w for u, w in zip(used, sum((ways[step] for step in peer[:3]), ()))]

    while left:
        far = max(sum(hops[step] for step in peer[:3]) for peer in left)
        ring = [peer for peer in left if sum(hops[step] for step in peer[:3]) == far]
        best = min(ring, key=lambda peer: (max(after(peer)), sum(u * u for u in after(peer))))
        used = after(best)
        order.append(best)
        left.remove(best)
    return tuple(order)


@functools.cache
def tables():
    tau = 2.0 * math.pi
    z = np.arange(NZ)
    cosine = np.cos(math.pi * (z[None, :] + 0.5) * z[:, None] / NZ)
    weight = np.where(z == 0, 1.0 / NZ, 2.0 / NZ)
    back = cosine * weight[:, None]
    rows, factor, seen = [], [], set()
    for p in range(16):
        for q in range(8):
            if (p, q) in seen:
                continue
            mirror = (-p % 16, -q % 8)
            seen.update({(p, q), mirror})
            rows.append((p, q))
            factor.append(1.0 if mirror == (p, q) else 2.0)
    pad = HALF - len(rows)
    low_x = np.array([r[0] for r in rows] + [0] * pad)
    low_y = np.array([r[1] for r in rows] + [0] * pad)
    factor = np.array(factor + [0.0] * pad)
    used = np.array([1.0] * len(rows) + [0.0] * pad)
    a = np.repeat(np.arange(16), 8)
    b = np.tile(np.arange(8), 16)
    first, last = [], []
    for c in range(4):
        angle = tau * (
            low_x[:, None] * a[None] / 16.0
            + low_y[:, None] * b[None] / 8.0
            + low_x[:, None] * c / 64.0
        )
        first.append(np.concatenate([np.cos(angle) * used[:, None], -np.sin(angle) * used[:, None]]))
        scale = factor[:, None] / (NX * NY)
        last.append(np.concatenate([np.cos(angle) * scale, -np.sin(angle) * scale]).T)
    lane_i = np.repeat(np.arange(4), 32)
    lane_j = np.tile(np.arange(32), 4)
    turn_cos, turn_sin, wave = [], [], []
    for q in range(4):
        kx0 = low_x + 16 * q
        angle = tau * (kx0[:, None] * lane_i[None] + low_y[:, None] * lane_j[None]) / 256.0
        turn_cos.append(np.cos(angle))
        turn_sin.append(np.sin(angle))
        kx = kx0[:, None] + 64 * lane_i[None]
        ky = low_y[:, None] + 8 * lane_j[None]
        wave.append(-4.0 * np.sin(math.pi * kx / NX) ** 2 - 4.0 * np.sin(math.pi * ky / NY) ** 2)
    turns = np.stack([np.concatenate(turn_cos), np.concatenate(turn_sin), np.concatenate(wave)])
    angle = tau * (lane_i[:, None] * lane_i[None] / 4.0 + lane_j[:, None] * lane_j[None] / 32.0)
    cos2, sin2 = np.cos(angle), np.sin(angle)
    ahead = np.block([[cos2, -sin2], [sin2, cos2]])
    behind = np.block([[cos2, sin2], [-sin2, cos2]])
    wave_z = -4.0 * np.sin(math.pi * z / (2.0 * NZ)) ** 2
    wave_z = np.broadcast_to(wave_z[:, None], (NZ, 128)).astype(np.float32)
    box = np.zeros((32, 128), np.float32)
    for column in range(4):
        for j in range(32):
            box[column * 8 + j // 4, column * 32 + j] = 1.0
    return dict(
        cosine=packed_left(cosine),
        first=packed_left(np.stack(first)),
        ahead=split_table(ahead),
        behind=split_table(behind),
        last=np.concatenate(list(split_table(np.stack(last))), axis=1),
        turns=turns.astype(np.float32),
        wave_z=wave_z,
        box=box.astype(jnp.bfloat16),
        back=np.block([[*split_table(back)], [split_table(back)[0], np.zeros((NZ, NZ), jnp.bfloat16)]]),
    )


def halves(values):
    high = values.astype(BF16)
    return high, (values - high.astype(F32)).astype(BF16)


def product(left, right, dims):
    def one(x, y):
        return lax.dot_general(x, y, (dims, ((), ())), preferred_element_type=F32)

    (left_high, left_low), (right_high, right_low) = left, right
    return one(left_high, right_high) + (one(left_high, right_low) + one(left_low, right_high))


def packed_left(table):
    high, low = split_table(table)
    return np.concatenate([high, low], axis=-1)


def fold(wide):
    return wide[:, :128] + wide[:, 128:]


def packed_right(high, low):
    zero = jnp.zeros_like(low)
    return jnp.concatenate(
        [jnp.concatenate([high, low], axis=1), jnp.concatenate([high, zero], axis=1)], axis=0
    )


def one_product(left, right, dims):
    return lax.dot_general(left, right, (dims, ((), ())), preferred_element_type=F32)


NN = ((1,), (0,))
NT = ((1,), (1,))
TN = ((0,), (0,))


def step_kernel(
    vel, theta, vapour, radius, multi, counts, pairing, dest,
    cosine_h, first_h, ahead_h, behind_h, last_h, turns_h, wave_h, box_h,
    modes, ad, moments_out,
    fp, before_u, xu2, yl, yh, corner, row_y0, below_y, quad, send1, got1, send2,
    cosine, first, ahead, behind, last, turns, wave, box,
    rad_v, mul_v, cnt_v, pair_v, dst_v, cond, load, near,
    known, load_sem, drop_sem, table_sem, hs_sem, hr_sem, s1_sem, r1_sem, s2_sem, r2_sem,
    ms_sem, mr_sem,
):
    gx = lax.axis_index("gx")
    gy = lax.axis_index("gy")
    me = gx * GY + gy
    east, west = lax.rem(gx + 1, GX), lax.rem(gx + GX - 1, GX)
    north, south = lax.rem(gy + 1, GY), lax.rem(gy + GY - 1, GY)

    loads = [
        pltpu.make_async_copy(vel, fp.at[pl.ds(0, 3), pl.ds(1, SX)], load_sem.at[0]),
        pltpu.make_async_copy(theta, fp.at[3, pl.ds(1, SX)], load_sem.at[1]),
        pltpu.make_async_copy(vapour, fp.at[4, pl.ds(1, SX)], load_sem.at[2]),
    ]
    drops = [
        pltpu.make_async_copy(source, target, drop_sem.at[k])
        for k, (source, target) in enumerate(
            [(radius, rad_v), (multi, mul_v), (counts, cnt_v), (pairing, pair_v), (dest, dst_v)]
        )
    ]
    table_pairs = [
        (cosine_h, cosine), (box_h, box), (first_h, first), (turns_h, turns), (ahead_h, ahead),
        (wave_h, wave), (behind_h, behind), (last_h, last),
    ]
    fetches = [
        pltpu.make_async_copy(source, target, table_sem.at[k])
        for k, (source, target) in enumerate(table_pairs)
    ]
    for copy in loads + drops + fetches:
        copy.start()

    barrier = pltpu.get_barrier_semaphore()

    chip_z, chip_x, chip_y, core = gx // 4, lax.rem(gx, 4), gy // 2, lax.rem(gy, 2)

    peers_x = [[lax.rem(chip_z + k, 4) * 4 + lax.rem(chip_x + i, 4) for i in range(4)] for k in range(4)]
    peers_y = [[lax.rem(chip_y + j, 4) * 2 + lax.rem(core + n, 2) for n in range(2)] for j in range(4)]

    def away(step_z, step_x, step_y, step_core):
        return peers_x[step_z % 4][step_x % 4], peers_y[step_y % 4][step_core]

    steps = [(k, i, j, n) for k in (0, 1, -1) for i in (1, -1, 0) for j in (1, -1, 0) for n in (0, 1)]
    steps.sort(key=lambda step: -sum(map(abs, step[:3])))
    around = [away(*step) for step in steps if any(step)]
    corners = [away(k, i, j, 0) for k in (1, -1) for i in (1, -1) for j in (1, -1)]
    for device in around:
        pl.semaphore_signal(barrier, inc=1, device_id=device, device_id_type=MESH)
    pl.semaphore_wait(barrier, len(around))

    def remote(source, target_ref, k, device):
        return pltpu.make_async_remote_copy(
            src_ref=source, dst_ref=target_ref, send_sem=hs_sem.at[k], recv_sem=hr_sem.at[k],
            device_id=device, device_id_type=MESH,
        )

    winds = fp.at[pl.ds(0, 3)]
    wind = [
        remote(winds.at[:, SX], fp.at[pl.ds(0, 3), 0], 0, (east, gy)),
        remote(winds.at[:, 1], fp.at[pl.ds(0, 3), SX + 1], 1, (west, gy)),
        remote(fp.at[0, SX - 1], xu2, 2, (east, gy)),
        remote(winds.at[:, pl.ds(1, SX), SY - 1], yl.at[pl.ds(0, 3)], 3, (gx, north)),
        remote(winds.at[:, pl.ds(1, SX), 0], yh.at[pl.ds(0, 3)], 4, (gx, south)),
        remote(fp.at[1, pl.ds(1, SX), SY - 2], yl.at[5], 5, (gx, north)),
        remote(fp.at[0, SX, pl.ds(SY - 1, 1)], corner.at[0, pl.ds(0, 1)], 6, (east, north)),
        remote(fp.at[0, SX, pl.ds(0, 1)], corner.at[1, pl.ds(0, 1)], 7, (east, south)),
        remote(fp.at[1, SX, pl.ds(SY - 1, 1)], corner.at[2, pl.ds(0, 1)], 8, (east, north)),
        remote(fp.at[1, 1, pl.ds(SY - 1, 1)], corner.at[3, pl.ds(0, 1)], 9, (west, north)),
    ]
    air = [
        remote(fp.at[3, SX], fp.at[3, 0], 10, (east, gy)),
        remote(fp.at[4, SX], fp.at[4, 0], 11, (east, gy)),
        remote(fp.at[3, 1], fp.at[3, SX + 1], 12, (west, gy)),
        remote(fp.at[4, 1], fp.at[4, SX + 1], 13, (west, gy)),
        remote(fp.at[3, pl.ds(1, SX), SY - 1], yl.at[3], 14, (gx, north)),
        remote(fp.at[4, pl.ds(1, SX), SY - 1], yl.at[4], 15, (gx, north)),
        remote(fp.at[3, pl.ds(1, SX), 0], yh.at[3], 16, (gx, south)),
        remote(fp.at[4, pl.ds(1, SX), 0], yh.at[4], 17, (gx, south)),
    ]
    halo = wind + air
    loads[0].wait()
    for copy in wind[6:] + wind[:6]:
        copy.start()

    def pass_on(k, devices):
        for device in devices:
            pl.semaphore_signal(known.at[k], inc=1, device_id=device, device_id_type=MESH)

    pass_on(0, corners)
    for copy in loads[1:]:
        copy.wait()

    row = lax.broadcasted_iota(jnp.int32, (SY, NZ), 0)
    lane = lax.broadcasted_iota(jnp.int32, (SY, NZ), 1)
    tile_row = lax.broadcasted_iota(jnp.int32, (8, NZ), 0)

    def upward(values):
        return pltpu.roll(values, NZ - 1, 1)

    def downward(values):
        return pltpu.roll(values, 1, 1)

    def coefficients(speed, shape_lane=None):
        scaled = 0.1 * speed
        return 0.01 - scaled, 0.01 + scaled

    def vertical(speed, lanes):
        up, down = coefficients(speed)
        top, bottom = lanes == NZ - 1, lanes == 0
        centre = 0.94 + jnp.where(top, up, 0.0) + jnp.where(bottom, down, 0.0)
        return jnp.where(top, 0.0, up), jnp.where(bottom, 0.0, down), centre

    def advect_plane(x, fields):
        c_east, c_west = coefficients(fp[0, x + 1])
        c_north, c_south = coefficients(fp[1, x + 1])
        c_north = jnp.where(row == SY - 1, 0.0, c_north)
        c_south = jnp.where(row == 0, 0.0, c_south)
        c_up, c_down, c_mid = vertical(fp[2, x + 1], lane)
        for f in fields:
            centre = fp[f, x + 1]
            ad[f, x] = (
                (c_mid * centre + c_east * fp[f, x + 2] + c_west * fp[f, x])
                + (c_north * pltpu.roll(centre, SY - 1, 0) + c_south * pltpu.roll(centre, 1, 0))
                + (c_up * upward(centre) + c_down * downward(centre))
            )

    def inner(x, carry):
        advect_plane(x, (0, 1, 2))
        row_y0[pl.ds(x, 1), :] = fp[1, x + 1, 0:1, :]
        return carry

    lax.fori_loop(1, SX - 1, inner, 0)
    for copy in air:
        copy.start()

    for copy in drops:
        copy.wait()
    box_row = lax.broadcasted_iota(jnp.int32, (32, 32), 0)
    box_lane = lax.broadcasted_iota(jnp.int32, (32, 32), 1)
    spread = jnp.where(box_row == box_lane, cnt_v[...][None, :].astype(F32), 0.0)
    used = jnp.sum(spread, axis=1, keepdims=True)
    slot = lax.broadcasted_iota(jnp.int32, (32, 64), 1).astype(F32)
    live = jnp.where(slot < used, mul_v[...], 0.0)
    target = dst_v[...]
    local_box = lax.broadcasted_iota(jnp.int32, (32, 64), 0)
    source_x = gx * 4 + (local_box >> 3)
    source_y = gy * 8 + (local_box & 7)
    target_x = (target >> 8) * 4 + ((target & 31) >> 3)
    target_y = ((target >> 5) & 7) * 8 + (target & 7)
    offset_x = (target_x - source_x + 1) & 63
    offset_y = (target_y - source_y + 1) & 63
    code = (offset_x * 3 + offset_y).astype(F32)

    def twice(values):
        return jnp.concatenate([values, values], axis=1)

    pair = twice(pair_v[...])
    order = jnp.where(lax.broadcasted_iota(jnp.int32, (32, 128), 1) < 64, pair, pltpu.roll(pair, 32, 1))
    radius_p = jnp.take_along_axis(twice(rad_v[...]), order, axis=1)
    live_p = jnp.take_along_axis(twice(live), order, axis=1)
    code_p = jnp.take_along_axis(twice(code), order, axis=1)

    for x in (0, SX - 1):
        row_y0[pl.ds(x, 1), :] = fp[1, x + 1, 0:1, :]
    for copy in wind[3:6]:
        copy.wait_recv()

    speed_v = yl[1]
    row_x = lax.broadcasted_iota(jnp.int32, (SX, NZ), 0)
    lane_x = lax.broadcasted_iota(jnp.int32, (SX, NZ), 1)
    c_east, c_west = coefficients(yl[0])
    c_north, c_south = coefficients(speed_v)
    c_up, c_down, c_mid = vertical(yl[2], lane_x)
    after = jnp.where(row_x == SX - 1, 0.0, pltpu.roll(speed_v, SX - 1, 0))
    before = jnp.where(row_x == 0, 0.0, pltpu.roll(speed_v, 1, 0))
    below_y[...] = (
        (c_mid * speed_v + c_east * after + c_west * before)
        + (c_north * row_y0[...] + c_south * yl[5])
        + (c_up * upward(speed_v) + c_down * downward(speed_v))
    )
    fetches[0].wait()

    def border(x, fields):
        _, c_south = coefficients(fp[1, x + 1, 0:8, :])
        c_north, _ = coefficients(fp[1, x + 1, SY - 8 : SY, :])
        c_south = jnp.where(tile_row == 0, c_south, 0.0)
        c_north = jnp.where(tile_row == 7, c_north, 0.0)
        for f in fields:
            ad[f, x, 0:8, :] += c_south * yl[f, pl.ds(x, 1), :]
            ad[f, x, SY - 8 : SY, :] += c_north * yh[f, pl.ds(x, 1), :]

    def block(c):
        parts = []
        for i in range(4):
            x = c * 4 + i
            if x != 3:
                border(x, (0, 1, 2))
            star_w = ad[2, x] + 0.1 * fp[3, x + 1]
            ad[2, x] = star_w
            star_v = ad[1, x]
            star_u = ad[0, x]
            if i == 0:
                last_u = before_u[...] if c == 0 else ad[0, x - 1]
            behind_v = jnp.where(row == 0, below_y[pl.ds(x, 1), :], pltpu.roll(star_v, 1, 0))
            below_w = jnp.where(lane == 0, 0.0, downward(star_w))
            parts.append((star_u - last_u) + (star_v - behind_v) + (star_w - below_w))
            last_u = star_u
        chunk = jnp.concatenate(parts, axis=0)
        high, low = halves(chunk)
        wide = jnp.concatenate(
            [jnp.concatenate([high, high], axis=1), jnp.concatenate([low, jnp.zeros_like(low)], axis=1)],
            axis=0,
        )
        send1[c] = fold(one_product(cosine[...], wide, NT))

    def scalars(c, carry):
        total = jnp.zeros((SY, NZ), F32)
        for i in range(4):
            x = c * 4 + i
            advect_plane(x, (3, 4))
            border(x, (3, 4))
            total = total + ad[4, x]
        quad[c] = total
        return carry

    border(3, (0, 1, 2))
    block(1)
    block(2)
    for copy in wind[:3]:
        copy.wait_recv()
    advect_plane(0, (0, 1, 2))
    advect_plane(SX - 1, (0, 1, 2))

    for copy in wind[6:]:
        copy.wait_recv()
    _, end_west = coefficients(yl[0, 0:1, :])
    end_east, _ = coefficients(yl[0, SX - 1 : SX, :])
    below_y[0:1, :] += end_west * corner[2, 0:1, :]
    below_y[SX - 1 : SX, :] += end_east * corner[3, 0:1, :]

    speed = fp[0, 0]
    c_east, c_west = coefficients(speed)
    c_north, c_south = coefficients(fp[1, 0])
    c_up, c_down, c_mid = vertical(fp[2, 0], lane)
    above = jnp.where(row == SY - 1, corner[1, 0:1, :], pltpu.roll(speed, SY - 1, 0))
    beneath = jnp.where(row == 0, corner[0, 0:1, :], pltpu.roll(speed, 1, 0))
    before_u[...] = (
        (c_mid * speed + c_east * fp[0, 1] + c_west * xu2[...])
        + (c_north * above + c_south * beneath)
        + (c_up * upward(speed) + c_down * downward(speed))
    )
    block(0)
    block(3)
    pl.semaphore_wait(known.at[0], len(corners))

    def scatter(source, target_ref, send_sem, recv_sem):
        for step_z, step_x, step_y, step_core in send_order():
            px, py = peers_x[step_z][step_x], peers_y[step_y][step_core]
            pltpu.make_async_remote_copy(
                src_ref=source.at[:, pl.ds(px * GY + py, 1), :],
                dst_ref=target_ref.at[:, pl.ds(me, 1), :],
                send_sem=send_sem, recv_sem=recv_sem, device_id=(px, py), device_id_type=MESH,
            ).start()

    def drained(source, target_ref, sem):
        count = pl.ds(0, DEV - 1)
        pltpu.make_async_copy(source.at[:, count, :], target_ref.at[:, count, :], sem).wait()

    scatter(send1, got1, s1_sem, r1_sem)
    got1[:, pl.ds(me, 1), :] = send1[:, pl.ds(me, 1), :]

    for copy in air:
        copy.wait_recv()
    lax.fori_loop(0, 4, scalars, 0)
    fetches[1].wait()
    high, low = halves(quad[...].reshape(128, NZ))
    sums = lax.dot_general(box[...], high, (NN, ((), ())), preferred_element_type=F32)
    sums = sums + lax.dot_general(box[...], low, (NN, ((), ())), preferred_element_type=F32)
    mean = jnp.sum(sums, axis=1, keepdims=True) * (1.0 / (16 * NZ))
    soft = jnp.maximum(mean, 0.0) + jnp.log1p(jnp.exp(-jnp.abs(mean)))
    grown = radius_p + 0.5 * soft
    root = jnp.sqrt(grown)
    mass = grown * root
    gain = mass - radius_p * jnp.sqrt(radius_p)

    def other(values):
        return pltpu.roll(values, 64, 1)

    root_sum = root + other(root)
    rate = 0.05 * (root_sum * root_sum * jnp.abs(grown - other(grown)) * other(live_p))
    final = (mass + rate * other(mass)) / (1.0 + rate)
    lanes = lax.broadcasted_iota(jnp.int32, (32, 128), 1)
    own_live = jnp.where(lanes < 64, live_p, 0.0)
    cond[...] = jnp.broadcast_to(jnp.sum(own_live * gain, axis=1, keepdims=True), (32, 128)) * 0.002
    carried = [own_live, own_live * final, own_live * final * final]
    packed = jnp.zeros((32, 128), F32)
    for d in range(9):
        chosen = code_p == float(d)
        for k in range(3):
            amount = jnp.sum(jnp.where(chosen, carried[k], 0.0), axis=1, keepdims=True)
            packed = packed + jnp.where(lanes == d * 3 + k, amount, 0.0)
    load[...] = packed

    def share(source, target_ref, k, device):
        return pltpu.make_async_remote_copy(
            src_ref=source, dst_ref=target_ref, send_sem=ms_sem.at[k], recv_sem=mr_sem.at[k],
            device_id=device, device_id_type=MESH,
        )

    top, bottom = pl.ds(24, 8), pl.ds(0, 8)
    shares = [
        share(load.at[top], near.at[0, bottom], 0, (east, gy)),
        share(load.at[bottom], near.at[1, bottom], 1, (west, gy)),
        share(load, near.at[2], 2, (gx, north)),
        share(load, near.at[3], 3, (gx, south)),
        share(load.at[top], near.at[4, bottom], 4, (east, north)),
        share(load.at[top], near.at[5, bottom], 5, (east, south)),
        share(load.at[bottom], near.at[6, bottom], 6, (west, north)),
        share(load.at[bottom], near.at[7, bottom], 7, (west, south)),
    ]
    for copy in shares:
        copy.start()

    def dry(x, carry):
        first_box = (x // 4) * 8
        for t in range(4):
            drop = jnp.where(
                tile_row < 4,
                cond[pl.ds(first_box + 2 * t, 1), :],
                cond[pl.ds(first_box + 2 * t + 1, 1), :],
            )
            ad[4, x, 8 * t : 8 * t + 8, :] -= drop
        return carry

    lax.fori_loop(0, SX, dry, 0)

    for copy in fetches[2:]:
        copy.wait()
    drained(send1, got1, r1_sem)
    z_re, z_im = [], []
    for c in range(4):
        both = fold(one_product(first[c], packed_right(*halves(got1[c])), NN))
        z_re.append(both[:HALF])
        z_im.append(both[HALF:])

    def butterfly(re, im, sign):
        s02r, s02i = re[0] + re[2], im[0] + im[2]
        d02r, d02i = re[0] - re[2], im[0] - im[2]
        s13r, s13i = re[1] + re[3], im[1] + im[3]
        d13r, d13i = re[1] - re[3], im[1] - im[3]
        if sign < 0:
            return (
                [s02r + s13r, d02r + d13i, s02r - s13r, d02r - d13i],
                [s02i + s13i, d02i - d13r, s02i - s13i, d02i + d13r],
            )
        return (
            [s02r + s13r, d02r - d13i, s02r - s13r, d02r + d13i],
            [s02i + s13i, d02i + d13r, s02i - s13i, d02i - d13r],
        )

    def stacked_product(values, table):
        high, low = halves(values)
        both = one_product(jnp.concatenate([high, low], axis=0), table[0], NN)
        rows = values.shape[0]
        return both[:rows] + (both[rows:] + one_product(high, table[1], NN))

    q_re, q_im = butterfly(z_re, z_im, -1)
    back_re, back_im = [], []
    for q in range(0, 4, 2):
        part = pl.ds(HALF * q, HALF * 2)
        re, im = (jnp.concatenate(side[q : q + 2], axis=0) for side in (q_re, q_im))
        turn_cos, turn_sin = turns[0, part, :], turns[1, part, :]
        joined = jnp.concatenate([re * turn_cos + im * turn_sin, im * turn_cos - re * turn_sin], axis=1)
        spectrum = stacked_product(joined, ahead)
        eigen = turns[2, part, :] + wave[pl.ds(me, 1), :]
        inverse = jnp.where(eigen == 0.0, 0.0, 1.0 / jnp.where(eigen == 0.0, 1.0, eigen))
        turned = stacked_product(spectrum * jnp.concatenate([inverse, inverse], axis=1), behind)
        re, im = turned[:, :128], turned[:, 128:]
        turned_re, turned_im = re * turn_cos - im * turn_sin, im * turn_cos + re * turn_sin
        for k in range(2):
            back_re.append(turned_re[HALF * k : HALF * (k + 1)])
            back_im.append(turned_im[HALF * k : HALF * (k + 1)])
    v_re, v_im = butterfly(back_re, back_im, 1)
    wide_lane = lax.broadcasted_iota(jnp.int32, (128, 128), 1)
    edge = None
    for c in range(4):
        stacked = jnp.concatenate([v_re[c], v_im[c]], axis=0)
        high, low = halves(stacked)
        wide = one_product(last[c], jnp.concatenate([high, low], axis=1), NN)
        plane = wide[:128, :128] + (wide[:128, 128:] + wide[128:, :128])
        send2[c] = plane
        if c == 0:
            next_x = pltpu.roll(plane, 120, 0)
        picked = jnp.where((wide_lane & 31) == 0, plane, 0.0)
        picked = picked if c == 0 else pltpu.roll(picked, c, 1)
        edge = picked if edge is None else edge + picked
    row_b = lax.broadcasted_iota(jnp.int32, (128, 128), 0) & 7
    edge = jnp.where(row_b == 7, pltpu.roll(edge, 7, 0), pltpu.roll(edge, 127, 0))
    moved = pltpu.roll(edge, 36, 1)
    in_move = (wide_lane >= 36) & (wide_lane < 40)
    send2[4] = jnp.where(wide_lane < 32, next_x, jnp.where(in_move, moved, edge))

    scatter(send2, modes, s2_sem, r2_sem)
    modes[:, pl.ds(me, 1), :] = send2[:, pl.ds(me, 1), :]

    for copy in shares:
        copy.wait_recv()
    tile_lane = lax.broadcasted_iota(jnp.int32, (8, 128), 1)

    def column_of(x):
        if x < 0:
            return near[0, 0:8, :], near[4, 7:8, :], near[5, 0:1, :]
        if x > 3:
            return near[1, 0:8, :], near[6, 7:8, :], near[7, 0:1, :]
        return load[8 * x : 8 * x + 8, :], near[2, 8 * x + 7 : 8 * x + 8, :], near[3, 8 * x : 8 * x + 1, :]

    arrived = [jnp.zeros((8, 128), F32) for _ in range(4)]
    for x in range(-1, 5):
        centre, low_row, high_row = column_of(x)
        shifted = [
            jnp.where(tile_row == 7, high_row, pltpu.roll(centre, 7, 0)),
            centre,
            jnp.where(tile_row == 0, low_row, pltpu.roll(centre, 1, 0)),
        ]
        for dx in (-1, 0, 1):
            if not 0 <= x + dx < 4:
                continue
            for dy in (-1, 0, 1):
                d = (dx + 1) * 3 + dy + 1
                values = shifted[dy + 1]
                values = values if d == 0 else pltpu.roll(values, 128 - 3 * d, 1)
                arrived[x + dx] = arrived[x + dx] + values
    stacked = jnp.concatenate(arrived + [jnp.zeros((96, 128), F32)], axis=0) * (1.0 / 64)
    moments_out[...] = stacked.T[0:8, :]

    for copy in halo:
        copy.wait_send()
    for copy in shares:
        copy.wait_send()
    drained(send1, got1, s1_sem)
    drained(send2, send2, s2_sem)
    drained(send2, modes, r2_sem)


def final_kernel(
    modes, ad, moments, back,
    vel_out, theta_out, vapour_out, moments_out,
    fresh, mom_o, pressure, out_sem,
):
    mom_o[...] = moments[0:3, 0:32]
    outs = [
        pltpu.make_async_copy(ad.at[3], theta_out, out_sem.at[0]),
        pltpu.make_async_copy(ad.at[4], vapour_out, out_sem.at[1]),
        pltpu.make_async_copy(mom_o, moments_out, out_sem.at[2]),
    ]
    for copy in outs:
        copy.start()
    row = lax.broadcasted_iota(jnp.int32, (SY, NZ), 0)
    lane = lax.broadcasted_iota(jnp.int32, (SY, NZ), 1)

    def levels(c):
        wide = one_product(jnp.concatenate(halves(modes[c]), axis=0), back[...], TN)
        pressure[pl.ds(128 * c, 128), :] = fold(wide)

    levels(4)
    for c in (3, 2, 1, 0):
        levels(c)
        for i in range(4):
            x = 4 * c + i
            here = pressure[pl.ds(32 * x, 32), :]
            ahead = pressure[pl.ds(32 * x + 32, 32), :]
            line = 512 + (36, 32, 64, 96)[i] + c
            side = jnp.where(row == SY - 1, pressure[line : line + 1, :], pltpu.roll(here, SY - 1, 0))
            above = jnp.where(lane == NZ - 1, here, pltpu.roll(here, NZ - 1, 1))
            fresh[0, x] = ad[0, x] - (ahead - here)
            fresh[1, x] = ad[1, x] - (side - here)
            fresh[2, x] = ad[2, x] - (above - here)
        part = pl.ds(4 * c, 4)
        copy = pltpu.make_async_copy(fresh.at[:, part], vel_out.at[:, part], out_sem.at[3 + c])
        copy.start()
        outs.append(copy)
    for copy in outs:
        copy.wait()


def shards(velocity, theta, vapour, radius_sq, multiplicity, counts, pairing, destination):
    t = tables()
    names = ["cosine", "first", "ahead", "behind", "last", "turns", "wave_z", "box"]
    held = [jnp.asarray(t[name]) for name in names]
    block = (SX, SY, NZ)
    shape = jax.ShapeDtypeStruct
    vmem = pltpu.VMEM
    dma = pltpu.SemaphoreType.DMA
    here = pl.BlockSpec(memory_space=pltpu.VMEM)
    modes, advected, moments = pl.pallas_call(
        step_kernel,
        out_shape=(
            vmem((5, DEV, 128), F32),
            vmem((5,) + block, F32),
            vmem((8, 128), F32),
        ),
        in_specs=[ANY] * 16,
        out_specs=(here,) * 3,
        scratch_shapes=[
            vmem((5, SX + 2, SY, NZ), F32),
            vmem((SY, NZ), F32),
            vmem((SY, NZ), F32),
            vmem((6, SX, NZ), F32),
            vmem((5, SX, NZ), F32),
            vmem((4, 8, NZ), F32),
            vmem((SX, NZ), F32),
            vmem((SX, NZ), F32),
            vmem((4, SY, NZ), F32),
            vmem((4, DEV, 128), F32),
            vmem((4, DEV, 128), F32),
            vmem((5, DEV, 128), F32),
        ]
        + [vmem(t[name].shape, t[name].dtype) for name in names]
        + [
            vmem((32, 64), F32),
            vmem((32, 64), F32),
            vmem((32,), jnp.int32),
            vmem((32, 64), jnp.int32),
            vmem((32, 64), jnp.int32),
            vmem((32, 128), F32),
            vmem((32, 128), F32),
            vmem((8, 32, 128), F32),
            pltpu.SemaphoreType.REGULAR((1,)),
            dma((3,)),
            dma((5,)),
            dma((8,)),
            dma((18,)),
            dma((18,)),
            dma(()),
            dma(()),
            dma(()),
            dma(()),
            dma((8,)),
            dma((8,)),
        ],
        compiler_params=pltpu.CompilerParams(
            has_side_effects=True, collective_id=1, vmem_limit_bytes=24 << 20
        ),
        name="cloud_step",
    )(*[
        pltpu.with_memory_space_constraint(value, pltpu.HBM)
        for value in (
            velocity, theta, vapour, radius_sq.T, multiplicity.T, counts, pairing, destination.T, *held
        )
    ])
    return pl.pallas_call(
        final_kernel,
        out_shape=(
            shape((3,) + block, F32),
            shape(block, F32),
            shape(block, F32),
            shape((3, 32), F32),
        ),
        in_specs=[here] * 4,
        out_specs=(ANY,) * 4,
        scratch_shapes=[
            vmem((3,) + block, F32),
            vmem((3, 32), F32),
            vmem((640, 128), F32),
            dma((7,)),
        ],
        compiler_params=pltpu.CompilerParams(vmem_limit_bytes=12 << 20),
        name="project",
    )(
        *[pltpu.with_memory_space_constraint(value, pltpu.VMEM) for value in (modes, advected, moments)],
        jnp.asarray(t["back"]),
    )


def solution(mesh):
    placed = (
        P(None, "gx", "gy", None),
        P("gx", "gy", None),
        P("gx", "gy", None),
        P(None, ("gx", "gy")),
        P(None, ("gx", "gy")),
        P(("gx", "gy")),
        P(("gx", "gy"), None),
        P(None, ("gx", "gy")),
    )
    return jax.shard_map(
        shards,
        mesh=mesh,
        in_specs=placed,
        out_specs=(
            P(None, "gx", "gy", None),
            P("gx", "gy", None),
            P("gx", "gy", None),
            P(None, ("gx", "gy")),
        ),
        check_vma=False,
    )
```

```python
import functools
import math

import jax
import jax.numpy as jnp
import numpy as np
from jax import lax
from jax.experimental import pallas as pl
from jax.experimental.pallas import tpu as pltpu
from jax.sharding import PartitionSpec as P

MESH = pl.DeviceIdType.MESH
GX, GY = 16, 8
DEV = GX * GY
SX, SY, NZ = 16, 32, 128
NX, NY = 256, 256
HALF = 72
F32 = jnp.float32
BF16 = jnp.bfloat16
ANY = pl.BlockSpec(memory_space=pl.ANY)


def split_table(table):
    table = np.asarray(table, np.float32)
    high = table.astype(jnp.bfloat16)
    low = (table - high.astype(np.float32)).astype(jnp.bfloat16)
    return np.stack([high, low])


@functools.cache
def send_order():
    hops = (0, 1, 2, 1)
    ways = ((0, 0), (1, 0), (1, 1), (0, 1))
    left = [(k, i, j, n) for k in range(4) for i in range(4) for j in range(4) for n in range(2)][1:]
    used, order = [0] * 6, []

    def after(peer):
        return [u + w for u, w in zip(used, sum((ways[step] for step in peer[:3]), ()))]

    while left:
        far = max(sum(hops[step] for step in peer[:3]) for peer in left)
        ring = [peer for peer in left if sum(hops[step] for step in peer[:3]) == far]
        best = min(ring, key=lambda peer: (max(after(peer)), sum(u * u for u in after(peer))))
        used = after(best)
        order.append(best)
        left.remove(best)
    return tuple(order)


@functools.cache
def tables():
    tau = 2.0 * math.pi
    z = np.arange(NZ)
    cosine = np.cos(math.pi * (z[None, :] + 0.5) * z[:, None] / NZ)
    weight = np.where(z == 0, 1.0 / NZ, 2.0 / NZ)
    back = cosine * weight[:, None]
    rows, factor, seen = [], [], set()
    for p in range(16):
        for q in range(8):
            if (p, q) in seen:
                continue
            mirror = (-p % 16, -q % 8)
            seen.update({(p, q), mirror})
            rows.append((p, q))
            factor.append(1.0 if mirror == (p, q) else 2.0)
    pad = HALF - len(rows)
    low_x = np.array([r[0] for r in rows] + [0] * pad)
    low_y = np.array([r[1] for r in rows] + [0] * pad)
    factor = np.array(factor + [0.0] * pad)
    used = np.array([1.0] * len(rows) + [0.0] * pad)
    a = np.repeat(np.arange(16), 8)
    b = np.tile(np.arange(8), 16)
    first, last = [], []
    for c in range(4):
        angle = tau * (
            low_x[:, None] * a[None] / 16.0
            + low_y[:, None] * b[None] / 8.0
            + low_x[:, None] * c / 64.0
        )
        first.append(np.concatenate([np.cos(angle) * used[:, None], -np.sin(angle) * used[:, None]]))
        scale = factor[:, None] / (NX * NY)
        last.append(np.concatenate([np.cos(angle) * scale, -np.sin(angle) * scale]).T)
    lane_i = np.repeat(np.arange(4), 32)
    lane_j = np.tile(np.arange(32), 4)
    turn_cos, turn_sin, wave = [], [], []
    for q in range(4):
        kx0 = low_x + 16 * q
        angle = tau * (kx0[:, None] * lane_i[None] + low_y[:, None] * lane_j[None]) / 256.0
        turn_cos.append(np.cos(angle))
        turn_sin.append(np.sin(angle))
        kx = kx0[:, None] + 64 * lane_i[None]
        ky = low_y[:, None] + 8 * lane_j[None]
        wave.append(-4.0 * np.sin(math.pi * kx / NX) ** 2 - 4.0 * np.sin(math.pi * ky / NY) ** 2)
    turns = np.stack([np.concatenate(turn_cos), np.concatenate(turn_sin), np.concatenate(wave)])
    angle = tau * (lane_i[:, None] * lane_i[None] / 4.0 + lane_j[:, None] * lane_j[None] / 32.0)
    cos2, sin2 = np.cos(angle), np.sin(angle)
    ahead = np.block([[cos2, -sin2], [sin2, cos2]])
    behind = np.block([[cos2, sin2], [-sin2, cos2]])
    wave_z = -4.0 * np.sin(math.pi * z / (2.0 * NZ)) ** 2
    wave_z = np.broadcast_to(wave_z[:, None], (NZ, 128)).astype(np.float32)
    box = np.zeros((32, 128), np.float32)
    for column in range(4):
        for j in range(32):
            box[column * 8 + j // 4, column * 32 + j] = 1.0
    return dict(
        cosine=packed_left(cosine),
        first=packed_left(np.stack(first)),
        ahead=split_table(ahead),
        behind=split_table(behind),
        last=np.concatenate(list(split_table(np.stack(last))), axis=1),
        turns=turns.astype(np.float32),
        wave_z=wave_z,
        box=box.astype(jnp.bfloat16),
        back=np.block([[*split_table(back)], [split_table(back)[0], np.zeros((NZ, NZ), jnp.bfloat16)]]),
    )


def halves(values):
    high = values.astype(BF16)
    return high, (values - high.astype(F32)).astype(BF16)


def product(left, right, dims):
    def one(x, y):
        return lax.dot_general(x, y, (dims, ((), ())), preferred_element_type=F32)

    (left_high, left_low), (right_high, right_low) = left, right
    return one(left_high, right_high) + (one(left_high, right_low) + one(left_low, right_high))


def packed_left(table):
    high, low = split_table(table)
    return np.concatenate([high, low], axis=-1)


def fold(wide):
    return wide[:, :128] + wide[:, 128:]


def packed_right(high, low):
    zero = jnp.zeros_like(low)
    return jnp.concatenate(
        [jnp.concatenate([high, low], axis=1), jnp.concatenate([high, zero], axis=1)], axis=0
    )


def one_product(left, right, dims):
    return lax.dot_general(left, right, (dims, ((), ())), preferred_element_type=F32)


NN = ((1,), (0,))
NT = ((1,), (1,))
TN = ((0,), (0,))


def step_kernel(
    vel, theta, vapour, radius, multi, counts, pairing, dest,
    cosine_h, first_h, ahead_h, behind_h, last_h, turns_h, wave_h, box_h,
    modes, ad, moments_out,
    fp, before_u, xu2, yl, yh, corner, row_y0, below_y, quad, send1, got1, send2,
    cosine, first, ahead, behind, last, turns, wave, box,
    rad_v, mul_v, cnt_v, pair_v, dst_v, cond, load, near,
    known, load_sem, drop_sem, table_sem, hs_sem, hr_sem, s1_sem, r1_sem, s2_sem, r2_sem,
    ms_sem, mr_sem,
):
    gx = lax.axis_index("gx")
    gy = lax.axis_index("gy")
    me = gx * GY + gy
    east, west = lax.rem(gx + 1, GX), lax.rem(gx + GX - 1, GX)
    north, south = lax.rem(gy + 1, GY), lax.rem(gy + GY - 1, GY)

    loads = [
        pltpu.make_async_copy(vel, fp.at[pl.ds(0, 3), pl.ds(1, SX)], load_sem.at[0]),
        pltpu.make_async_copy(theta, fp.at[3, pl.ds(1, SX)], load_sem.at[1]),
        pltpu.make_async_copy(vapour, fp.at[4, pl.ds(1, SX)], load_sem.at[2]),
    ]
    drops = [
        pltpu.make_async_copy(source, target, drop_sem.at[k])
        for k, (source, target) in enumerate(
            [(radius, rad_v), (multi, mul_v), (counts, cnt_v), (pairing, pair_v), (dest, dst_v)]
        )
    ]
    table_pairs = [
        (cosine_h, cosine), (box_h, box), (first_h, first), (turns_h, turns), (ahead_h, ahead),
        (wave_h, wave), (behind_h, behind), (last_h, last),
    ]
    fetches = [
        pltpu.make_async_copy(source, target, table_sem.at[k])
        for k, (source, target) in enumerate(table_pairs)
    ]
    for copy in loads:
        copy.start()

    barrier = pltpu.get_barrier_semaphore()

    chip_z, chip_x, chip_y, core = gx // 4, lax.rem(gx, 4), gy // 2, lax.rem(gy, 2)

    peers_x = [[lax.rem(chip_z + k, 4) * 4 + lax.rem(chip_x + i, 4) for i in range(4)] for k in range(4)]
    peers_y = [[lax.rem(chip_y + j, 4) * 2 + lax.rem(core + n, 2) for n in range(2)] for j in range(4)]

    def away(step_z, step_x, step_y, step_core):
        return peers_x[step_z % 4][step_x % 4], peers_y[step_y % 4][step_core]

    steps = [(k, i, j, n) for k in (0, 1, -1) for i in (1, -1, 0) for j in (1, -1, 0) for n in (0, 1)]
    steps.sort(key=lambda step: -sum(map(abs, step[:3])))
    around = [away(*step) for step in steps if any(step)]
    corners = [away(k, i, j, 0) for k in (1, -1) for i in (1, -1) for j in (1, -1)]
    for device in around:
        pl.semaphore_signal(barrier, inc=1, device_id=device, device_id_type=MESH)
    pl.semaphore_wait(barrier, len(around))

    def remote(source, target_ref, k, device):
        return pltpu.make_async_remote_copy(
            src_ref=source, dst_ref=target_ref, send_sem=hs_sem.at[k], recv_sem=hr_sem.at[k],
            device_id=device, device_id_type=MESH,
        )

    winds = fp.at[pl.ds(0, 3)]
    wind = [
        remote(winds.at[:, SX], fp.at[pl.ds(0, 3), 0], 0, (east, gy)),
        remote(winds.at[:, 1], fp.at[pl.ds(0, 3), SX + 1], 1, (west, gy)),
        remote(fp.at[0, SX - 1], xu2, 2, (east, gy)),
        remote(winds.at[:, pl.ds(1, SX), SY - 1], yl.at[pl.ds(0, 3)], 3, (gx, north)),
        remote(winds.at[:, pl.ds(1, SX), 0], yh.at[pl.ds(0, 3)], 4, (gx, south)),
        remote(fp.at[1, pl.ds(1, SX), SY - 2], yl.at[5], 5, (gx, north)),
        remote(fp.at[0, SX, pl.ds(SY - 1, 1)], corner.at[0, pl.ds(0, 1)], 6, (east, north)),
        remote(fp.at[0, SX, pl.ds(0, 1)], corner.at[1, pl.ds(0, 1)], 7, (east, south)),
        remote(fp.at[1, SX, pl.ds(SY - 1, 1)], corner.at[2, pl.ds(0, 1)], 8, (east, north)),
        remote(fp.at[1, 1, pl.ds(SY - 1, 1)], corner.at[3, pl.ds(0, 1)], 9, (west, north)),
    ]
    air = [
        remote(fp.at[3, SX], fp.at[3, 0], 10, (east, gy)),
        remote(fp.at[4, SX], fp.at[4, 0], 11, (east, gy)),
        remote(fp.at[3, 1], fp.at[3, SX + 1], 12, (west, gy)),
        remote(fp.at[4, 1], fp.at[4, SX + 1], 13, (west, gy)),
        remote(fp.at[3, pl.ds(1, SX), SY - 1], yl.at[3], 14, (gx, north)),
        remote(fp.at[4, pl.ds(1, SX), SY - 1], yl.at[4], 15, (gx, north)),
        remote(fp.at[3, pl.ds(1, SX), 0], yh.at[3], 16, (gx, south)),
        remote(fp.at[4, pl.ds(1, SX), 0], yh.at[4], 17, (gx, south)),
    ]
    halo = wind + air
    loads[0].wait()
    for copy in wind[6:] + wind[:6]:
        copy.start()

    def pass_on(k, devices):
        for device in devices:
            pl.semaphore_signal(known.at[k], inc=1, device_id=device, device_id_type=MESH)

    pass_on(0, corners)
    for copy in fetches + drops:
        copy.start()
    for copy in loads[1:]:
        copy.wait()

    row = lax.broadcasted_iota(jnp.int32, (SY, NZ), 0)
    lane = lax.broadcasted_iota(jnp.int32, (SY, NZ), 1)
    tile_row = lax.broadcasted_iota(jnp.int32, (8, NZ), 0)

    def upward(values):
        return pltpu.roll(values, NZ - 1, 1)

    def downward(values):
        return pltpu.roll(values, 1, 1)

    def coefficients(speed, shape_lane=None):
        scaled = 0.1 * speed
        return 0.01 - scaled, 0.01 + scaled

    def vertical(speed, lanes):
        up, down = coefficients(speed)
        top, bottom = lanes == NZ - 1, lanes == 0
        centre = 0.94 + jnp.where(top, up, 0.0) + jnp.where(bottom, down, 0.0)
        return jnp.where(top, 0.0, up), jnp.where(bottom, 0.0, down), centre

    def advect_plane(x, fields):
        c_east, c_west = coefficients(fp[0, x + 1])
        c_north, c_south = coefficients(fp[1, x + 1])
        c_north = jnp.where(row == SY - 1, 0.0, c_north)
        c_south = jnp.where(row == 0, 0.0, c_south)
        c_up, c_down, c_mid = vertical(fp[2, x + 1], lane)
        for f in fields:
            centre = fp[f, x + 1]
            ad[f, x] = (
                (c_mid * centre + c_east * fp[f, x + 2] + c_west * fp[f, x])
                + (c_north * pltpu.roll(centre, SY - 1, 0) + c_south * pltpu.roll(centre, 1, 0))
                + (c_up * upward(centre) + c_down * downward(centre))
            )

    def inner(x, carry):
        advect_plane(x, (0, 1, 2))
        row_y0[pl.ds(x, 1), :] = fp[1, x + 1, 0:1, :]
        return carry

    lax.fori_loop(1, SX - 1, inner, 0)
    for copy in air:
        copy.start()

    for copy in drops:
        copy.wait()
    box_row = lax.broadcasted_iota(jnp.int32, (32, 32), 0)
    box_lane = lax.broadcasted_iota(jnp.int32, (32, 32), 1)
    spread = jnp.where(box_row == box_lane, cnt_v[...][None, :].astype(F32), 0.0)
    used = jnp.sum(spread, axis=1, keepdims=True)
    slot = lax.broadcasted_iota(jnp.int32, (32, 64), 1).astype(F32)
    live = jnp.where(slot < used, mul_v[...], 0.0)
    target = dst_v[...]
    local_box = lax.broadcasted_iota(jnp.int32, (32, 64), 0)
    source_x = gx * 4 + (local_box >> 3)
    source_y = gy * 8 + (local_box & 7)
    target_x = (target >> 8) * 4 + ((target & 31) >> 3)
    target_y = ((target >> 5) & 7) * 8 + (target & 7)
    offset_x = (target_x - source_x + 1) & 63
    offset_y = (target_y - source_y + 1) & 63
    code = (offset_x * 3 + offset_y).astype(F32)

    def twice(values):
        return jnp.concatenate([values, values], axis=1)

    pair = twice(pair_v[...])
    order = jnp.where(lax.broadcasted_iota(jnp.int32, (32, 128), 1) < 64, pair, pltpu.roll(pair, 32, 1))
    radius_p = jnp.take_along_axis(twice(rad_v[...]), order, axis=1)
    live_p = jnp.take_along_axis(twice(live), order, axis=1)
    code_p = jnp.take_along_axis(twice(code), order, axis=1)

    for x in (0, SX - 1):
        row_y0[pl.ds(x, 1), :] = fp[1, x + 1, 0:1, :]
    for copy in wind[3:6]:
        copy.wait_recv()

    speed_v = yl[1]
    row_x = lax.broadcasted_iota(jnp.int32, (SX, NZ), 0)
    lane_x = lax.broadcasted_iota(jnp.int32, (SX, NZ), 1)
    c_east, c_west = coefficients(yl[0])
    c_north, c_south = coefficients(speed_v)
    c_up, c_down, c_mid = vertical(yl[2], lane_x)
    after = jnp.where(row_x == SX - 1, 0.0, pltpu.roll(speed_v, SX - 1, 0))
    before = jnp.where(row_x == 0, 0.0, pltpu.roll(speed_v, 1, 0))
    below_y[...] = (
        (c_mid * speed_v + c_east * after + c_west * before)
        + (c_north * row_y0[...] + c_south * yl[5])
        + (c_up * upward(speed_v) + c_down * downward(speed_v))
    )
    fetches[0].wait()

    def border(x, fields):
        _, c_south = coefficients(fp[1, x + 1, 0:8, :])
        c_north, _ = coefficients(fp[1, x + 1, SY - 8 : SY, :])
        c_south = jnp.where(tile_row == 0, c_south, 0.0)
        c_north = jnp.where(tile_row == 7, c_north, 0.0)
        for f in fields:
            ad[f, x, 0:8, :] += c_south * yl[f, pl.ds(x, 1), :]
            ad[f, x, SY - 8 : SY, :] += c_north * yh[f, pl.ds(x, 1), :]

    def block(c):
        parts = []
        for i in range(4):
            x = c * 4 + i
            if x != 3:
                border(x, (0, 1, 2))
            star_w = ad[2, x] + 0.1 * fp[3, x + 1]
            ad[2, x] = star_w
            star_v = ad[1, x]
            star_u = ad[0, x]
            if i == 0:
                last_u = before_u[...] if c == 0 else ad[0, x - 1]
            behind_v = jnp.where(row == 0, below_y[pl.ds(x, 1), :], pltpu.roll(star_v, 1, 0))
            below_w = jnp.where(lane == 0, 0.0, downward(star_w))
            parts.append((star_u - last_u) + (star_v - behind_v) + (star_w - below_w))
            last_u = star_u
        chunk = jnp.concatenate(parts, axis=0)
        high, low = halves(chunk)
        wide = jnp.concatenate(
            [jnp.concatenate([high, high], axis=1), jnp.concatenate([low, jnp.zeros_like(low)], axis=1)],
            axis=0,
        )
        send1[c] = fold(one_product(cosine[...], wide, NT))

    def scalars(c, carry):
        total = jnp.zeros((SY, NZ), F32)
        for i in range(4):
            x = c * 4 + i
            advect_plane(x, (3, 4))
            border(x, (3, 4))
            total = total + ad[4, x]
        quad[c] = total
        return carry

    border(3, (0, 1, 2))
    block(1)
    block(2)
    for copy in wind[:3]:
        copy.wait_recv()
    advect_plane(0, (0, 1, 2))
    advect_plane(SX - 1, (0, 1, 2))

    for copy in wind[6:]:
        copy.wait_recv()
    _, end_west = coefficients(yl[0, 0:1, :])
    end_east, _ = coefficients(yl[0, SX - 1 : SX, :])
    below_y[0:1, :] += end_west * corner[2, 0:1, :]
    below_y[SX - 1 : SX, :] += end_east * corner[3, 0:1, :]

    speed = fp[0, 0]
    c_east, c_west = coefficients(speed)
    c_north, c_south = coefficients(fp[1, 0])
    c_up, c_down, c_mid = vertical(fp[2, 0], lane)
    above = jnp.where(row == SY - 1, corner[1, 0:1, :], pltpu.roll(speed, SY - 1, 0))
    beneath = jnp.where(row == 0, corner[0, 0:1, :], pltpu.roll(speed, 1, 0))
    before_u[...] = (
        (c_mid * speed + c_east * fp[0, 1] + c_west * xu2[...])
        + (c_north * above + c_south * beneath)
        + (c_up * upward(speed) + c_down * downward(speed))
    )
    block(0)
    block(3)
    pl.semaphore_wait(known.at[0], len(corners))

    def scatter(source, target_ref, send_sem, recv_sem):
        for step_z, step_x, step_y, step_core in send_order():
            px, py = peers_x[step_z][step_x], peers_y[step_y][step_core]
            pltpu.make_async_remote_copy(
                src_ref=source.at[:, pl.ds(px * GY + py, 1), :],
                dst_ref=target_ref.at[:, pl.ds(me, 1), :],
                send_sem=send_sem, recv_sem=recv_sem, device_id=(px, py), device_id_type=MESH,
            ).start()

    def drained(source, target_ref, sem):
        count = pl.ds(0, DEV - 1)
        pltpu.make_async_copy(source.at[:, count, :], target_ref.at[:, count, :], sem).wait()

    scatter(send1, got1, s1_sem, r1_sem)
    got1[:, pl.ds(me, 1), :] = send1[:, pl.ds(me, 1), :]

    for copy in air:
        copy.wait_recv()
    lax.fori_loop(0, 4, scalars, 0)
    fetches[1].wait()
    high, low = halves(quad[...].reshape(128, NZ))
    sums = lax.dot_general(box[...], high, (NN, ((), ())), preferred_element_type=F32)
    sums = sums + lax.dot_general(box[...], low, (NN, ((), ())), preferred_element_type=F32)
    mean = jnp.sum(sums, axis=1, keepdims=True) * (1.0 / (16 * NZ))
    soft = jnp.maximum(mean, 0.0) + jnp.log1p(jnp.exp(-jnp.abs(mean)))
    grown = radius_p + 0.5 * soft
    root = jnp.sqrt(grown)
    mass = grown * root
    gain = mass - radius_p * jnp.sqrt(radius_p)

    def other(values):
        return pltpu.roll(values, 64, 1)

    root_sum = root + other(root)
    rate = 0.05 * (root_sum * root_sum * jnp.abs(grown - other(grown)) * other(live_p))
    final = (mass + rate * other(mass)) / (1.0 + rate)
    lanes = lax.broadcasted_iota(jnp.int32, (32, 128), 1)
    own_live = jnp.where(lanes < 64, live_p, 0.0)
    cond[...] = jnp.broadcast_to(jnp.sum(own_live * gain, axis=1, keepdims=True), (32, 128)) * 0.002
    carried = [own_live, own_live * final, own_live * final * final]
    packed = jnp.zeros((32, 128), F32)
    for d in range(9):
        chosen = code_p == float(d)
        for k in range(3):
            amount = jnp.sum(jnp.where(chosen, carried[k], 0.0), axis=1, keepdims=True)
            packed = packed + jnp.where(lanes == d * 3 + k, amount, 0.0)
    load[...] = packed

    def share(source, target_ref, k, device):
        return pltpu.make_async_remote_copy(
            src_ref=source, dst_ref=target_ref, send_sem=ms_sem.at[k], recv_sem=mr_sem.at[k],
            device_id=device, device_id_type=MESH,
        )

    top, bottom = pl.ds(24, 8), pl.ds(0, 8)
    shares = [
        share(load.at[top], near.at[0, bottom], 0, (east, gy)),
        share(load.at[bottom], near.at[1, bottom], 1, (west, gy)),
        share(load, near.at[2], 2, (gx, north)),
        share(load, near.at[3], 3, (gx, south)),
        share(load.at[top], near.at[4, bottom], 4, (east, north)),
        share(load.at[top], near.at[5, bottom], 5, (east, south)),
        share(load.at[bottom], near.at[6, bottom], 6, (west, north)),
        share(load.at[bottom], near.at[7, bottom], 7, (west, south)),
    ]
    for copy in shares:
        copy.start()

    def dry(x, carry):
        first_box = (x // 4) * 8
        for t in range(4):
            drop = jnp.where(
                tile_row < 4,
                cond[pl.ds(first_box + 2 * t, 1), :],
                cond[pl.ds(first_box + 2 * t + 1, 1), :],
            )
            ad[4, x, 8 * t : 8 * t + 8, :] -= drop
        return carry

    lax.fori_loop(0, SX, dry, 0)

    for copy in fetches[2:]:
        copy.wait()
    drained(send1, got1, r1_sem)
    z_re, z_im = [], []
    for c in range(4):
        both = fold(one_product(first[c], packed_right(*halves(got1[c])), NN))
        z_re.append(both[:HALF])
        z_im.append(both[HALF:])

    def butterfly(re, im, sign):
        s02r, s02i = re[0] + re[2], im[0] + im[2]
        d02r, d02i = re[0] - re[2], im[0] - im[2]
        s13r, s13i = re[1] + re[3], im[1] + im[3]
        d13r, d13i = re[1] - re[3], im[1] - im[3]
        if sign < 0:
            return (
                [s02r + s13r, d02r + d13i, s02r - s13r, d02r - d13i],
                [s02i + s13i, d02i - d13r, s02i - s13i, d02i + d13r],
            )
        return (
            [s02r + s13r, d02r - d13i, s02r - s13r, d02r + d13i],
            [s02i + s13i, d02i + d13r, s02i - s13i, d02i - d13r],
        )

    def stacked_product(values, table):
        high, low = halves(values)
        both = one_product(jnp.concatenate([high, low], axis=0), table[0], NN)
        rows = values.shape[0]
        return both[:rows] + (both[rows:] + one_product(high, table[1], NN))

    q_re, q_im = butterfly(z_re, z_im, -1)
    back_re, back_im = [], []
    for q in range(0, 4, 2):
        part = pl.ds(HALF * q, HALF * 2)
        re, im = (jnp.concatenate(side[q : q + 2], axis=0) for side in (q_re, q_im))
        turn_cos, turn_sin = turns[0, part, :], turns[1, part, :]
        joined = jnp.concatenate([re * turn_cos + im * turn_sin, im * turn_cos - re * turn_sin], axis=1)
        spectrum = stacked_product(joined, ahead)
        eigen = turns[2, part, :] + wave[pl.ds(me, 1), :]
        inverse = jnp.where(eigen == 0.0, 0.0, 1.0 / jnp.where(eigen == 0.0, 1.0, eigen))
        turned = stacked_product(spectrum * jnp.concatenate([inverse, inverse], axis=1), behind)
        re, im = turned[:, :128], turned[:, 128:]
        turned_re, turned_im = re * turn_cos - im * turn_sin, im * turn_cos + re * turn_sin
        for k in range(2):
            back_re.append(turned_re[HALF * k : HALF * (k + 1)])
            back_im.append(turned_im[HALF * k : HALF * (k + 1)])
    v_re, v_im = butterfly(back_re, back_im, 1)
    wide_lane = lax.broadcasted_iota(jnp.int32, (128, 128), 1)
    edge = None
    for c in range(4):
        stacked = jnp.concatenate([v_re[c], v_im[c]], axis=0)
        high, low = halves(stacked)
        wide = one_product(last[c], jnp.concatenate([high, low], axis=1), NN)
        plane = wide[:128, :128] + (wide[:128, 128:] + wide[128:, :128])
        send2[c] = plane
        if c == 0:
            next_x = pltpu.roll(plane, 120, 0)
        picked = jnp.where((wide_lane & 31) == 0, plane, 0.0)
        picked = picked if c == 0 else pltpu.roll(picked, c, 1)
        edge = picked if edge is None else edge + picked
    row_b = lax.broadcasted_iota(jnp.int32, (128, 128), 0) & 7
    edge = jnp.where(row_b == 7, pltpu.roll(edge, 7, 0), pltpu.roll(edge, 127, 0))
    moved = pltpu.roll(edge, 36, 1)
    in_move = (wide_lane >= 36) & (wide_lane < 40)
    send2[4] = jnp.where(wide_lane < 32, next_x, jnp.where(in_move, moved, edge))

    scatter(send2, modes, s2_sem, r2_sem)
    modes[:, pl.ds(me, 1), :] = send2[:, pl.ds(me, 1), :]

    for copy in shares:
        copy.wait_recv()
    tile_lane = lax.broadcasted_iota(jnp.int32, (8, 128), 1)

    def column_of(x):
        if x < 0:
            return near[0, 0:8, :], near[4, 7:8, :], near[5, 0:1, :]
        if x > 3:
            return near[1, 0:8, :], near[6, 7:8, :], near[7, 0:1, :]
        return load[8 * x : 8 * x + 8, :], near[2, 8 * x + 7 : 8 * x + 8, :], near[3, 8 * x : 8 * x + 1, :]

    arrived = [jnp.zeros((8, 128), F32) for _ in range(4)]
    for x in range(-1, 5):
        centre, low_row, high_row = column_of(x)
        shifted = [
            jnp.where(tile_row == 7, high_row, pltpu.roll(centre, 7, 0)),
            centre,
            jnp.where(tile_row == 0, low_row, pltpu.roll(centre, 1, 0)),
        ]
        for dx in (-1, 0, 1):
            if not 0 <= x + dx < 4:
                continue
            for dy in (-1, 0, 1):
                d = (dx + 1) * 3 + dy + 1
                values = shifted[dy + 1]
                values = values if d == 0 else pltpu.roll(values, 128 - 3 * d, 1)
                arrived[x + dx] = arrived[x + dx] + values
    stacked = jnp.concatenate(arrived + [jnp.zeros((96, 128), F32)], axis=0) * (1.0 / 64)
    moments_out[...] = stacked.T[0:8, :]

    for copy in halo:
        copy.wait_send()
    for copy in shares:
        copy.wait_send()
    drained(send1, got1, s1_sem)
    drained(send2, send2, s2_sem)
    drained(send2, modes, r2_sem)


def final_kernel(
    modes, ad, moments, back,
    vel_out, theta_out, vapour_out, moments_out,
    fresh, mom_o, pressure, out_sem,
):
    mom_o[...] = moments[0:3, 0:32]
    outs = [
        pltpu.make_async_copy(ad.at[3], theta_out, out_sem.at[0]),
        pltpu.make_async_copy(ad.at[4], vapour_out, out_sem.at[1]),
        pltpu.make_async_copy(mom_o, moments_out, out_sem.at[2]),
    ]
    for copy in outs:
        copy.start()
    row = lax.broadcasted_iota(jnp.int32, (SY, NZ), 0)
    lane = lax.broadcasted_iota(jnp.int32, (SY, NZ), 1)

    def levels(c):
        wide = one_product(jnp.concatenate(halves(modes[c]), axis=0), back[...], TN)
        pressure[pl.ds(128 * c, 128), :] = fold(wide)

    levels(4)
    for c in (3, 2, 1, 0):
        levels(c)
        for i in range(4):
            x = 4 * c + i
            here = pressure[pl.ds(32 * x, 32), :]
            ahead = pressure[pl.ds(32 * x + 32, 32), :]
            line = 512 + (36, 32, 64, 96)[i] + c
            side = jnp.where(row == SY - 1, pressure[line : line + 1, :], pltpu.roll(here, SY - 1, 0))
            above = jnp.where(lane == NZ - 1, here, pltpu.roll(here, NZ - 1, 1))
            fresh[0, x] = ad[0, x] - (ahead - here)
            fresh[1, x] = ad[1, x] - (side - here)
            fresh[2, x] = ad[2, x] - (above - here)
        part = pl.ds(4 * c, 4)
        copy = pltpu.make_async_copy(fresh.at[:, part], vel_out.at[:, part], out_sem.at[3 + c])
        copy.start()
        outs.append(copy)
    for copy in outs:
        copy.wait()


def shards(velocity, theta, vapour, radius_sq, multiplicity, counts, pairing, destination):
    t = tables()
    names = ["cosine", "first", "ahead", "behind", "last", "turns", "wave_z", "box"]
    held = [jnp.asarray(t[name]) for name in names]
    block = (SX, SY, NZ)
    shape = jax.ShapeDtypeStruct
    vmem = pltpu.VMEM
    dma = pltpu.SemaphoreType.DMA
    here = pl.BlockSpec(memory_space=pltpu.VMEM)
    modes, advected, moments = pl.pallas_call(
        step_kernel,
        out_shape=(
            vmem((5, DEV, 128), F32),
            vmem((5,) + block, F32),
            vmem((8, 128), F32),
        ),
        in_specs=[ANY] * 16,
        out_specs=(here,) * 3,
        scratch_shapes=[
            vmem((5, SX + 2, SY, NZ), F32),
            vmem((SY, NZ), F32),
            vmem((SY, NZ), F32),
            vmem((6, SX, NZ), F32),
            vmem((5, SX, NZ), F32),
            vmem((4, 8, NZ), F32),
            vmem((SX, NZ), F32),
            vmem((SX, NZ), F32),
            vmem((4, SY, NZ), F32),
            vmem((4, DEV, 128), F32),
            vmem((4, DEV, 128), F32),
            vmem((5, DEV, 128), F32),
        ]
        + [vmem(t[name].shape, t[name].dtype) for name in names]
        + [
            vmem((32, 64), F32),
            vmem((32, 64), F32),
            vmem((32,), jnp.int32),
            vmem((32, 64), jnp.int32),
            vmem((32, 64), jnp.int32),
            vmem((32, 128), F32),
            vmem((32, 128), F32),
            vmem((8, 32, 128), F32),
            pltpu.SemaphoreType.REGULAR((1,)),
            dma((3,)),
            dma((5,)),
            dma((8,)),
            dma((18,)),
            dma((18,)),
            dma(()),
            dma(()),
            dma(()),
            dma(()),
            dma((8,)),
            dma((8,)),
        ],
        compiler_params=pltpu.CompilerParams(
            has_side_effects=True, collective_id=1, vmem_limit_bytes=24 << 20,
        ),
        name="cloud_step",
    )(*[
        pltpu.with_memory_space_constraint(value, pltpu.HBM)
        for value in (
            velocity, theta, vapour, radius_sq.T, multiplicity.T, counts, pairing, destination.T, *held
        )
    ])
    return pl.pallas_call(
        final_kernel,
        out_shape=(
            shape((3,) + block, F32),
            shape(block, F32),
            shape(block, F32),
            shape((3, 32), F32),
        ),
        in_specs=[here] * 4,
        out_specs=(ANY,) * 4,
        scratch_shapes=[
            vmem((3,) + block, F32),
            vmem((3, 32), F32),
            vmem((640, 128), F32),
            dma((7,)),
        ],
        compiler_params=pltpu.CompilerParams(vmem_limit_bytes=12 << 20),
        name="project",
    )(
        *[pltpu.with_memory_space_constraint(value, pltpu.VMEM) for value in (modes, advected, moments)],
        jnp.asarray(t["back"]),
    )


def solution(mesh):
    placed = (
        P(None, "gx", "gy", None),
        P("gx", "gy", None),
        P("gx", "gy", None),
        P(None, ("gx", "gy")),
        P(None, ("gx", "gy")),
        P(("gx", "gy")),
        P(("gx", "gy"), None),
        P(None, ("gx", "gy")),
    )
    return jax.shard_map(
        shards,
        mesh=mesh,
        in_specs=placed,
        out_specs=(
            P(None, "gx", "gy", None),
            P("gx", "gy", None),
            P("gx", "gy", None),
            P(None, ("gx", "gy")),
        ),
        check_vma=False,
    )
```

```python
import functools
import math

import jax
import jax.numpy as jnp
import numpy as np
from jax import lax
from jax.experimental import pallas as pl
from jax.experimental.pallas import tpu as pltpu
from jax.sharding import PartitionSpec as P

MESH = pl.DeviceIdType.MESH
GX, GY = 16, 8
DEV = GX * GY
SX, SY, NZ = 16, 32, 128
NX, NY = 256, 256
HALF = 72
F32 = jnp.float32
BF16 = jnp.bfloat16
ANY = pl.BlockSpec(memory_space=pl.ANY)


def split_table(table):
    table = np.asarray(table, np.float32)
    high = table.astype(jnp.bfloat16)
    low = (table - high.astype(np.float32)).astype(jnp.bfloat16)
    return np.stack([high, low])


@functools.cache
def send_order():
    hops = (0, 1, 2, 1)
    ways = ((0, 0), (1, 0), (1, 1), (0, 1))
    left = [(k, i, j, n) for k in range(4) for i in range(4) for j in range(4) for n in range(2)][1:]
    used, order = [0] * 6, []

    def after(peer):
        return [u + w for u, w in zip(used, sum((ways[step] for step in peer[:3]), ()))]

    while left:
        far = max(sum(hops[step] for step in peer[:3]) for peer in left)
        ring = [peer for peer in left if sum(hops[step] for step in peer[:3]) == far]
        best = min(ring, key=lambda peer: (max(after(peer)), sum(u * u for u in after(peer))))
        used = after(best)
        order.append(best)
        left.remove(best)
    return tuple(order)


@functools.cache
def tables():
    tau = 2.0 * math.pi
    z = np.arange(NZ)
    cosine = np.cos(math.pi * (z[None, :] + 0.5) * z[:, None] / NZ)
    weight = np.where(z == 0, 1.0 / NZ, 2.0 / NZ)
    back = cosine * weight[:, None]
    rows, factor, seen = [], [], set()
    for p in range(16):
        for q in range(8):
            if (p, q) in seen:
                continue
            mirror = (-p % 16, -q % 8)
            seen.update({(p, q), mirror})
            rows.append((p, q))
            factor.append(1.0 if mirror == (p, q) else 2.0)
    pad = HALF - len(rows)
    low_x = np.array([r[0] for r in rows] + [0] * pad)
    low_y = np.array([r[1] for r in rows] + [0] * pad)
    factor = np.array(factor + [0.0] * pad)
    used = np.array([1.0] * len(rows) + [0.0] * pad)
    a = np.repeat(np.arange(16), 8)
    b = np.tile(np.arange(8), 16)
    first, last = [], []
    for c in range(4):
        angle = tau * (
            low_x[:, None] * a[None] / 16.0
            + low_y[:, None] * b[None] / 8.0
            + low_x[:, None] * c / 64.0
        )
        first.append(np.concatenate([np.cos(angle) * used[:, None], -np.sin(angle) * used[:, None]]))
        scale = factor[:, None] / (NX * NY)
        last.append(np.concatenate([np.cos(angle) * scale, -np.sin(angle) * scale]).T)
    lane_i = np.repeat(np.arange(4), 32)
    lane_j = np.tile(np.arange(32), 4)
    turn_cos, turn_sin, wave = [], [], []
    for q in range(4):
        kx0 = low_x + 16 * q
        angle = tau * (kx0[:, None] * lane_i[None] + low_y[:, None] * lane_j[None]) / 256.0
        turn_cos.append(np.cos(angle))
        turn_sin.append(np.sin(angle))
        kx = kx0[:, None] + 64 * lane_i[None]
        ky = low_y[:, None] + 8 * lane_j[None]
        wave.append(-4.0 * np.sin(math.pi * kx / NX) ** 2 - 4.0 * np.sin(math.pi * ky / NY) ** 2)
    turns = np.stack([np.concatenate(turn_cos), np.concatenate(turn_sin), np.concatenate(wave)])
    angle = tau * (lane_i[:, None] * lane_i[None] / 4.0 + lane_j[:, None] * lane_j[None] / 32.0)
    cos2, sin2 = np.cos(angle), np.sin(angle)
    ahead = np.block([[cos2, -sin2], [sin2, cos2]])
    behind = np.block([[cos2, sin2], [-sin2, cos2]])
    wave_z = -4.0 * np.sin(math.pi * z / (2.0 * NZ)) ** 2
    wave_z = np.broadcast_to(wave_z[:, None], (NZ, 128)).astype(np.float32)
    box = np.zeros((32, 128), np.float32)
    for column in range(4):
        for j in range(32):
            box[column * 8 + j // 4, column * 32 + j] = 1.0
    return dict(
        cosine=packed_left(cosine),
        first=packed_left(np.stack(first)),
        ahead=split_table(ahead),
        behind=split_table(behind),
        last=np.concatenate(list(split_table(np.stack(last))), axis=1),
        turns=turns.astype(np.float32),
        wave_z=wave_z,
        box=box.astype(jnp.bfloat16),
        back=np.block([[*split_table(back)], [split_table(back)[0], np.zeros((NZ, NZ), jnp.bfloat16)]]),
    )


def halves(values):
    high = values.astype(BF16)
    return high, (values - high.astype(F32)).astype(BF16)


def product(left, right, dims):
    def one(x, y):
        return lax.dot_general(x, y, (dims, ((), ())), preferred_element_type=F32)

    (left_high, left_low), (right_high, right_low) = left, right
    return one(left_high, right_high) + (one(left_high, right_low) + one(left_low, right_high))


def packed_left(table):
    high, low = split_table(table)
    return np.concatenate([high, low], axis=-1)


def fold(wide):
    return wide[:, :128] + wide[:, 128:]


def packed_right(high, low):
    zero = jnp.zeros_like(low)
    return jnp.concatenate(
        [jnp.concatenate([high, low], axis=1), jnp.concatenate([high, zero], axis=1)], axis=0
    )


def one_product(left, right, dims):
    return lax.dot_general(left, right, (dims, ((), ())), preferred_element_type=F32)


NN = ((1,), (0,))
NT = ((1,), (1,))
TN = ((0,), (0,))


def step_kernel(
    vel, theta, vapour, radius, multi, counts, pairing, dest,
    cosine_h, first_h, ahead_h, behind_h, last_h, turns_h, wave_h, box_h,
    modes, ad, moments_out,
    fp, before_u, xu2, yl, yh, corner, row_y0, below_y, quad, send1, got1, send2,
    cosine, first, ahead, behind, last, turns, wave, box,
    rad_v, mul_v, cnt_v, pair_v, dst_v, cond, load, near,
    known, load_sem, drop_sem, table_sem, hs_sem, hr_sem, s1_sem, r1_sem, s2_sem, r2_sem,
    ms_sem, mr_sem,
):
    gx = lax.axis_index("gx")
    gy = lax.axis_index("gy")
    me = gx * GY + gy
    east, west = lax.rem(gx + 1, GX), lax.rem(gx + GX - 1, GX)
    north, south = lax.rem(gy + 1, GY), lax.rem(gy + GY - 1, GY)

    loads = [
        pltpu.make_async_copy(vel, fp.at[pl.ds(0, 3), pl.ds(1, SX)], load_sem.at[0]),
        pltpu.make_async_copy(theta, fp.at[3, pl.ds(1, SX)], load_sem.at[1]),
        pltpu.make_async_copy(vapour, fp.at[4, pl.ds(1, SX)], load_sem.at[2]),
    ]
    drops = [
        pltpu.make_async_copy(source, target, drop_sem.at[k])
        for k, (source, target) in enumerate(
            [(radius, rad_v), (multi, mul_v), (counts, cnt_v), (pairing, pair_v), (dest, dst_v)]
        )
    ]
    table_pairs = [
        (cosine_h, cosine), (box_h, box), (first_h, first), (turns_h, turns), (ahead_h, ahead),
        (wave_h, wave), (behind_h, behind), (last_h, last),
    ]
    fetches = [
        pltpu.make_async_copy(source, target, table_sem.at[k])
        for k, (source, target) in enumerate(table_pairs)
    ]
    for copy in loads + drops + fetches:
        copy.start()

    barrier = pltpu.get_barrier_semaphore()

    chip_z, chip_x, chip_y, core = gx // 4, lax.rem(gx, 4), gy // 2, lax.rem(gy, 2)

    peers_x = [[lax.rem(chip_z + k, 4) * 4 + lax.rem(chip_x + i, 4) for i in range(4)] for k in range(4)]
    peers_y = [[lax.rem(chip_y + j, 4) * 2 + lax.rem(core + n, 2) for n in range(2)] for j in range(4)]

    def away(step_z, step_x, step_y, step_core):
        return peers_x[step_z % 4][step_x % 4], peers_y[step_y % 4][step_core]

    cube = [(k, i, j) for k in (0, 1, -1) for i in (1, -1, 0) for j in (1, -1, 0)]
    spare = [(k, 0, -k) for k in (1, -1)] + [(k, -k, j) for k in (1, -1) for j in (1, -1, 0)]
    steps = [(*step, n) for step in cube for n in (0, 1) if n == 0 or step not in spare]
    steps.sort(key=lambda step: -sum(map(abs, step[:3])))
    around = [away(*step) for step in steps if any(step)]
    corners = [away(k, i, j, 0) for k in (1, -1) for i in (1, -1) for j in (1, -1)]
    for device in around:
        pl.semaphore_signal(barrier, inc=1, device_id=device, device_id_type=MESH)
    pl.semaphore_wait(barrier, len(around))

    def remote(source, target_ref, k, device):
        return pltpu.make_async_remote_copy(
            src_ref=source, dst_ref=target_ref, send_sem=hs_sem.at[k], recv_sem=hr_sem.at[k],
            device_id=device, device_id_type=MESH,
        )

    winds = fp.at[pl.ds(0, 3)]
    wind = [
        remote(winds.at[:, SX], fp.at[pl.ds(0, 3), 0], 0, (east, gy)),
        remote(winds.at[:, 1], fp.at[pl.ds(0, 3), SX + 1], 1, (west, gy)),
        remote(fp.at[0, SX - 1], xu2, 2, (east, gy)),
        remote(winds.at[:, pl.ds(1, SX), SY - 1], yl.at[pl.ds(0, 3)], 3, (gx, north)),
        remote(winds.at[:, pl.ds(1, SX), 0], yh.at[pl.ds(0, 3)], 4, (gx, south)),
        remote(fp.at[1, pl.ds(1, SX), SY - 2], yl.at[5], 5, (gx, north)),
        remote(fp.at[0, SX, pl.ds(SY - 1, 1)], corner.at[0, pl.ds(0, 1)], 6, (east, north)),
        remote(fp.at[0, SX, pl.ds(0, 1)], corner.at[1, pl.ds(0, 1)], 7, (east, south)),
        remote(fp.at[1, SX, pl.ds(SY - 1, 1)], corner.at[2, pl.ds(0, 1)], 8, (east, north)),
        remote(fp.at[1, 1, pl.ds(SY - 1, 1)], corner.at[3, pl.ds(0, 1)], 9, (west, north)),
    ]
    air = [
        remote(fp.at[3, SX], fp.at[3, 0], 10, (east, gy)),
        remote(fp.at[4, SX], fp.at[4, 0], 11, (east, gy)),
        remote(fp.at[3, 1], fp.at[3, SX + 1], 12, (west, gy)),
        remote(fp.at[4, 1], fp.at[4, SX + 1], 13, (west, gy)),
        remote(fp.at[3, pl.ds(1, SX), SY - 1], yl.at[3], 14, (gx, north)),
        remote(fp.at[4, pl.ds(1, SX), SY - 1], yl.at[4], 15, (gx, north)),
        remote(fp.at[3, pl.ds(1, SX), 0], yh.at[3], 16, (gx, south)),
        remote(fp.at[4, pl.ds(1, SX), 0], yh.at[4], 17, (gx, south)),
    ]
    halo = wind + air
    loads[0].wait()
    for copy in wind[6:] + wind[:6]:
        copy.start()

    def pass_on(k, devices):
        for device in devices:
            pl.semaphore_signal(known.at[k], inc=1, device_id=device, device_id_type=MESH)

    pass_on(0, corners)
    for copy in loads[1:]:
        copy.wait()

    row = lax.broadcasted_iota(jnp.int32, (SY, NZ), 0)
    lane = lax.broadcasted_iota(jnp.int32, (SY, NZ), 1)
    tile_row = lax.broadcasted_iota(jnp.int32, (8, NZ), 0)

    def upward(values):
        return pltpu.roll(values, NZ - 1, 1)

    def downward(values):
        return pltpu.roll(values, 1, 1)

    def coefficients(speed, shape_lane=None):
        scaled = 0.1 * speed
        return 0.01 - scaled, 0.01 + scaled

    def vertical(speed, lanes):
        up, down = coefficients(speed)
        top, bottom = lanes == NZ - 1, lanes == 0
        centre = 0.94 + jnp.where(top, up, 0.0) + jnp.where(bottom, down, 0.0)
        return jnp.where(top, 0.0, up), jnp.where(bottom, 0.0, down), centre

    def advect_plane(x, fields):
        c_east, c_west = coefficients(fp[0, x + 1])
        c_north, c_south = coefficients(fp[1, x + 1])
        c_north = jnp.where(row == SY - 1, 0.0, c_north)
        c_south = jnp.where(row == 0, 0.0, c_south)
        c_up, c_down, c_mid = vertical(fp[2, x + 1], lane)
        for f in fields:
            centre = fp[f, x + 1]
            ad[f, x] = (
                (c_mid * centre + c_east * fp[f, x + 2] + c_west * fp[f, x])
                + (c_north * pltpu.roll(centre, SY - 1, 0) + c_south * pltpu.roll(centre, 1, 0))
                + (c_up * upward(centre) + c_down * downward(centre))
            )

    def inner(x, carry):
        advect_plane(x, (0, 1, 2))
        row_y0[pl.ds(x, 1), :] = fp[1, x + 1, 0:1, :]
        return carry

    lax.fori_loop(1, SX - 1, inner, 0)
    for copy in air:
        copy.start()

    for copy in drops:
        copy.wait()
    box_row = lax.broadcasted_iota(jnp.int32, (32, 32), 0)
    box_lane = lax.broadcasted_iota(jnp.int32, (32, 32), 1)
    spread = jnp.where(box_row == box_lane, cnt_v[...][None, :].astype(F32), 0.0)
    used = jnp.sum(spread, axis=1, keepdims=True)
    slot = lax.broadcasted_iota(jnp.int32, (32, 64), 1).astype(F32)
    live = jnp.where(slot < used, mul_v[...], 0.0)
    target = dst_v[...]
    local_box = lax.broadcasted_iota(jnp.int32, (32, 64), 0)
    source_x = gx * 4 + (local_box >> 3)
    source_y = gy * 8 + (local_box & 7)
    target_x = (target >> 8) * 4 + ((target & 31) >> 3)
    target_y = ((target >> 5) & 7) * 8 + (target & 7)
    offset_x = (target_x - source_x + 1) & 63
    offset_y = (target_y - source_y + 1) & 63
    code = (offset_x * 3 + offset_y).astype(F32)

    def twice(values):
        return jnp.concatenate([values, values], axis=1)

    pair = twice(pair_v[...])
    order = jnp.where(lax.broadcasted_iota(jnp.int32, (32, 128), 1) < 64, pair, pltpu.roll(pair, 32, 1))
    radius_p = jnp.take_along_axis(twice(rad_v[...]), order, axis=1)
    live_p = jnp.take_along_axis(twice(live), order, axis=1)
    code_p = jnp.take_along_axis(twice(code), order, axis=1)

    for x in (0, SX - 1):
        row_y0[pl.ds(x, 1), :] = fp[1, x + 1, 0:1, :]
    for copy in wind[3:6]:
        copy.wait_recv()

    speed_v = yl[1]
    row_x = lax.broadcasted_iota(jnp.int32, (SX, NZ), 0)
    lane_x = lax.broadcasted_iota(jnp.int32, (SX, NZ), 1)
    c_east, c_west = coefficients(yl[0])
    c_north, c_south = coefficients(speed_v)
    c_up, c_down, c_mid = vertical(yl[2], lane_x)
    after = jnp.where(row_x == SX - 1, 0.0, pltpu.roll(speed_v, SX - 1, 0))
    before = jnp.where(row_x == 0, 0.0, pltpu.roll(speed_v, 1, 0))
    below_y[...] = (
        (c_mid * speed_v + c_east * after + c_west * before)
        + (c_north * row_y0[...] + c_south * yl[5])
        + (c_up * upward(speed_v) + c_down * downward(speed_v))
    )
    fetches[0].wait()

    def border(x, fields):
        _, c_south = coefficients(fp[1, x + 1, 0:8, :])
        c_north, _ = coefficients(fp[1, x + 1, SY - 8 : SY, :])
        c_south = jnp.where(tile_row == 0, c_south, 0.0)
        c_north = jnp.where(tile_row == 7, c_north, 0.0)
        for f in fields:
            ad[f, x, 0:8, :] += c_south * yl[f, pl.ds(x, 1), :]
            ad[f, x, SY - 8 : SY, :] += c_north * yh[f, pl.ds(x, 1), :]

    def block(c):
        parts = []
        for i in range(4):
            x = c * 4 + i
            if x != 3:
                border(x, (0, 1, 2))
            star_w = ad[2, x] + 0.1 * fp[3, x + 1]
            ad[2, x] = star_w
            star_v = ad[1, x]
            star_u = ad[0, x]
            if i == 0:
                last_u = before_u[...] if c == 0 else ad[0, x - 1]
            behind_v = jnp.where(row == 0, below_y[pl.ds(x, 1), :], pltpu.roll(star_v, 1, 0))
            below_w = jnp.where(lane == 0, 0.0, downward(star_w))
            parts.append((star_u - last_u) + (star_v - behind_v) + (star_w - below_w))
            last_u = star_u
        chunk = jnp.concatenate(parts, axis=0)
        high, low = halves(chunk)
        wide = jnp.concatenate(
            [jnp.concatenate([high, high], axis=1), jnp.concatenate([low, jnp.zeros_like(low)], axis=1)],
            axis=0,
        )
        send1[c] = fold(one_product(cosine[...], wide, NT))

    def scalars(c, carry):
        total = jnp.zeros((SY, NZ), F32)
        for i in range(4):
            x = c * 4 + i
            advect_plane(x, (3, 4))
            border(x, (3, 4))
            total = total + ad[4, x]
        quad[c] = total
        return carry

    border(3, (0, 1, 2))
    block(1)
    block(2)
    for copy in wind[:3]:
        copy.wait_recv()
    advect_plane(0, (0, 1, 2))
    advect_plane(SX - 1, (0, 1, 2))

    for copy in wind[6:]:
        copy.wait_recv()
    _, end_west = coefficients(yl[0, 0:1, :])
    end_east, _ = coefficients(yl[0, SX - 1 : SX, :])
    below_y[0:1, :] += end_west * corner[2, 0:1, :]
    below_y[SX - 1 : SX, :] += end_east * corner[3, 0:1, :]

    speed = fp[0, 0]
    c_east, c_west = coefficients(speed)
    c_north, c_south = coefficients(fp[1, 0])
    c_up, c_down, c_mid = vertical(fp[2, 0], lane)
    above = jnp.where(row == SY - 1, corner[1, 0:1, :], pltpu.roll(speed, SY - 1, 0))
    beneath = jnp.where(row == 0, corner[0, 0:1, :], pltpu.roll(speed, 1, 0))
    before_u[...] = (
        (c_mid * speed + c_east * fp[0, 1] + c_west * xu2[...])
        + (c_north * above + c_south * beneath)
        + (c_up * upward(speed) + c_down * downward(speed))
    )
    block(0)
    block(3)
    pl.semaphore_wait(known.at[0], len(corners))

    def scatter(source, target_ref, send_sem, recv_sem):
        for step_z, step_x, step_y, step_core in send_order():
            px, py = peers_x[step_z][step_x], peers_y[step_y][step_core]
            pltpu.make_async_remote_copy(
                src_ref=source.at[:, pl.ds(px * GY + py, 1), :],
                dst_ref=target_ref.at[:, pl.ds(me, 1), :],
                send_sem=send_sem, recv_sem=recv_sem, device_id=(px, py), device_id_type=MESH,
            ).start()

    def drained(source, target_ref, sem):
        count = pl.ds(0, DEV - 1)
        pltpu.make_async_copy(source.at[:, count, :], target_ref.at[:, count, :], sem).wait()

    scatter(send1, got1, s1_sem, r1_sem)
    got1[:, pl.ds(me, 1), :] = send1[:, pl.ds(me, 1), :]

    for copy in air:
        copy.wait_recv()
    lax.fori_loop(0, 4, scalars, 0)
    fetches[1].wait()
    high, low = halves(quad[...].reshape(128, NZ))
    sums = lax.dot_general(box[...], high, (NN, ((), ())), preferred_element_type=F32)
    sums = sums + lax.dot_general(box[...], low, (NN, ((), ())), preferred_element_type=F32)
    mean = jnp.sum(sums, axis=1, keepdims=True) * (1.0 / (16 * NZ))
    soft = jnp.maximum(mean, 0.0) + jnp.log1p(jnp.exp(-jnp.abs(mean)))
    grown = radius_p + 0.5 * soft
    root = jnp.sqrt(grown)
    mass = grown * root
    gain = mass - radius_p * jnp.sqrt(radius_p)

    def other(values):
        return pltpu.roll(values, 64, 1)

    root_sum = root + other(root)
    rate = 0.05 * (root_sum * root_sum * jnp.abs(grown - other(grown)) * other(live_p))
    final = (mass + rate * other(mass)) / (1.0 + rate)
    lanes = lax.broadcasted_iota(jnp.int32, (32, 128), 1)
    own_live = jnp.where(lanes < 64, live_p, 0.0)
    cond[...] = jnp.broadcast_to(jnp.sum(own_live * gain, axis=1, keepdims=True), (32, 128)) * 0.002
    carried = [own_live, own_live * final, own_live * final * final]
    packed = jnp.zeros((32, 128), F32)
    for d in range(9):
        chosen = code_p == float(d)
        for k in range(3):
            amount = jnp.sum(jnp.where(chosen, carried[k], 0.0), axis=1, keepdims=True)
            packed = packed + jnp.where(lanes == d * 3 + k, amount, 0.0)
    load[...] = packed

    def share(source, target_ref, k, device):
        return pltpu.make_async_remote_copy(
            src_ref=source, dst_ref=target_ref, send_sem=ms_sem.at[k], recv_sem=mr_sem.at[k],
            device_id=device, device_id_type=MESH,
        )

    top, bottom = pl.ds(24, 8), pl.ds(0, 8)
    shares = [
        share(load.at[top], near.at[0, bottom], 0, (east, gy)),
        share(load.at[bottom], near.at[1, bottom], 1, (west, gy)),
        share(load, near.at[2], 2, (gx, north)),
        share(load, near.at[3], 3, (gx, south)),
        share(load.at[top], near.at[4, bottom], 4, (east, north)),
        share(load.at[top], near.at[5, bottom], 5, (east, south)),
        share(load.at[bottom], near.at[6, bottom], 6, (west, north)),
        share(load.at[bottom], near.at[7, bottom], 7, (west, south)),
    ]
    for copy in shares:
        copy.start()

    def dry(x, carry):
        first_box = (x // 4) * 8
        for t in range(4):
            drop = jnp.where(
                tile_row < 4,
                cond[pl.ds(first_box + 2 * t, 1), :],
                cond[pl.ds(first_box + 2 * t + 1, 1), :],
            )
            ad[4, x, 8 * t : 8 * t + 8, :] -= drop
        return carry

    lax.fori_loop(0, SX, dry, 0)

    for copy in fetches[2:]:
        copy.wait()
    drained(send1, got1, r1_sem)
    z_re, z_im = [], []
    for c in range(4):
        both = fold(one_product(first[c], packed_right(*halves(got1[c])), NN))
        z_re.append(both[:HALF])
        z_im.append(both[HALF:])

    def butterfly(re, im, sign):
        s02r, s02i = re[0] + re[2], im[0] + im[2]
        d02r, d02i = re[0] - re[2], im[0] - im[2]
        s13r, s13i = re[1] + re[3], im[1] + im[3]
        d13r, d13i = re[1] - re[3], im[1] - im[3]
        if sign < 0:
            return (
                [s02r + s13r, d02r + d13i, s02r - s13r, d02r - d13i],
                [s02i + s13i, d02i - d13r, s02i - s13i, d02i + d13r],
            )
        return (
            [s02r + s13r, d02r - d13i, s02r - s13r, d02r + d13i],
            [s02i + s13i, d02i + d13r, s02i - s13i, d02i - d13r],
        )

    def stacked_product(values, table):
        high, low = halves(values)
        both = one_product(jnp.concatenate([high, low], axis=0), table[0], NN)
        rows = values.shape[0]
        return both[:rows] + (both[rows:] + one_product(high, table[1], NN))

    q_re, q_im = butterfly(z_re, z_im, -1)
    back_re, back_im = [], []
    for q in range(0, 4, 2):
        part = pl.ds(HALF * q, HALF * 2)
        re, im = (jnp.concatenate(side[q : q + 2], axis=0) for side in (q_re, q_im))
        turn_cos, turn_sin = turns[0, part, :], turns[1, part, :]
        joined = jnp.concatenate([re * turn_cos + im * turn_sin, im * turn_cos - re * turn_sin], axis=1)
        spectrum = stacked_product(joined, ahead)
        eigen = turns[2, part, :] + wave[pl.ds(me, 1), :]
        inverse = jnp.where(eigen == 0.0, 0.0, 1.0 / jnp.where(eigen == 0.0, 1.0, eigen))
        turned = stacked_product(spectrum * jnp.concatenate([inverse, inverse], axis=1), behind)
        re, im = turned[:, :128], turned[:, 128:]
        turned_re, turned_im = re * turn_cos - im * turn_sin, im * turn_cos + re * turn_sin
        for k in range(2):
            back_re.append(turned_re[HALF * k : HALF * (k + 1)])
            back_im.append(turned_im[HALF * k : HALF * (k + 1)])
    v_re, v_im = butterfly(back_re, back_im, 1)
    wide_lane = lax.broadcasted_iota(jnp.int32, (128, 128), 1)
    edge = None
    for c in range(4):
        stacked = jnp.concatenate([v_re[c], v_im[c]], axis=0)
        high, low = halves(stacked)
        wide = one_product(last[c], jnp.concatenate([high, low], axis=1), NN)
        plane = wide[:128, :128] + (wide[:128, 128:] + wide[128:, :128])
        send2[c] = plane
        if c == 0:
            next_x = pltpu.roll(plane, 120, 0)
        picked = jnp.where((wide_lane & 31) == 0, plane, 0.0)
        picked = picked if c == 0 else pltpu.roll(picked, c, 1)
        edge = picked if edge is None else edge + picked
    row_b = lax.broadcasted_iota(jnp.int32, (128, 128), 0) & 7
    edge = jnp.where(row_b == 7, pltpu.roll(edge, 7, 0), pltpu.roll(edge, 127, 0))
    moved = pltpu.roll(edge, 36, 1)
    in_move = (wide_lane >= 36) & (wide_lane < 40)
    send2[4] = jnp.where(wide_lane < 32, next_x, jnp.where(in_move, moved, edge))

    scatter(send2, modes, s2_sem, r2_sem)
    modes[:, pl.ds(me, 1), :] = send2[:, pl.ds(me, 1), :]

    for copy in shares:
        copy.wait_recv()
    tile_lane = lax.broadcasted_iota(jnp.int32, (8, 128), 1)

    def column_of(x):
        if x < 0:
            return near[0, 0:8, :], near[4, 7:8, :], near[5, 0:1, :]
        if x > 3:
            return near[1, 0:8, :], near[6, 7:8, :], near[7, 0:1, :]
        return load[8 * x : 8 * x + 8, :], near[2, 8 * x + 7 : 8 * x + 8, :], near[3, 8 * x : 8 * x + 1, :]

    arrived = [jnp.zeros((8, 128), F32) for _ in range(4)]
    for x in range(-1, 5):
        centre, low_row, high_row = column_of(x)
        shifted = [
            jnp.where(tile_row == 7, high_row, pltpu.roll(centre, 7, 0)),
            centre,
            jnp.where(tile_row == 0, low_row, pltpu.roll(centre, 1, 0)),
        ]
        for dx in (-1, 0, 1):
            if not 0 <= x + dx < 4:
                continue
            for dy in (-1, 0, 1):
                d = (dx + 1) * 3 + dy + 1
                values = shifted[dy + 1]
                values = values if d == 0 else pltpu.roll(values, 128 - 3 * d, 1)
                arrived[x + dx] = arrived[x + dx] + values
    stacked = jnp.concatenate(arrived + [jnp.zeros((96, 128), F32)], axis=0) * (1.0 / 64)
    moments_out[...] = stacked.T[0:8, :]

    for copy in halo:
        copy.wait_send()
    for copy in shares:
        copy.wait_send()
    drained(send1, got1, s1_sem)
    drained(send2, send2, s2_sem)
    drained(send2, modes, r2_sem)


def final_kernel(
    modes, ad, moments, back,
    vel_out, theta_out, vapour_out, moments_out,
    fresh, mom_o, pressure, out_sem,
):
    mom_o[...] = moments[0:3, 0:32]
    outs = [
        pltpu.make_async_copy(ad.at[3], theta_out, out_sem.at[0]),
        pltpu.make_async_copy(ad.at[4], vapour_out, out_sem.at[1]),
        pltpu.make_async_copy(mom_o, moments_out, out_sem.at[2]),
    ]
    for copy in outs:
        copy.start()
    row = lax.broadcasted_iota(jnp.int32, (SY, NZ), 0)
    lane = lax.broadcasted_iota(jnp.int32, (SY, NZ), 1)

    def levels(c):
        wide = one_product(jnp.concatenate(halves(modes[c]), axis=0), back[...], TN)
        pressure[pl.ds(128 * c, 128), :] = fold(wide)

    levels(4)
    for c in (3, 2, 1, 0):
        levels(c)
        for i in range(4):
            x = 4 * c + i
            here = pressure[pl.ds(32 * x, 32), :]
            ahead = pressure[pl.ds(32 * x + 32, 32), :]
            line = 512 + (36, 32, 64, 96)[i] + c
            side = jnp.where(row == SY - 1, pressure[line : line + 1, :], pltpu.roll(here, SY - 1, 0))
            above = jnp.where(lane == NZ - 1, here, pltpu.roll(here, NZ - 1, 1))
            fresh[0, x] = ad[0, x] - (ahead - here)
            fresh[1, x] = ad[1, x] - (side - here)
            fresh[2, x] = ad[2, x] - (above - here)
        part = pl.ds(4 * c, 4)
        copy = pltpu.make_async_copy(fresh.at[:, part], vel_out.at[:, part], out_sem.at[3 + c])
        copy.start()
        outs.append(copy)
    for copy in outs:
        copy.wait()


def shards(velocity, theta, vapour, radius_sq, multiplicity, counts, pairing, destination):
    t = tables()
    names = ["cosine", "first", "ahead", "behind", "last", "turns", "wave_z", "box"]
    held = [jnp.asarray(t[name]) for name in names]
    block = (SX, SY, NZ)
    shape = jax.ShapeDtypeStruct
    vmem = pltpu.VMEM
    dma = pltpu.SemaphoreType.DMA
    here = pl.BlockSpec(memory_space=pltpu.VMEM)
    modes, advected, moments = pl.pallas_call(
        step_kernel,
        out_shape=(
            vmem((5, DEV, 128), F32),
            vmem((5,) + block, F32),
            vmem((8, 128), F32),
        ),
        in_specs=[ANY] * 16,
        out_specs=(here,) * 3,
        scratch_shapes=[
            vmem((5, SX + 2, SY, NZ), F32),
            vmem((SY, NZ), F32),
            vmem((SY, NZ), F32),
            vmem((6, SX, NZ), F32),
            vmem((5, SX, NZ), F32),
            vmem((4, 8, NZ), F32),
            vmem((SX, NZ), F32),
            vmem((SX, NZ), F32),
            vmem((4, SY, NZ), F32),
            vmem((4, DEV, 128), F32),
            vmem((4, DEV, 128), F32),
            vmem((5, DEV, 128), F32),
        ]
        + [vmem(t[name].shape, t[name].dtype) for name in names]
        + [
            vmem((32, 64), F32),
            vmem((32, 64), F32),
            vmem((32,), jnp.int32),
            vmem((32, 64), jnp.int32),
            vmem((32, 64), jnp.int32),
            vmem((32, 128), F32),
            vmem((32, 128), F32),
            vmem((8, 32, 128), F32),
            pltpu.SemaphoreType.REGULAR((1,)),
            dma((3,)),
            dma((5,)),
            dma((8,)),
            dma((18,)),
            dma((18,)),
            dma(()),
            dma(()),
            dma(()),
            dma(()),
            dma((8,)),
            dma((8,)),
        ],
        compiler_params=pltpu.CompilerParams(
            has_side_effects=True, collective_id=1, vmem_limit_bytes=24 << 20
        ),
        name="cloud_step",
    )(*[
        pltpu.with_memory_space_constraint(value, pltpu.HBM)
        for value in (
            velocity, theta, vapour, radius_sq.T, multiplicity.T, counts, pairing, destination.T, *held
        )
    ])
    return pl.pallas_call(
        final_kernel,
        out_shape=(
            shape((3,) + block, F32),
            shape(block, F32),
            shape(block, F32),
            shape((3, 32), F32),
        ),
        in_specs=[here] * 4,
        out_specs=(ANY,) * 4,
        scratch_shapes=[
            vmem((3,) + block, F32),
            vmem((3, 32), F32),
            vmem((640, 128), F32),
            dma((7,)),
        ],
        compiler_params=pltpu.CompilerParams(vmem_limit_bytes=12 << 20),
        name="project",
    )(
        *[pltpu.with_memory_space_constraint(value, pltpu.VMEM) for value in (modes, advected, moments)],
        jnp.asarray(t["back"]),
    )


def solution(mesh):
    placed = (
        P(None, "gx", "gy", None),
        P("gx", "gy", None),
        P("gx", "gy", None),
        P(None, ("gx", "gy")),
        P(None, ("gx", "gy")),
        P(("gx", "gy")),
        P(("gx", "gy"), None),
        P(None, ("gx", "gy")),
    )
    return jax.shard_map(
        shards,
        mesh=mesh,
        in_specs=placed,
        out_specs=(
            P(None, "gx", "gy", None),
            P("gx", "gy", None),
            P("gx", "gy", None),
            P(None, ("gx", "gy")),
        ),
        check_vma=False,
    )
```

```python
import functools
import math

import jax
import jax.numpy as jnp
import numpy as np
from jax import lax
from jax.experimental import pallas as pl
from jax.experimental.pallas import tpu as pltpu
from jax.sharding import PartitionSpec as P

MESH = pl.DeviceIdType.MESH
GX, GY = 16, 8
DEV = GX * GY
SX, SY, NZ = 16, 32, 128
NX, NY = 256, 256
HALF = 72
F32 = jnp.float32
BF16 = jnp.bfloat16
ANY = pl.BlockSpec(memory_space=pl.ANY)


def split_table(table):
    table = np.asarray(table, np.float32)
    high = table.astype(jnp.bfloat16)
    low = (table - high.astype(np.float32)).astype(jnp.bfloat16)
    return np.stack([high, low])


@functools.cache
def send_order():
    hops = (0, 1, 2, 1)
    ways = ((0, 0), (1, 0), (1, 1), (0, 1))
    left = [(k, i, j, n) for k in range(4) for i in range(4) for j in range(4) for n in range(2)][1:]
    used, order = [0] * 6, []

    def after(peer):
        return [u + w for u, w in zip(used, sum((ways[step] for step in peer[:3]), ()))]

    while left:
        far = max(sum(hops[step] for step in peer[:3]) for peer in left)
        ring = [peer for peer in left if sum(hops[step] for step in peer[:3]) == far]
        best = min(ring, key=lambda peer: (max(after(peer)), sum(u * u for u in after(peer))))
        used = after(best)
        order.append(best)
        left.remove(best)
    return tuple(order)


@functools.cache
def tables():
    tau = 2.0 * math.pi
    z = np.arange(NZ)
    cosine = np.cos(math.pi * (z[None, :] + 0.5) * z[:, None] / NZ)
    weight = np.where(z == 0, 1.0 / NZ, 2.0 / NZ)
    back = cosine * weight[:, None]
    rows, factor, seen = [], [], set()
    for p in range(16):
        for q in range(8):
            if (p, q) in seen:
                continue
            mirror = (-p % 16, -q % 8)
            seen.update({(p, q), mirror})
            rows.append((p, q))
            factor.append(1.0 if mirror == (p, q) else 2.0)
    pad = HALF - len(rows)
    low_x = np.array([r[0] for r in rows] + [0] * pad)
    low_y = np.array([r[1] for r in rows] + [0] * pad)
    factor = np.array(factor + [0.0] * pad)
    used = np.array([1.0] * len(rows) + [0.0] * pad)
    a = np.repeat(np.arange(16), 8)
    b = np.tile(np.arange(8), 16)
    first, last = [], []
    for c in range(4):
        angle = tau * (
            low_x[:, None] * a[None] / 16.0
            + low_y[:, None] * b[None] / 8.0
            + low_x[:, None] * c / 64.0
        )
        first.append(np.concatenate([np.cos(angle) * used[:, None], -np.sin(angle) * used[:, None]]))
        scale = factor[:, None] / (NX * NY)
        last.append(np.concatenate([np.cos(angle) * scale, -np.sin(angle) * scale]).T)
    lane_i = np.repeat(np.arange(4), 32)
    lane_j = np.tile(np.arange(32), 4)
    turn_cos, turn_sin, wave = [], [], []
    for q in range(4):
        kx0 = low_x + 16 * q
        angle = tau * (kx0[:, None] * lane_i[None] + low_y[:, None] * lane_j[None]) / 256.0
        turn_cos.append(np.cos(angle))
        turn_sin.append(np.sin(angle))
        kx = kx0[:, None] + 64 * lane_i[None]
        ky = low_y[:, None] + 8 * lane_j[None]
        wave.append(-4.0 * np.sin(math.pi * kx / NX) ** 2 - 4.0 * np.sin(math.pi * ky / NY) ** 2)
    turns = np.stack([np.concatenate(turn_cos), np.concatenate(turn_sin), np.concatenate(wave)])
    angle = tau * (lane_i[:, None] * lane_i[None] / 4.0 + lane_j[:, None] * lane_j[None] / 32.0)
    cos2, sin2 = np.cos(angle), np.sin(angle)
    ahead = np.block([[cos2, -sin2], [sin2, cos2]])
    behind = np.block([[cos2, sin2], [-sin2, cos2]])
    wave_z = -4.0 * np.sin(math.pi * z / (2.0 * NZ)) ** 2
    wave_z = np.broadcast_to(wave_z[:, None], (NZ, 128)).astype(np.float32)
    box = np.zeros((32, 128), np.float32)
    for column in range(4):
        for j in range(32):
            box[column * 8 + j // 4, column * 32 + j] = 1.0
    return dict(
        cosine=packed_left(cosine),
        first=packed_left(np.stack(first)),
        ahead=split_table(ahead),
        behind=split_table(behind),
        last=np.concatenate(list(split_table(np.stack(last))), axis=1),
        turns=turns.astype(np.float32),
        wave_z=wave_z,
        box=box.astype(jnp.bfloat16),
        back=np.block([[*split_table(back)], [split_table(back)[0], np.zeros((NZ, NZ), jnp.bfloat16)]]),
    )


def halves(values):
    high = values.astype(BF16)
    return high, (values - high.astype(F32)).astype(BF16)


def product(left, right, dims):
    def one(x, y):
        return lax.dot_general(x, y, (dims, ((), ())), preferred_element_type=F32)

    (left_high, left_low), (right_high, right_low) = left, right
    return one(left_high, right_high) + (one(left_high, right_low) + one(left_low, right_high))


def packed_left(table):
    high, low = split_table(table)
    return np.concatenate([high, low], axis=-1)


def fold(wide):
    return wide[:, :128] + wide[:, 128:]


def packed_right(high, low):
    zero = jnp.zeros_like(low)
    return jnp.concatenate(
        [jnp.concatenate([high, low], axis=1), jnp.concatenate([high, zero], axis=1)], axis=0
    )


def one_product(left, right, dims):
    return lax.dot_general(left, right, (dims, ((), ())), preferred_element_type=F32)


NN = ((1,), (0,))
NT = ((1,), (1,))
TN = ((0,), (0,))


def step_kernel(
    vel, theta, vapour, radius, multi, counts, pairing, dest,
    cosine_h, first_h, ahead_h, behind_h, last_h, turns_h, wave_h, box_h,
    modes, ad, moments_out,
    fp, before_u, xu2, yl, yh, corner, row_y0, below_y, quad, send1, got1, send2,
    cosine, first, ahead, behind, last, turns, wave, box,
    rad_v, mul_v, cnt_v, pair_v, dst_v, cond, load, near,
    known, load_sem, drop_sem, table_sem, hs_sem, hr_sem, s1_sem, r1_sem, s2_sem, r2_sem,
    ms_sem, mr_sem,
):
    gx = lax.axis_index("gx")
    gy = lax.axis_index("gy")
    me = gx * GY + gy
    east, west = lax.rem(gx + 1, GX), lax.rem(gx + GX - 1, GX)
    north, south = lax.rem(gy + 1, GY), lax.rem(gy + GY - 1, GY)

    loads = [
        pltpu.make_async_copy(vel, fp.at[pl.ds(0, 3), pl.ds(1, SX)], load_sem.at[0]),
        pltpu.make_async_copy(theta, fp.at[3, pl.ds(1, SX)], load_sem.at[1]),
        pltpu.make_async_copy(vapour, fp.at[4, pl.ds(1, SX)], load_sem.at[2]),
    ]
    drops = [
        pltpu.make_async_copy(source, target, drop_sem.at[k])
        for k, (source, target) in enumerate(
            [(radius, rad_v), (multi, mul_v), (counts, cnt_v), (pairing, pair_v), (dest, dst_v)]
        )
    ]
    table_pairs = [
        (cosine_h, cosine), (box_h, box), (first_h, first), (turns_h, turns), (ahead_h, ahead),
        (wave_h, wave), (behind_h, behind), (last_h, last),
    ]
    fetches = [
        pltpu.make_async_copy(source, target, table_sem.at[k])
        for k, (source, target) in enumerate(table_pairs)
    ]
    for copy in loads + drops + fetches:
        copy.start()

    barrier = pltpu.get_barrier_semaphore()

    chip_z, chip_x, chip_y, core = gx // 4, lax.rem(gx, 4), gy // 2, lax.rem(gy, 2)

    peers_x = [[lax.rem(chip_z + k, 4) * 4 + lax.rem(chip_x + i, 4) for i in range(4)] for k in range(4)]
    peers_y = [[lax.rem(chip_y + j, 4) * 2 + lax.rem(core + n, 2) for n in range(2)] for j in range(4)]

    def away(step_z, step_x, step_y, step_core):
        return peers_x[step_z % 4][step_x % 4], peers_y[step_y % 4][step_core]

    steps = [(k, i, j, n) for k in (0, 1, -1) for i in (1, -1, 0) for j in (1, -1, 0) for n in (0, 1)]
    steps.sort(key=lambda step: -sum(map(abs, step[:3])))
    around = [away(*step) for step in steps if any(step)]
    corners = [away(k, i, j, 0) for k in (1, -1) for i in (1, -1) for j in (1, -1)]
    for device in around:
        pl.semaphore_signal(barrier, inc=1, device_id=device, device_id_type=MESH)
    pl.semaphore_wait(barrier, len(around))

    def remote(source, target_ref, k, device):
        return pltpu.make_async_remote_copy(
            src_ref=source, dst_ref=target_ref, send_sem=hs_sem.at[k], recv_sem=hr_sem.at[k],
            device_id=device, device_id_type=MESH,
        )

    winds = fp.at[pl.ds(0, 3)]
    wind = [
        remote(winds.at[:, SX], fp.at[pl.ds(0, 3), 0], 0, (east, gy)),
        remote(winds.at[:, 1], fp.at[pl.ds(0, 3), SX + 1], 1, (west, gy)),
        remote(fp.at[0, SX - 1], xu2, 2, (east, gy)),
        remote(winds.at[:, pl.ds(1, SX), SY - 1], yl.at[pl.ds(0, 3)], 3, (gx, north)),
        remote(winds.at[:, pl.ds(1, SX), 0], yh.at[pl.ds(0, 3)], 4, (gx, south)),
        remote(fp.at[1, pl.ds(1, SX), SY - 2], yl.at[5], 5, (gx, north)),
        remote(fp.at[0, SX, pl.ds(SY - 1, 1)], corner.at[0, pl.ds(0, 1)], 6, (east, north)),
        remote(fp.at[0, SX, pl.ds(0, 1)], corner.at[1, pl.ds(0, 1)], 7, (east, south)),
        remote(fp.at[1, SX, pl.ds(SY - 1, 1)], corner.at[2, pl.ds(0, 1)], 8, (east, north)),
        remote(fp.at[1, 1, pl.ds(SY - 1, 1)], corner.at[3, pl.ds(0, 1)], 9, (west, north)),
    ]
    air = [
        remote(fp.at[3, SX], fp.at[3, 0], 10, (east, gy)),
        remote(fp.at[4, SX], fp.at[4, 0], 11, (east, gy)),
        remote(fp.at[3, 1], fp.at[3, SX + 1], 12, (west, gy)),
        remote(fp.at[4, 1], fp.at[4, SX + 1], 13, (west, gy)),
        remote(fp.at[3, pl.ds(1, SX), SY - 1], yl.at[3], 14, (gx, north)),
        remote(fp.at[4, pl.ds(1, SX), SY - 1], yl.at[4], 15, (gx, north)),
        remote(fp.at[3, pl.ds(1, SX), 0], yh.at[3], 16, (gx, south)),
        remote(fp.at[4, pl.ds(1, SX), 0], yh.at[4], 17, (gx, south)),
    ]
    halo = wind + air
    loads[0].wait()
    for copy in wind[6:] + wind[:6]:
        copy.start()

    def pass_on(k, devices):
        for device in devices:
            pl.semaphore_signal(known.at[k], inc=1, device_id=device, device_id_type=MESH)

    pass_on(0, corners)
    for copy in loads[1:]:
        copy.wait()

    row = lax.broadcasted_iota(jnp.int32, (SY, NZ), 0)
    lane = lax.broadcasted_iota(jnp.int32, (SY, NZ), 1)
    tile_row = lax.broadcasted_iota(jnp.int32, (8, NZ), 0)

    def upward(values):
        return pltpu.roll(values, NZ - 1, 1)

    def downward(values):
        return pltpu.roll(values, 1, 1)

    def coefficients(speed, shape_lane=None):
        scaled = 0.1 * speed
        return 0.01 - scaled, 0.01 + scaled

    def vertical(speed, lanes):
        up, down = coefficients(speed)
        top, bottom = lanes == NZ - 1, lanes == 0
        centre = 0.94 + jnp.where(top, up, 0.0) + jnp.where(bottom, down, 0.0)
        return jnp.where(top, 0.0, up), jnp.where(bottom, 0.0, down), centre

    def advect_plane(x, fields):
        c_east, c_west = coefficients(fp[0, x + 1])
        c_north, c_south = coefficients(fp[1, x + 1])
        c_north = jnp.where(row == SY - 1, 0.0, c_north)
        c_south = jnp.where(row == 0, 0.0, c_south)
        c_up, c_down, c_mid = vertical(fp[2, x + 1], lane)
        for f in fields:
            centre = fp[f, x + 1]
            ad[f, x] = (
                (c_mid * centre + c_east * fp[f, x + 2] + c_west * fp[f, x])
                + (c_north * pltpu.roll(centre, SY - 1, 0) + c_south * pltpu.roll(centre, 1, 0))
                + (c_up * upward(centre) + c_down * downward(centre))
            )

    def inner(x, carry):
        advect_plane(x, (0, 1, 2))
        row_y0[pl.ds(x, 1), :] = fp[1, x + 1, 0:1, :]
        return carry

    lax.fori_loop(1, SX - 1, inner, 0)
    for copy in air:
        copy.start()

    for copy in drops:
        copy.wait()
    box_row = lax.broadcasted_iota(jnp.int32, (32, 32), 0)
    box_lane = lax.broadcasted_iota(jnp.int32, (32, 32), 1)
    spread = jnp.where(box_row == box_lane, cnt_v[...][None, :].astype(F32), 0.0)
    used = jnp.sum(spread, axis=1, keepdims=True)
    slot = lax.broadcasted_iota(jnp.int32, (32, 64), 1).astype(F32)
    live = jnp.where(slot < used, mul_v[...], 0.0)
    target = dst_v[...]
    local_box = lax.broadcasted_iota(jnp.int32, (32, 64), 0)
    source_x = gx * 4 + (local_box >> 3)
    source_y = gy * 8 + (local_box & 7)
    target_x = (target >> 8) * 4 + ((target & 31) >> 3)
    target_y = ((target >> 5) & 7) * 8 + (target & 7)
    offset_x = (target_x - source_x + 1) & 63
    offset_y = (target_y - source_y + 1) & 63
    code = (offset_x * 3 + offset_y).astype(F32)

    def twice(values):
        return jnp.concatenate([values, values], axis=1)

    pair = twice(pair_v[...])
    order = jnp.where(lax.broadcasted_iota(jnp.int32, (32, 128), 1) < 64, pair, pltpu.roll(pair, 32, 1))
    radius_p = jnp.take_along_axis(twice(rad_v[...]), order, axis=1)
    live_p = jnp.take_along_axis(twice(live), order, axis=1)
    code_p = jnp.take_along_axis(twice(code), order, axis=1)

    for x in (0, SX - 1):
        row_y0[pl.ds(x, 1), :] = fp[1, x + 1, 0:1, :]
    for copy in wind:
        copy.wait_recv()
    advect_plane(0, (0, 1, 2))
    advect_plane(SX - 1, (0, 1, 2))

    speed = fp[0, 0]
    c_east, c_west = coefficients(speed)
    c_north, c_south = coefficients(fp[1, 0])
    c_up, c_down, c_mid = vertical(fp[2, 0], lane)
    above = jnp.where(row == SY - 1, corner[1, 0:1, :], pltpu.roll(speed, SY - 1, 0))
    beneath = jnp.where(row == 0, corner[0, 0:1, :], pltpu.roll(speed, 1, 0))
    before_u[...] = (
        (c_mid * speed + c_east * fp[0, 1] + c_west * xu2[...])
        + (c_north * above + c_south * beneath)
        + (c_up * upward(speed) + c_down * downward(speed))
    )
    speed = yl[1]
    row_x = lax.broadcasted_iota(jnp.int32, (SX, NZ), 0)
    lane_x = lax.broadcasted_iota(jnp.int32, (SX, NZ), 1)
    c_east, c_west = coefficients(yl[0])
    c_north, c_south = coefficients(speed)
    c_up, c_down, c_mid = vertical(yl[2], lane_x)
    after = jnp.where(row_x == SX - 1, corner[3, 0:1, :], pltpu.roll(speed, SX - 1, 0))
    before = jnp.where(row_x == 0, corner[2, 0:1, :], pltpu.roll(speed, 1, 0))
    below_y[...] = (
        (c_mid * speed + c_east * after + c_west * before)
        + (c_north * row_y0[...] + c_south * yl[5])
        + (c_up * upward(speed) + c_down * downward(speed))
    )
    fetches[0].wait()

    def border(x, fields):
        _, c_south = coefficients(fp[1, x + 1, 0:8, :])
        c_north, _ = coefficients(fp[1, x + 1, SY - 8 : SY, :])
        c_south = jnp.where(tile_row == 0, c_south, 0.0)
        c_north = jnp.where(tile_row == 7, c_north, 0.0)
        for f in fields:
            ad[f, x, 0:8, :] += c_south * yl[f, pl.ds(x, 1), :]
            ad[f, x, SY - 8 : SY, :] += c_north * yh[f, pl.ds(x, 1), :]

    def block(c):
        parts = []
        for i in range(4):
            x = c * 4 + i
            border(x, (0, 1, 2))
            star_w = ad[2, x] + 0.1 * fp[3, x + 1]
            ad[2, x] = star_w
            star_v = ad[1, x]
            star_u = ad[0, x]
            if i == 0:
                last_u = before_u[...] if c == 0 else ad[0, x - 1]
            behind_v = jnp.where(row == 0, below_y[pl.ds(x, 1), :], pltpu.roll(star_v, 1, 0))
            below_w = jnp.where(lane == 0, 0.0, downward(star_w))
            parts.append((star_u - last_u) + (star_v - behind_v) + (star_w - below_w))
            last_u = star_u
        chunk = jnp.concatenate(parts, axis=0)
        high, low = halves(chunk)
        wide = jnp.concatenate(
            [jnp.concatenate([high, high], axis=1), jnp.concatenate([low, jnp.zeros_like(low)], axis=1)],
            axis=0,
        )
        send1[c] = fold(one_product(cosine[...], wide, NT))

    def scalars(c, carry):
        total = jnp.zeros((SY, NZ), F32)
        for i in range(4):
            x = c * 4 + i
            advect_plane(x, (3, 4))
            border(x, (3, 4))
            total = total + ad[4, x]
        quad[c] = total
        return carry

    for c in range(4):
        block(c)
    pl.semaphore_wait(known.at[0], len(corners))

    def scatter(source, target_ref, send_sem, recv_sem):
        for step_z, step_x, step_y, step_core in send_order():
            px, py = peers_x[step_z][step_x], peers_y[step_y][step_core]
            pltpu.make_async_remote_copy(
                src_ref=source.at[:, pl.ds(px * GY + py, 1), :],
                dst_ref=target_ref.at[:, pl.ds(me, 1), :],
                send_sem=send_sem, recv_sem=recv_sem, device_id=(px, py), device_id_type=MESH,
            ).start()

    def drained(source, target_ref, sem):
        count = pl.ds(0, DEV - 1)
        pltpu.make_async_copy(source.at[:, count, :], target_ref.at[:, count, :], sem).wait()

    scatter(send1, got1, s1_sem, r1_sem)
    got1[:, pl.ds(me, 1), :] = send1[:, pl.ds(me, 1), :]

    for copy in air:
        copy.wait_recv()
    lax.fori_loop(0, 4, scalars, 0)
    fetches[1].wait()
    high, low = halves(quad[...].reshape(128, NZ))
    sums = lax.dot_general(box[...], high, (NN, ((), ())), preferred_element_type=F32)
    sums = sums + lax.dot_general(box[...], low, (NN, ((), ())), preferred_element_type=F32)
    mean = jnp.sum(sums, axis=1, keepdims=True) * (1.0 / (16 * NZ))
    soft = jnp.maximum(mean, 0.0) + jnp.log1p(jnp.exp(-jnp.abs(mean)))
    grown = radius_p + 0.5 * soft
    root = jnp.sqrt(grown)
    mass = grown * root
    gain = mass - radius_p * jnp.sqrt(radius_p)

    def other(values):
        return pltpu.roll(values, 64, 1)

    root_sum = root + other(root)
    rate = 0.05 * (root_sum * root_sum * jnp.abs(grown - other(grown)) * other(live_p))
    final = (mass + rate * other(mass)) / (1.0 + rate)
    lanes = lax.broadcasted_iota(jnp.int32, (32, 128), 1)
    own_live = jnp.where(lanes < 64, live_p, 0.0)
    cond[...] = jnp.broadcast_to(jnp.sum(own_live * gain, axis=1, keepdims=True), (32, 128)) * 0.002
    carried = [own_live, own_live * final, own_live * final * final]
    packed = jnp.zeros((32, 128), F32)
    for d in range(9):
        chosen = code_p == float(d)
        for k in range(3):
            amount = jnp.sum(jnp.where(chosen, carried[k], 0.0), axis=1, keepdims=True)
            packed = packed + jnp.where(lanes == d * 3 + k, amount, 0.0)
    load[...] = packed

    def share(source, target_ref, k, device):
        return pltpu.make_async_remote_copy(
            src_ref=source, dst_ref=target_ref, send_sem=ms_sem.at[k], recv_sem=mr_sem.at[k],
            device_id=device, device_id_type=MESH,
        )

    top, bottom = pl.ds(24, 8), pl.ds(0, 8)
    shares = [
        share(load.at[top], near.at[0, bottom], 0, (east, gy)),
        share(load.at[bottom], near.at[1, bottom], 1, (west, gy)),
        share(load, near.at[2], 2, (gx, north)),
        share(load, near.at[3], 3, (gx, south)),
        share(load.at[top], near.at[4, bottom], 4, (east, north)),
        share(load.at[top], near.at[5, bottom], 5, (east, south)),
        share(load.at[bottom], near.at[6, bottom], 6, (west, north)),
        share(load.at[bottom], near.at[7, bottom], 7, (west, south)),
    ]
    for copy in shares:
        copy.start()

    def dry(x, carry):
        first_box = (x // 4) * 8
        for t in range(4):
            drop = jnp.where(
                tile_row < 4,
                cond[pl.ds(first_box + 2 * t, 1), :],
                cond[pl.ds(first_box + 2 * t + 1, 1), :],
            )
            ad[4, x, 8 * t : 8 * t + 8, :] -= drop
        return carry

    lax.fori_loop(0, SX, dry, 0)

    for copy in fetches[2:]:
        copy.wait()
    drained(send1, got1, r1_sem)
    z_re, z_im = [], []
    for c in range(4):
        both = fold(one_product(first[c], packed_right(*halves(got1[c])), NN))
        z_re.append(both[:HALF])
        z_im.append(both[HALF:])

    def butterfly(re, im, sign):
        s02r, s02i = re[0] + re[2], im[0] + im[2]
        d02r, d02i = re[0] - re[2], im[0] - im[2]
        s13r, s13i = re[1] + re[3], im[1] + im[3]
        d13r, d13i = re[1] - re[3], im[1] - im[3]
        if sign < 0:
            return (
                [s02r + s13r, d02r + d13i, s02r - s13r, d02r - d13i],
                [s02i + s13i, d02i - d13r, s02i - s13i, d02i + d13r],
            )
        return (
            [s02r + s13r, d02r - d13i, s02r - s13r, d02r + d13i],
            [s02i + s13i, d02i + d13r, s02i - s13i, d02i - d13r],
        )

    def stacked_product(values, table):
        high, low = halves(values)
        both = one_product(jnp.concatenate([high, low], axis=0), table[0], NN)
        rows = values.shape[0]
        return both[:rows] + (both[rows:] + one_product(high, table[1], NN))

    q_re, q_im = butterfly(z_re, z_im, -1)
    back_re, back_im = [], []
    for q in range(0, 4, 2):
        part = pl.ds(HALF * q, HALF * 2)
        re, im = (jnp.concatenate(side[q : q + 2], axis=0) for side in (q_re, q_im))
        turn_cos, turn_sin = turns[0, part, :], turns[1, part, :]
        joined = jnp.concatenate([re * turn_cos + im * turn_sin, im * turn_cos - re * turn_sin], axis=1)
        spectrum = stacked_product(joined, ahead)
        eigen = turns[2, part, :] + wave[pl.ds(me, 1), :]
        inverse = jnp.where(eigen == 0.0, 0.0, 1.0 / jnp.where(eigen == 0.0, 1.0, eigen))
        turned = stacked_product(spectrum * jnp.concatenate([inverse, inverse], axis=1), behind)
        re, im = turned[:, :128], turned[:, 128:]
        turned_re, turned_im = re * turn_cos - im * turn_sin, im * turn_cos + re * turn_sin
        for k in range(2):
            back_re.append(turned_re[HALF * k : HALF * (k + 1)])
            back_im.append(turned_im[HALF * k : HALF * (k + 1)])
    v_re, v_im = butterfly(back_re, back_im, 1)
    wide_lane = lax.broadcasted_iota(jnp.int32, (128, 128), 1)
    edge = None
    for c in range(4):
        stacked = jnp.concatenate([v_re[c], v_im[c]], axis=0)
        high, low = halves(stacked)
        wide = one_product(last[c], jnp.concatenate([high, low], axis=1), NN)
        plane = wide[:128, :128] + (wide[:128, 128:] + wide[128:, :128])
        send2[c] = plane
        if c == 0:
            next_x = pltpu.roll(plane, 120, 0)
        picked = jnp.where((wide_lane & 31) == 0, plane, 0.0)
        picked = picked if c == 0 else pltpu.roll(picked, c, 1)
        edge = picked if edge is None else edge + picked
    row_b = lax.broadcasted_iota(jnp.int32, (128, 128), 0) & 7
    edge = jnp.where(row_b == 7, pltpu.roll(edge, 7, 0), pltpu.roll(edge, 127, 0))
    moved = pltpu.roll(edge, 36, 1)
    in_move = (wide_lane >= 36) & (wide_lane < 40)
    send2[4] = jnp.where(wide_lane < 32, next_x, jnp.where(in_move, moved, edge))

    scatter(send2, modes, s2_sem, r2_sem)
    modes[:, pl.ds(me, 1), :] = send2[:, pl.ds(me, 1), :]

    for copy in shares:
        copy.wait_recv()
    tile_lane = lax.broadcasted_iota(jnp.int32, (8, 128), 1)

    def column_of(x):
        if x < 0:
            return near[0, 0:8, :], near[4, 7:8, :], near[5, 0:1, :]
        if x > 3:
            return near[1, 0:8, :], near[6, 7:8, :], near[7, 0:1, :]
        return load[8 * x : 8 * x + 8, :], near[2, 8 * x + 7 : 8 * x + 8, :], near[3, 8 * x : 8 * x + 1, :]

    arrived = [jnp.zeros((8, 128), F32) for _ in range(4)]
    for x in range(-1, 5):
        centre, low_row, high_row = column_of(x)
        shifted = [
            jnp.where(tile_row == 7, high_row, pltpu.roll(centre, 7, 0)),
            centre,
            jnp.where(tile_row == 0, low_row, pltpu.roll(centre, 1, 0)),
        ]
        for dx in (-1, 0, 1):
            if not 0 <= x + dx < 4:
                continue
            for dy in (-1, 0, 1):
                d = (dx + 1) * 3 + dy + 1
                values = shifted[dy + 1]
                values = values if d == 0 else pltpu.roll(values, 128 - 3 * d, 1)
                arrived[x + dx] = arrived[x + dx] + values
    stacked = jnp.concatenate(arrived + [jnp.zeros((96, 128), F32)], axis=0) * (1.0 / 64)
    moments_out[...] = stacked.T[0:8, :]

    for copy in halo:
        copy.wait_send()
    for copy in shares:
        copy.wait_send()
    drained(send1, got1, s1_sem)
    drained(send2, send2, s2_sem)
    drained(send2, modes, r2_sem)


def final_kernel(
    modes, ad, moments, back,
    vel_out, theta_out, vapour_out, moments_out,
    fresh, mom_o, pressure, out_sem,
):
    mom_o[...] = moments[0:3, 0:32]
    outs = [
        pltpu.make_async_copy(ad.at[3], theta_out, out_sem.at[0]),
        pltpu.make_async_copy(ad.at[4], vapour_out, out_sem.at[1]),
        pltpu.make_async_copy(mom_o, moments_out, out_sem.at[2]),
    ]
    for copy in outs:
        copy.start()
    row = lax.broadcasted_iota(jnp.int32, (SY, NZ), 0)
    lane = lax.broadcasted_iota(jnp.int32, (SY, NZ), 1)

    def levels(c):
        wide = one_product(jnp.concatenate(halves(modes[c]), axis=0), back[...], TN)
        pressure[pl.ds(128 * c, 128), :] = fold(wide)

    levels(4)
    for c in (3, 2, 1, 0):
        levels(c)
        for i in range(4):
            x = 4 * c + i
            here = pressure[pl.ds(32 * x, 32), :]
            ahead = pressure[pl.ds(32 * x + 32, 32), :]
            line = 512 + (36, 32, 64, 96)[i] + c
            side = jnp.where(row == SY - 1, pressure[line : line + 1, :], pltpu.roll(here, SY - 1, 0))
            above = jnp.where(lane == NZ - 1, here, pltpu.roll(here, NZ - 1, 1))
            fresh[0, x] = ad[0, x] - (ahead - here)
            fresh[1, x] = ad[1, x] - (side - here)
            fresh[2, x] = ad[2, x] - (above - here)
        part = pl.ds(4 * c, 4)
        copy = pltpu.make_async_copy(fresh.at[:, part], vel_out.at[:, part], out_sem.at[3 + c])
        copy.start()
        outs.append(copy)
    for copy in outs:
        copy.wait()


def shards(velocity, theta, vapour, radius_sq, multiplicity, counts, pairing, destination):
    t = tables()
    names = ["cosine", "first", "ahead", "behind", "last", "turns", "wave_z", "box"]
    held = [jnp.asarray(t[name]) for name in names]
    block = (SX, SY, NZ)
    shape = jax.ShapeDtypeStruct
    vmem = pltpu.VMEM
    dma = pltpu.SemaphoreType.DMA
    here = pl.BlockSpec(memory_space=pltpu.VMEM)
    modes, advected, moments = pl.pallas_call(
        step_kernel,
        out_shape=(
            vmem((5, DEV, 128), F32),
            vmem((5,) + block, F32),
            vmem((8, 128), F32),
        ),
        in_specs=[ANY] * 16,
        out_specs=(here,) * 3,
        scratch_shapes=[
            vmem((5, SX + 2, SY, NZ), F32),
            vmem((SY, NZ), F32),
            vmem((SY, NZ), F32),
            vmem((6, SX, NZ), F32),
            vmem((5, SX, NZ), F32),
            vmem((4, 8, NZ), F32),
            vmem((SX, NZ), F32),
            vmem((SX, NZ), F32),
            vmem((4, SY, NZ), F32),
            vmem((4, DEV, 128), F32),
            vmem((4, DEV, 128), F32),
            vmem((5, DEV, 128), F32),
        ]
        + [vmem(t[name].shape, t[name].dtype) for name in names]
        + [
            vmem((32, 64), F32),
            vmem((32, 64), F32),
            vmem((32,), jnp.int32),
            vmem((32, 64), jnp.int32),
            vmem((32, 64), jnp.int32),
            vmem((32, 128), F32),
            vmem((32, 128), F32),
            vmem((8, 32, 128), F32),
            pltpu.SemaphoreType.REGULAR((1,)),
            dma((3,)),
            dma((5,)),
            dma((8,)),
            dma((18,)),
            dma((18,)),
            dma(()),
            dma(()),
            dma(()),
            dma(()),
            dma((8,)),
            dma((8,)),
        ],
        compiler_params=pltpu.CompilerParams(
            has_side_effects=True, collective_id=1, vmem_limit_bytes=24 << 20
        ),
        name="cloud_step",
    )(*[
        pltpu.with_memory_space_constraint(value, pltpu.HBM)
        for value in (
            velocity, theta, vapour, radius_sq.T, multiplicity.T, counts, pairing, destination.T, *held
        )
    ])
    return pl.pallas_call(
        final_kernel,
        out_shape=(
            shape((3,) + block, F32),
            shape(block, F32),
            shape(block, F32),
            shape((3, 32), F32),
        ),
        in_specs=[here] * 4,
        out_specs=(ANY,) * 4,
        scratch_shapes=[
            vmem((3,) + block, F32),
            vmem((3, 32), F32),
            vmem((640, 128), F32),
            dma((7,)),
        ],
        compiler_params=pltpu.CompilerParams(vmem_limit_bytes=12 << 20),
        name="project",
    )(
        *[pltpu.with_memory_space_constraint(value, pltpu.VMEM) for value in (modes, advected, moments)],
        jnp.asarray(t["back"]),
    )


def solution(mesh):
    placed = (
        P(None, "gx", "gy", None),
        P("gx", "gy", None),
        P("gx", "gy", None),
        P(None, ("gx", "gy")),
        P(None, ("gx", "gy")),
        P(("gx", "gy")),
        P(("gx", "gy"), None),
        P(None, ("gx", "gy")),
    )
    return jax.shard_map(
        shards,
        mesh=mesh,
        in_specs=placed,
        out_specs=(
            P(None, "gx", "gy", None),
            P("gx", "gy", None),
            P("gx", "gy", None),
            P(None, ("gx", "gy")),
        ),
        check_vma=False,
    )
```
